32 devices in a mesh: dp: 16 (over z, y, x), tensor: 2 (over core).
Axes of the slice: x: 2, y: 2, z: 4, core: 2. Of those that a mesh axis runs over, the one named last changes fastest.
Arguments:
- tokens: bfloat16 [4096, 1536], P('dp'), may hold values from -6 to 6
- doc_lens: int32 [16, 3], P('dp'), may hold values from 1 to 128, 256 in all within a row
- routes: int32 [4096, 6], P('dp'), may hold values from 0 to 15, all different within a row; in each aligned block of 256 rows (0 to 255, 256 to 511, ...) at most 144 rows name the same one
- gate_weights: float32 [4096, 6], P('dp'), may hold values from 0.15 to 0.45
- norm_attn: float32 [1536], replicated, may hold values from 0.5 to 1.5
- w_query: bfloat16 [1536, 1536], P(None, 'tensor'), may hold values from -0.3125 to 0.3125
- w_key: bfloat16 [1536, 512], P(None, 'tensor'), may hold values from -0.15625 to 0.15625
- w_value: bfloat16 [1536, 512], P(None, 'tensor'), may hold values from -0.15625 to 0.15625
- w_out: bfloat16 [1536, 1536], P('tensor'), may hold values from -0.625 to 0.625
- norm_ffn: float32 [1536], replicated, may hold values from 0.5 to 1.5
- shared_gate: bfloat16 [1536, 1024], P(None, 'tensor'), may hold values from -0.15625 to 0.15625
- shared_up: bfloat16 [1536, 1024], P(None, 'tensor'), may hold values from -0.15625 to 0.15625
- shared_down: bfloat16 [1024, 1536], P('tensor'), may hold values from -0.375 to 0.375
- expert_gate: bfloat16 [16, 1536, 512], P('dp', None, 'tensor'), may hold values from -0.15625 to 0.15625
- expert_up: bfloat16 [16, 1536, 512], P('dp', None, 'tensor'), may hold values from -0.15625 to 0.15625
- expert_down: bfloat16 [16, 512, 1536], P('dp', 'tensor'), may hold values from -0.5 to 0.5
- cotangent: bfloat16 [4096, 1536], P('dp'), may hold values from -6 to 6
Outputs:
- output: bfloat16 [4096, 1536], P('dp')
- grad_tokens: bfloat16 [4096, 1536], P('dp')
- grad_norm_attn: float32 [1536], replicated
- grad_w_query: float32 [1536, 1536], P(None, 'tensor')
- grad_w_key: float32 [1536, 512], P(None, 'tensor')
- grad_w_value: float32 [1536, 512], P(None, 'tensor')
- grad_w_out: float32 [1536, 1536], P('tensor')
- grad_norm_ffn: float32 [1536], replicated
- grad_shared_gate: float32 [1536, 1024], P(None, 'tensor')
- grad_shared_up: float32 [1536, 1024], P(None, 'tensor')
- grad_shared_down: float32 [1024, 1536], P('tensor')
- grad_expert_gate: float32 [16, 1536, 512], P('dp', None, 'tensor')
- grad_expert_up: float32 [16, 1536, 512], P('dp', None, 'tensor')
- grad_expert_down: float32 [16, 512, 1536], P('dp', 'tensor')
The draws below stay inside these ranges and needn't reach their ends.
Inputs may be any that keep to these rules, and one draw needn't show every extreme that they name: `routes`: each row names 6 different experts; within each block of 256 rows of one device, no expert is named by more than 144 rows. `doc_lens`: each row holds the lengths of the 3 sequences packed into one block of 256 tokens, in order; they sum to 256.
All inputs are finite; a program needn't handle non-finite values.
Results may differ from the reference program's by a relative error of at most 0.019.
Values may be sent and summed in bfloat16 or wider, within the bound.
A program may use at most 384 MiB of HBM per device.

```python
import math
import jax
import jax.numpy as jnp
import numpy as np
from jax import lax

D = 1536
HQ = 12
HK = 4
DH = 128
FE = 512
FS = 1024
TOPK = 6
SEQ = 256
DOCS = 3
BLOCKS = 16
EXPERTS = 16
TOKENS = 4096
CAP = 144


def block_scale(rng, dims, cuts, smallest, top_value):
    gain, own = 1.0, jax.random.fold_in(rng, 6)
    for axis_at, blocks in cuts:
        heights = jnp.exp(jax.random.uniform(jax.random.fold_in(own, axis_at), (blocks,), jnp.float32, smallest / len(cuts), top_value / len(cuts)))
        gain = gain * jnp.repeat(heights, dims[axis_at] // blocks).reshape([-1 if axis == axis_at else 1 for axis in range(len(dims))])
    return gain


def split_up(number_of, total, bound, skew):
    portions = [(1 << 20) // math.isqrt(rank ** skew) + 1 for rank in range(2, number_of + 1)]
    rest, given = total - bound - (number_of - 1), [1] * (number_of - 1)
    while rest > 0:
        free = [i for i in range(number_of - 1) if given[i] < bound]
        mass, left = sum([portions[i] for i in free]), rest
        for i in free:
            addition = min(bound - given[i], max(1, left * portions[i] // mass), rest)
            given[i] = given[i] + addition
            rest = rest - addition
    return np.array([bound] + given)


def ragged_sizes(own_key, amount, total, most, slope):
    if amount == 2:
        one = jax.random.randint(own_key, (), max(1, total - most), min(most, total - 1) + 1)
        return jnp.stack([one, total - one])
    tallies = jnp.asarray(split_up(amount, total, most, slope), jnp.int32)
    pairs = (amount - 1) // 2
    source_of, sink = tallies[1:1 + 2 * pairs:2], tallies[2:2 + 2 * pairs:2]
    room = jnp.minimum(source_of - 1, most - sink)
    moved = jax.random.randint(jax.random.fold_in(own_key, 1), (pairs,), 0, 1 << 20) % (room + 1)
    tallies = tallies.at[1:1 + 2 * pairs:2].set(source_of - moved).at[2:2 + 2 * pairs:2].set(sink + moved)
    return tallies[jax.random.permutation(jax.random.fold_in(own_key, 2), amount)]


def assign_block(stream_key, own, number, rows, amount, top, limit, lean):
    ranking = jax.random.permutation(stream_key, amount)
    packed, ordinary = portions_of(amount, rows * top, limit, lean, True), portions_of(amount, rows * top, limit, lean, False)
    places = jnp.arange(amount)

    def named(lengths, offset_by):
        used = int((lengths > 0).sum())
        fixed = max(1, used // 4)
        shifted = fixed + (places - fixed + offset_by * (used - fixed)) % max(1, amount - fixed)
        return jnp.zeros((amount,), jnp.int32).at[ranking[jnp.where(places < fixed, places, shifted)]].set(jnp.asarray(lengths, jnp.int32))

    lengths = jnp.where(number % 4 == 0, named(packed, number // 4), named(ordinary, number - number // 4 - 1))
    mixed = jax.random.permutation(jax.random.fold_in(own, 3), amount)
    source_of, taker = mixed[0:amount // 2 * 2:2], mixed[1:amount // 2 * 2:2]
    margin = jnp.minimum(lengths[source_of] - 1, limit - lengths[taker]) // 2
    margin = jnp.where((source_of == ranking[0]) | (taker == ranking[0]) | (lengths[taker] == 0), 0, jnp.maximum(margin, 0))
    shifted = jax.random.randint(jax.random.fold_in(own, 4), (amount // 2,), 0, 1 << 20) % (margin + 1)
    lengths = lengths.at[source_of].add(-shifted).at[taker].add(shifted)
    members = jnp.searchsorted(jnp.cumsum(lengths), jnp.arange(rows * top), side="right").astype(jnp.int32)
    grid = members.reshape(top, rows).T
    grid = grid[jax.random.permutation(jax.random.fold_in(own, 1), rows)]
    offset_by = jax.random.randint(jax.random.fold_in(own, 2), (rows, 1), 0, top)
    return jnp.take_along_axis(grid, (jnp.arange(top)[None, :] + offset_by) % top, axis=1)


def portions_of(number_of, total, bound, slope, full):
    loads = [(1 << 20) // math.isqrt(grade ** slope) + 1 for grade in range(1, number_of + 1)]
    largest = bound if full else min(bound, max(-(-total // number_of), total * loads[0] // sum(loads)))
    least = 1 if total - largest >= number_of - 1 else 0
    holding, surplus = [largest] + [least] * (number_of - 1), total - largest - least * (number_of - 1)
    while surplus > 0:
        candidates = [i for i in range(1, number_of) if holding[i] < largest] or [i for i in range(1, number_of) if holding[i] < bound]
        pool, remaining = sum([loads[i] for i in candidates]), surplus
        for i in candidates:
            addition = min(bound - holding[i], max(1, remaining * loads[i] // pool), surplus)
            holding[i] = holding[i] + addition
            surplus = surplus - addition
    return np.array(holding)


def gaussian(rng, dims, width, limit, split=(), held_as=jnp.bfloat16):
    array = jax.random.normal(rng, dims, jnp.float32) * width
    if len(split) > 0:
        array = block_scale(rng, dims, split, -0.22, 0.18) * array
    return jnp.clip(array, min=-limit, max=limit).astype(held_as)


def setup_inputs(seed: int = 0) -> dict:
    key_list = jax.random.split(jax.random.key(seed), 18)
    tokens = gaussian(key_list[0], (TOKENS, D), 1.0, 6.0, ((0, 16),))
    doc_lens = jax.vmap(lambda own: ragged_sizes(own, DOCS, SEQ, SEQ // 2, 1))(jax.random.split(key_list[1], BLOCKS)).reshape((BLOCKS, DOCS)).astype(jnp.int32)
    routes_keys = jax.random.split(jax.random.fold_in(key_list[2], 1), TOKENS // SEQ)
    routes_turns = jax.random.permutation(jax.random.fold_in(key_list[2], 3), TOKENS // SEQ)
    routes = jax.vmap(lambda own, number: assign_block(jax.random.fold_in(key_list[2], 2), own, number, SEQ, EXPERTS, TOPK, CAP, 2))(routes_keys, routes_turns).reshape((TOKENS, TOPK))
    gate_weights = jnp.clip(0.15 + 0.29999998 * jax.random.uniform(key_list[3], (TOKENS, TOPK), jnp.float32) ** block_scale(key_list[3], (TOKENS, TOPK), ((0, 16),), -0.2, 0.2), 0.15, 0.45)
    norm_attn = jnp.clip(1.0 + 0.1 * jax.random.normal(key_list[4], (D,), jnp.float32), 0.5, 1.5)
    w_query = gaussian(key_list[5], (D, HQ * DH), (D // 4) ** -0.5, 0.3125, ((1, 2),))
    w_key = gaussian(key_list[6], (D, HK * DH), D ** -0.5, 0.15625, ((1, 2),))
    w_value = gaussian(key_list[7], (D, HK * DH), D ** -0.5, 0.15625, ((1, 2),))
    w_out = gaussian(key_list[8], (HQ * DH, D), (HQ * DH // 16) ** -0.5, 0.625, ((0, 2),))
    norm_ffn = jnp.clip(1.0 + 0.1 * jax.random.normal(key_list[9], (D,), jnp.float32), 0.5, 1.5)
    shared_gate = gaussian(key_list[10], (D, FS), D ** -0.5, 0.15625, ((1, 2),))
    shared_up = gaussian(key_list[11], (D, FS), D ** -0.5, 0.15625, ((1, 2),))
    shared_down = gaussian(key_list[12], (FS, D), (FS // 4) ** -0.5, 0.375, ((0, 2),))
    expert_gate = gaussian(key_list[13], (EXPERTS, D, FE), D ** -0.5, 0.15625, ((0, 16), (2, 2)))
    expert_up = gaussian(key_list[14], (EXPERTS, D, FE), D ** -0.5, 0.15625, ((0, 16), (2, 2)))
    expert_down = gaussian(key_list[15], (EXPERTS, FE, D), (FE // 4) ** -0.5, 0.5, ((0, 16), (1, 2)))
    cotangent = gaussian(key_list[16], (TOKENS, D), 1.0, 6.0, ((0, 16),))
    return {"tokens": tokens, "doc_lens": doc_lens, "routes": routes, "gate_weights": gate_weights, "norm_attn": norm_attn, "w_query": w_query, "w_key": w_key, "w_value": w_value, "w_out": w_out, "norm_ffn": norm_ffn, "shared_gate": shared_gate, "shared_up": shared_up, "shared_down": shared_down, "expert_gate": expert_gate, "expert_up": expert_up, "expert_down": expert_down, "cotangent": cotangent}


highest = lax.Precision.HIGHEST
epsilon = 1e-05
masked_value = -1e+30

@jax.custom_vjp
def low(v):
    return lax.optimization_barrier(v.astype(jnp.bfloat16)).astype(jnp.float32)

@jax.custom_vjp
def low_back(v):
    return v

def low_keep(v):
    return (low(v), None)

def low_pass(kept, grad):
    return (grad,)

def back_keep(v):
    return (v, None)

def back_low(kept, grad):
    return (low(grad),)
low.defvjp(low_keep, low_pass)
low_back.defvjp(back_keep, back_low)

def both_ways(values):
    return low_back(low(values))

def product(first, second):
    return jnp.dot(first, second, precision=highest)

def rms_normed(values, gain_vector):
    factor = lax.rsqrt(lax.optimization_barrier(jnp.mean(values * values, axis=-1, keepdims=True)) + epsilon)
    return values * factor * gain_vector

def swish_product(gated, upward):
    return gated * jax.nn.sigmoid(gated) * upward

def slot_positions(block_routes):
    flat_routes = block_routes.reshape(-1)
    onehot = (flat_routes[:, None] == jnp.arange(EXPERTS, dtype=jnp.int32)[None, :]).astype(jnp.int32)
    earlier = jnp.cumsum(onehot, axis=0) - onehot
    return lax.optimization_barrier(jnp.sum(earlier * onehot, axis=1)).reshape(SEQ, TOPK)

def block_forward(params, block_tokens, block_lens, block_routes, block_gates):
    norm_attn, w_query, w_key, w_value, w_out, norm_ffn, shared_gate, shared_up, shared_down, expert_gate, expert_up, expert_down = params
    positions = jnp.arange(SEQ, dtype=jnp.int32)
    doc_ends = jnp.cumsum(block_lens)
    doc_index = lax.optimization_barrier(jnp.sum((positions[:, None] >= doc_ends[None, :]).astype(jnp.int32), axis=1))
    visible = (doc_index[:, None] == doc_index[None, :]) & (positions[None, :] <= positions[:, None])
    group_size = HQ // HK
    normed_one = low(rms_normed(block_tokens, norm_attn))
    query = both_ways(product(normed_one, w_query)).reshape(SEQ, HK, group_size, DH)
    keys = both_ways(product(normed_one, w_key)).reshape(SEQ, HK, DH)
    values = both_ways(product(normed_one, w_value)).reshape(SEQ, HK, DH)
    scores = low_back(jnp.einsum('ikgd,jkd->kgij', query, keys, precision=highest) * DH ** (-0.5))
    scores = jnp.where(visible, scores, masked_value)
    row_max = lax.optimization_barrier(jnp.max(scores, axis=-1, keepdims=True))
    weights_exp = jnp.exp(scores - row_max)
    probs = low(weights_exp / lax.optimization_barrier(jnp.sum(weights_exp, axis=-1, keepdims=True)))
    attended = both_ways(jnp.einsum('kgij,jkd->ikgd', probs, values, precision=highest)).reshape(SEQ, HQ * DH)
    hidden_state = block_tokens + low_back(product(attended, w_out))
    normed_two = low(rms_normed(hidden_state, norm_ffn))
    shared_hidden = low(swish_product(low_back(product(normed_two, shared_gate)), low_back(product(normed_two, shared_up))))
    shared_out = low_back(product(shared_hidden, shared_down))
    position = slot_positions(block_routes)
    owners = jnp.repeat(jnp.arange(SEQ, dtype=jnp.int32), TOPK)
    slot_rows = jnp.full((EXPERTS, CAP), SEQ, jnp.int32).at[block_routes.reshape(-1), position.reshape(-1)].set(owners)
    padded = jnp.concatenate([normed_two, jnp.zeros((1, D), jnp.float32)], axis=0)
    local_rows = padded[slot_rows]
    expert_gated = low_back(jnp.einsum('ecd,edf->ecf', local_rows, expert_gate, precision=highest))
    expert_upward = low_back(jnp.einsum('ecd,edf->ecf', local_rows, expert_up, precision=highest))
    expert_hidden = low(swish_product(expert_gated, expert_upward))
    expert_out = low_back(jnp.einsum('ecf,efd->ecd', expert_hidden, expert_down, precision=highest))
    picked = expert_out[block_routes, position]
    mixture = lax.optimization_barrier(jnp.sum(block_gates[:, :, None] * picked, axis=1))
    return hidden_state + shared_out + mixture

def reference(tokens, doc_lens, routes, gate_weights, norm_attn, w_query, w_key, w_value, w_out, norm_ffn, shared_gate, shared_up, shared_down, expert_gate, expert_up, expert_down, cotangent):
    params = tuple((weight.astype(jnp.float32) for weight in (norm_attn, w_query, w_key, w_value, w_out, norm_ffn, shared_gate, shared_up, shared_down, expert_gate, expert_up, expert_down)))
    inputs = tokens.astype(jnp.float32).reshape(BLOCKS, SEQ, D)
    routes_blocks = routes.reshape(BLOCKS, SEQ, TOPK)
    gates_blocks = gate_weights.astype(jnp.float32).reshape(BLOCKS, SEQ, TOPK)

    def forward(all_tokens, all_params):

        def one_block(pieces):
            return block_forward(all_params, pieces[0], pieces[1], pieces[2], pieces[3])
        return lax.map(jax.checkpoint(one_block), (all_tokens, doc_lens, routes_blocks, gates_blocks))
    result, pullback = jax.vjp(forward, inputs, params)
    grad_inputs, grad_params = pullback(cotangent.astype(jnp.float32).reshape(BLOCKS, SEQ, D))
    return (result.reshape(TOKENS, D).astype(jnp.bfloat16), grad_inputs.reshape(TOKENS, D).astype(jnp.bfloat16), grad_params[0], grad_params[1], grad_params[2], grad_params[3], grad_params[4], grad_params[5], grad_params[6], grad_params[7], grad_params[8], grad_params[9], grad_params[10], grad_params[11])
```

```python
import functools
import jax
import jax.numpy as jnp
from jax import lax
from jax.experimental import pallas as pl
from jax.experimental.pallas import tpu as pltpu
from jax.sharding import PartitionSpec as P

DH = 128


epsilon = 1e-05
masked_value = -1e30


def rms_factor(values):
    return lax.rsqrt(jnp.mean(values * values, axis=-1, keepdims=True) + epsilon)


def norm_backward(grad_normed, gain_vector, factor, scaled):
    grad_scaled = grad_normed * gain_vector
    inner_mean = jnp.mean(grad_scaled * scaled, axis=-1, keepdims=True)
    return (factor * (grad_scaled - scaled * inner_mean), jnp.sum(grad_normed * scaled, axis=0))


def swish_grads(gated, upward, grad_hidden):
    sigma = jax.nn.sigmoid(gated)
    grad_gated = grad_hidden * upward * sigma * (1.0 + gated * (1.0 - sigma))
    grad_upward = grad_hidden * gated * sigma
    return (grad_gated.astype(jnp.bfloat16), grad_upward.astype(jnp.bfloat16))


def slot_positions(routes, expert_count):
    flat_routes = routes.reshape(-1)
    onehot = (flat_routes[:, None] == jnp.arange(expert_count, dtype=jnp.int32)[None, :]).astype(
        jnp.int32
    )
    earlier = jnp.cumsum(onehot, axis=0) - onehot
    return jnp.sum(earlier * onehot, axis=1).reshape(routes.shape)


def to_experts(buffer):
    return lax.all_to_all(buffer, "dp", split_axis=0, concat_axis=0, tiled=True)


def from_experts(partial_value):
    own_part = lax.psum_scatter(
        partial_value.astype(jnp.bfloat16), "tensor", scatter_dimension=1, tiled=True
    ).astype(jnp.float32)
    joined = lax.all_gather(own_part.astype(jnp.bfloat16), "tensor", axis=1, tiled=True).astype(
        own_part.dtype
    )
    return lax.all_to_all(
        joined.astype(jnp.bfloat16), "dp", split_axis=0, concat_axis=0, tiled=True
    ).astype(joined.dtype)


MESH = pl.DeviceIdType.MESH
ANY = pl.BlockSpec(memory_space=pl.ANY)


class Place:
    def __init__(self):
        self.dp = lax.axis_index("dp")
        self.t = lax.axis_index("tensor")
        self.x, self.y, self.z = self.dp % 2, (self.dp // 2) % 2, self.dp // 4

    def rel(self, da, db, k):
        t = self.t
        x = (self.x + (1 - t) * da + t * db) % 2
        y = (self.y + t * da + (1 - t) * db) % 2
        z = (self.z + k) % 4
        return z * 4 + y * 2 + x

    def core(self):
        return (self.dp, 1 - self.t)

    def a(self):
        return (self.rel(1, 0, 0), self.t)

    def b(self):
        return (self.rel(0, 1, 0), self.t)

    def zk(self, k):
        return (self.rel(0, 0, k), self.t)


def greet(place):
    barrier = pltpu.get_barrier_semaphore()
    partners = [place.core(), place.a(), place.b()] + [place.zk(k) for k in (1, 2, 3)]
    for partner in partners:
        pl.semaphore_signal(barrier, inc=1, device_id=partner, device_id_type=MESH)
    pl.semaphore_wait(barrier, len(partners))


def remote(src, dst, send, recv, device):
    return pltpu.make_async_remote_copy(
        src_ref=src, dst_ref=dst, send_sem=send, recv_sem=recv, device_id=device, device_id_type=MESH
    )


class Gather:
    def __init__(self, place, own, part, sems, swap):
        self.p, self.own, self.part, self.swap = place, own, part, swap
        self.zs, self.zr, self.as_, self.ar, self.bs, self.br = sems[:6]
        if swap:
            self.cs, self.cr = sems[6:]

    def z(self, k, rel=0):
        return remote(self.own, self.part(self.p.dp), self.zs.at[k - 1], self.zr.at[k - 1], self.p.zk(k))

    def to_a(self, k):
        j = self.p.rel(0, 0, k)
        src = self.own if isinstance(k, int) and k == 0 else self.part(j)
        return remote(src, self.part(j), self.as_.at[k], self.ar.at[k], self.p.a())

    def to_b(self, da, k):
        j = self.p.rel(da, 0, k)
        src = self.own if isinstance(k, int) and k == 0 and da == 0 else self.part(j)
        return remote(src, self.part(j), self.bs.at[da, k], self.br.at[da, k], self.p.b())

    def to_core(self, j):
        return remote(self.part(j), self.part(j), self.cs.at[j], self.cr.at[j], self.p.core())

    def start(self):
        self.to_b(0, 0).start()
        for k in (1, 2, 3):
            self.z(k).start()
        self.to_a(0).start()

    def got_z(self, k):
        self.z(k).wait_recv()
        kk = (4 - k) % 4
        self.to_b(0, kk).start()
        self.to_a(kk).start()
        if self.swap:
            self.to_core(self.p.rel(0, 0, kk)).start()

    def got_a(self, k):
        self.to_a(k).wait_recv()
        self.to_b(1, k).start()
        if self.swap:
            self.to_core(self.p.rel(1, 0, k)).start()

    def got_b(self, da, k):
        self.to_b(da, k).wait_recv()
        if self.swap:
            self.to_core(self.p.rel(da, 1, k)).start()

    def got_core(self, da, db, k):
        self.to_core(self.p.rel(da, db, k)).wait_recv()

    def finish(self):
        for k in (1, 2, 3):
            self.z(k).wait_send()

        def ends(k, _):
            self.to_a(k).wait_send()
            self.to_b(0, k).wait_send()
            self.to_b(1, k).wait_send()
            return 0

        lax.fori_loop(0, 4, ends, 0)
        if self.swap:

            def swaps(i, _):
                self.to_core((self.p.dp + 1 + i) % 16).wait_send()
                return 0

            lax.fori_loop(0, 15, swaps, 0)


def gather_sems(swap):
    kinds = [(3,), (3,), (4,), (4,), (2, 4), (2, 4)] + ([(16,), (16,)] if swap else [])
    return [pltpu.SemaphoreType.DMA(kind) for kind in kinds]


def add_into(dst, src):
    rows = dst.shape[0]

    def step(i, _):
        at = pl.ds(pl.multiple_of(i * 16, 16), 16)
        dst[at, :] = dst[at, :] + src[at, :]
        return 0

    lax.fori_loop(0, rows // 16, step, 0)


class Scatter:
    def __init__(self, place, own, land, sems):
        self.p, self.own = place, own
        self.rb, self.ra, self.rz = land
        self.bs, self.br, self.as_, self.ar, self.zs, self.zr = sems

    def to_b(self, da, k):
        j = self.p.rel(da, 1, k)
        return remote(self.own.at[j], self.rb.at[da, k], self.bs.at[da, k], self.br.at[da, k], self.p.b())

    def to_a(self, k):
        j = self.p.rel(1, 0, k)
        return remote(self.own.at[j], self.ra.at[k], self.as_.at[k], self.ar.at[k], self.p.a())

    def to_z(self, k):
        j = self.p.rel(0, 0, k)
        return remote(self.own.at[j], self.rz.at[k - 1], self.zs.at[k - 1], self.zr.at[k - 1], self.p.zk(k))

    def got_b(self, da, k):
        self.to_b(da, k).wait_recv()
        add_into(self.own.at[self.p.rel(da, 0, k)], self.rb.at[da, k])

    def got_a(self, k):
        self.to_a(k).wait_recv()
        add_into(self.own.at[self.p.rel(0, 0, k)], self.ra.at[k])

    def run(self):
        def far(k, _):
            self.got_b(1, k)
            self.to_a(k).start()
            return 0

        def near(i, _):
            k = (i + 1) % 4
            self.got_b(0, k)
            self.got_a(k)
            return 0

        lax.fori_loop(0, 4, far, 0)
        for k in (1, 2, 3, 0):
            self.got_b(0, k)
            self.got_a(k)
            if k:
                self.to_z(k).start()
        for k in (1, 2, 3):
            self.to_z(k).wait_recv()

    def total(self, put):
        mine = self.own.at[self.p.dp]
        rows = mine.shape[0]

        def step(i, _):
            at = pl.ds(pl.multiple_of(i * 16, 16), 16)
            total = mine[at, :].astype(jnp.float32)
            for k in range(3):
                total = total + self.rz[k, at, :].astype(jnp.float32)
            put(at, total)
            return 0

        lax.fori_loop(0, rows // 16, step, 0)

    def finish(self):
        def ends(k, _):
            self.to_a(k).wait_send()
            self.to_b(0, k).wait_send()
            self.to_b(1, k).wait_send()
            return 0

        lax.fori_loop(0, 4, ends, 0)
        for k in (1, 2, 3):
            self.to_z(k).wait_send()


def scatter_land(rows, cols):
    return [pltpu.VMEM((2, 4, rows, cols), jnp.bfloat16), pltpu.VMEM((4, rows, cols), jnp.bfloat16), pltpu.VMEM((3, rows, cols), jnp.bfloat16)]


def scatter_sems():
    return [pltpu.SemaphoreType.DMA(kind) for kind in [(2, 4), (2, 4), (4,), (4,), (3,), (3,)]]


def gather_kernel(n, *refs):
    ins, outs = refs[:n], refs[n : 2 * n]
    local = refs[2 * n]
    sems = refs[2 * n + 1 :]
    p = Place()
    greet(p)
    off = pl.multiple_of(p.t * 768, 768)
    gathers, copies = [], []
    for i in range(n):
        g = Gather(p, ins[i].at[:, pl.ds(off, 768)], lambda j, o=outs[i]: o.at[j, :, pl.ds(off, 768)], sems[8 * i : 8 * i + 8], True)
        g.start()
        copy = pltpu.make_async_copy(ins[i], outs[i].at[p.dp], local.at[i])
        copy.start()
        gathers.append(g)
        copies.append(copy)
    for g in gathers:
        for k in (1, 2, 3):
            g.got_z(k)
        for k in (0, 3, 2, 1):
            g.got_a(k)
        for da in range(2):
            for k in range(4):
                g.got_b(da, k)
    for g in gathers:

        def waits(i, _, g=g):
            g.to_core((p.dp + 1 + i) % 16).wait_recv()
            return 0

        lax.fori_loop(0, 15, waits, 0)
        g.finish()
    for copy in copies:
        copy.wait()


def gather_blocks(*xs):
    n = len(xs)
    return pl.pallas_call(
        functools.partial(gather_kernel, n),
        out_shape=tuple(jax.ShapeDtypeStruct((16, 256, 1536), jnp.bfloat16) for _ in xs),
        in_specs=[ANY] * n,
        out_specs=(ANY,) * n,
        scratch_shapes=[pltpu.SemaphoreType.DMA((n,))] + [s for _ in xs for s in gather_sems(True)],
        compiler_params=pltpu.CompilerParams(collective_id=1, has_side_effects=True),
    )(*xs)


def scatter_kernel(n, *refs):
    ins, outs = refs[:n], refs[n : 2 * n]
    refs = refs[2 * n :]
    p = Place()
    greet(p)
    mine = pl.multiple_of(p.t * 768, 768)
    other = pl.multiple_of((1 - p.t) * 768, 768)
    plans = []
    for i in range(n):
        own, came, res, ls, cs, cr, fs = refs[:7]
        s = Scatter(p, own, refs[7:10], refs[10:16])
        plans.append((ins[i], outs[i], own, came, res, ls, cs, cr, fs, s))
        refs = refs[16:]
    for src, out, own, came, res, ls, cs, cr, fs, s in plans:

        def swap(j):
            return remote(src.at[j, :, pl.ds(other, 768)], came.at[j], cs.at[j], cr.at[j], p.core())

        def load(j):
            return pltpu.make_async_copy(src.at[j, :, pl.ds(mine, 768)], own.at[j], ls.at[j])

        for da in (1, 0):
            for db in (1, 0):
                for k in range(4):
                    swap(p.rel(da, db, k)).start()
                    load(p.rel(db, da, k)).start()
    for src, out, own, came, res, ls, cs, cr, fs, s in plans:

        def swap(j):
            return remote(src.at[j, :, pl.ds(other, 768)], came.at[j], cs.at[j], cr.at[j], p.core())

        def load(j):
            return pltpu.make_async_copy(src.at[j, :, pl.ds(mine, 768)], own.at[j], ls.at[j])

        for db in (1, 0):
            for da in (1, 0):

                def pair(k, _):
                    j = p.rel(da, db, k)
                    load(j).wait()
                    swap(j).wait_recv()
                    add_into(own.at[j], came.at[j])
                    if db:
                        s.to_b(da, k).start()
                    return 0

                lax.fori_loop(0, 4, pair, 0)
    for src, out, own, came, res, ls, cs, cr, fs, s in plans:
        s.run()

        def put(at, total):
            res[at, :] = total

        s.total(put)
        remote(res, out.at[:, pl.ds(mine, 768)], fs.at[0], fs.at[1], p.core()).start()
        pltpu.make_async_copy(res, out.at[:, pl.ds(mine, 768)], fs.at[2]).start()
    for src, out, own, came, res, ls, cs, cr, fs, s in plans:

        def ends(j, _):
            remote(src.at[j, :, pl.ds(other, 768)], came.at[j], cs.at[j], cr.at[j], p.core()).wait_send()
            return 0

        lax.fori_loop(0, 16, ends, 0)
        s.finish()
        remote(res, out.at[:, pl.ds(other, 768)], fs.at[0], fs.at[1], p.core()).wait()
        pltpu.make_async_copy(res, out.at[:, pl.ds(mine, 768)], fs.at[2]).wait()


def scatter_blocks(*xs):
    n = len(xs)
    dma = pltpu.SemaphoreType.DMA
    scratch = []
    for _ in xs:
        scratch += [pltpu.VMEM((16, 256, 768), jnp.bfloat16), pltpu.VMEM((16, 256, 768), jnp.bfloat16), pltpu.VMEM((256, 768), jnp.float32), dma((16,)), dma((16,)), dma((16,)), dma((3,))]
        scratch += scatter_land(256, 768) + scatter_sems()
    return pl.pallas_call(
        functools.partial(scatter_kernel, n),
        out_shape=tuple(jax.ShapeDtypeStruct((256, 1536), jnp.float32) for _ in xs),
        in_specs=[ANY] * n,
        out_specs=(ANY,) * n,
        scratch_shapes=scratch,
        compiler_params=pltpu.CompilerParams(collective_id=2, has_side_effects=True, vmem_limit_bytes=56 << 20),
    )(*xs)


def reduce_kernel(ga, gb, gn, oa, ob, on, *refs):
    p = Place()
    greet(p)
    plans = []
    for src, out in ((ga, oa), (gb, ob)):
        own, blk, ls = refs[:3]
        plans.append((src, out, own, blk, ls, Scatter(p, own, refs[3:6], refs[6:12]), refs[12:18]))
        refs = refs[18:]
    allgains = refs[0]
    gains = Gather(p, gn, lambda j: allgains.at[j], refs[1:7], False)
    gains.start()
    allgains[p.dp] = gn[...]
    for src, out, own, blk, ls, s, gsems in plans:

        def load(j):
            return pltpu.make_async_copy(src.at[j], own.at[j], ls.at[j])

        for db in (1, 0):
            for da in (1, 0):
                for k in range(4):
                    load(p.rel(da, db, k)).start()
    for src, out, own, blk, ls, s, gsems in plans:
        for db in (1, 0):
            for da in (1, 0):
                for k in range(4):
                    j = p.rel(da, db, k)
                    pltpu.make_async_copy(src.at[j], own.at[j], ls.at[j]).wait()
                    if db:
                        s.to_b(da, k).start()
    for k in (1, 2, 3):
        gains.got_z(k)
    for k in (0, 3, 2, 1):
        gains.got_a(k)
    gathers = []
    for src, out, own, blk, ls, s, gsems in plans:
        s.run()

        def put(at, total):
            blk[at, :] = total.astype(jnp.bfloat16)

        s.total(put)
        g = Gather(p, blk, lambda j, out=out: out.at[j], gsems, False)
        g.start()
        pltpu.make_async_copy(blk, out.at[p.dp], ls.at[0]).start()
        gathers.append(g)
    for da in range(2):
        for k in range(4):
            gains.got_b(da, k)
    total = allgains[0]
    for j in range(1, 16):
        total = total + allgains[j]
    on[...] = total
    for g in gathers:
        for k in (1, 2, 3):
            g.got_z(k)
        for k in (0, 3, 2, 1):
            g.got_a(k)
    for g in gathers:
        for da in range(2):
            for k in range(4):
                g.got_b(da, k)
        g.finish()
    gains.finish()
    for src, out, own, blk, ls, s, gsems in plans:
        s.finish()
        pltpu.make_async_copy(blk, out.at[p.dp], ls.at[0]).wait()


def reduce_grads(ga, gb, gn):
    dma = pltpu.SemaphoreType.DMA
    scratch = []
    for g in (ga, gb):
        scratch += [pltpu.VMEM(g.shape, jnp.bfloat16), pltpu.VMEM(g.shape[1:], jnp.bfloat16), dma((16,))]
        scratch += scatter_land(*g.shape[1:]) + scatter_sems() + gather_sems(False)
    scratch += [pltpu.VMEM((16, 8, 384), jnp.float32)] + gather_sems(False)
    return pl.pallas_call(
        reduce_kernel,
        out_shape=(jax.ShapeDtypeStruct(ga.shape, jnp.bfloat16), jax.ShapeDtypeStruct(gb.shape, jnp.bfloat16), jax.ShapeDtypeStruct(gn.shape, jnp.float32)),
        in_specs=[ANY, ANY, pl.BlockSpec(memory_space=pltpu.VMEM)],
        out_specs=(ANY, ANY, pl.BlockSpec(memory_space=pltpu.VMEM)),
        scratch_shapes=scratch,
        compiler_params=pltpu.CompilerParams(collective_id=3, has_side_effects=True, vmem_limit_bytes=56 << 20),
    )(ga, gb, gn)


def shards_fast(
    tokens, doc_lens, routes, gate_weights, norm_attn, w_query, w_key, w_value, w_out, norm_ffn,
    shared_gate, shared_up, shared_down, expert_gate, expert_up, expert_down, cotangent,
):
    seq_len, width = tokens.shape
    head_dim = DH
    kv_heads = w_key.shape[1] // head_dim
    q_heads = w_query.shape[1] // head_dim
    group_size = q_heads // kv_heads
    score_scale = head_dim ** (-0.5)
    chip = lax.axis_index("dp")
    expert_count = lax.axis_size("dp")
    named = (routes[:, :, None] == jnp.arange(expert_count, dtype=jnp.int32)).astype(jnp.float32)
    gates = lax.all_gather(jnp.sum(gate_weights[:, :, None] * named, axis=1), "dp")
    gate = lax.dynamic_index_in_dim(gates, chip, 2).reshape(-1, 1)
    positions = jnp.arange(seq_len, dtype=jnp.int32)
    doc_ends = jnp.cumsum(doc_lens[0])
    doc_index = jnp.sum((positions[:, None] >= doc_ends[None, :]).astype(jnp.int32), axis=1)
    visible = (doc_index[:, None] == doc_index[None, :]) & (
        positions[None, :] <= positions[:, None]
    )
    inputs = tokens.astype(jnp.float32)
    factor_one = rms_factor(inputs)
    scaled_one = inputs * factor_one
    normed_one = (scaled_one * norm_attn).astype(jnp.bfloat16)
    query = (
        jnp.dot(normed_one, w_query, preferred_element_type=jnp.float32)
        .astype(jnp.bfloat16)
        .reshape(seq_len, kv_heads, group_size, head_dim)
    )
    keys = (
        jnp.dot(normed_one, w_key, preferred_element_type=jnp.float32)
        .astype(jnp.bfloat16)
        .reshape(seq_len, kv_heads, head_dim)
    )
    values = (
        jnp.dot(normed_one, w_value, preferred_element_type=jnp.float32)
        .astype(jnp.bfloat16)
        .reshape(seq_len, kv_heads, head_dim)
    )

    def score_block():
        raw = (
            jnp.einsum("ikgd,jkd->kgij", query, keys, preferred_element_type=jnp.float32)
            * score_scale
        )
        return jnp.where(visible, raw, masked_value)

    scores = score_block()
    row_max = jnp.max(scores, axis=-1, keepdims=True)
    log_total = row_max + jnp.log(jnp.sum(jnp.exp(scores - row_max), axis=-1, keepdims=True))
    probs_low = jnp.exp(scores - log_total).astype(jnp.bfloat16)
    attended = (
        jnp.einsum("kgij,jkd->ikgd", probs_low, values, preferred_element_type=jnp.float32)
        .astype(jnp.bfloat16)
        .reshape(seq_len, q_heads * head_dim)
    )
    attn_part = jnp.dot(attended, w_out, preferred_element_type=jnp.float32)
    hidden_state = inputs + lax.psum(attn_part, "tensor")
    factor_two = rms_factor(hidden_state)
    scaled_two = hidden_state * factor_two
    normed_two = (scaled_two * norm_ffn).astype(jnp.bfloat16)

    normed_all, cot_all = gather_blocks(normed_two, cotangent)
    normed_all = normed_all.reshape(-1, width)
    cot_all = cot_all.reshape(-1, width)
    own = chip * seq_len

    def dot(first, second):
        return jnp.dot(first, second, preferred_element_type=jnp.float32)

    def dot_t(first, second):
        return lax.dot_general(first, second, (((1,), (1,)), ((), ())), preferred_element_type=jnp.float32)

    def dot_rows(first, second):
        return lax.dot_general(first, second, (((0,), (0,)), ((), ())), preferred_element_type=jnp.float32)

    def mine(rows):
        return lax.dynamic_slice_in_dim(rows, own, seq_len, 0)

    def add_mine(rows, more):
        return lax.dynamic_update_slice_in_dim(rows, mine(rows) + more.astype(rows.dtype), own, 0)

    expert_gated, expert_upward = dot(normed_all, expert_gate[0]), dot(normed_all, expert_up[0])
    expert_hidden = (expert_gated * jax.nn.sigmoid(expert_gated) * expert_upward).astype(jnp.bfloat16)
    routed_grad = (gate * cot_all.astype(jnp.float32)).astype(jnp.bfloat16)
    grad_eg, grad_eu = swish_grads(expert_gated, expert_upward, dot_t(routed_grad, expert_down[0]))
    back_part = (dot_t(grad_eg, expert_gate[0]) + dot_t(grad_eu, expert_up[0])).astype(jnp.bfloat16)
    mix_part = (gate * dot(expert_hidden, expert_down[0])).astype(jnp.bfloat16)
    shared_gated, shared_upward = dot(normed_all, shared_gate), dot(normed_all, shared_up)
    shared_hidden = (shared_gated * jax.nn.sigmoid(shared_gated) * shared_upward).astype(jnp.bfloat16)
    grad_sg, grad_su = swish_grads(shared_gated, shared_upward, dot_t(cot_all, shared_down))
    mix_part = add_mine(mix_part, dot(mine(shared_hidden), shared_down))
    back_part = add_mine(back_part, dot_t(mine(grad_sg), shared_gate) + dot_t(mine(grad_su), shared_up))
    normed_grad, branches = scatter_blocks(
        back_part.reshape(-1, seq_len, width), mix_part.reshape(-1, seq_len, width)
    )
    grad_expert_gate = dot_rows(normed_all, grad_eg)[None]
    grad_expert_up = dot_rows(normed_all, grad_eu)[None]
    grad_expert_down = dot_rows(expert_hidden, routed_grad)[None]
    grad_shared_gate = dot_rows(normed_all, grad_sg)
    grad_shared_up = dot_rows(normed_all, grad_su)
    grad_shared_down = dot_rows(shared_hidden, cot_all)
    output = (hidden_state + branches).astype(jnp.bfloat16)
    grad_result = cotangent.astype(jnp.float32)
    grad_hidden_norm, grad_norm_ffn = norm_backward(normed_grad, norm_ffn, factor_two, scaled_two)
    grad_hidden = grad_result + grad_hidden_norm
    grad_attn = grad_hidden.astype(jnp.bfloat16)
    grad_w_out = jnp.einsum("sa,sd->ad", attended, grad_attn, preferred_element_type=jnp.float32)
    grad_attended = (
        jnp.einsum("sd,ad->sa", grad_attn, w_out, preferred_element_type=jnp.float32)
        .astype(jnp.bfloat16)
        .reshape(seq_len, kv_heads, group_size, head_dim)
    )
    probs_again = jnp.exp(score_block() - log_total)
    grad_probs = jnp.einsum(
        "ikgd,jkd->kgij", grad_attended, values, preferred_element_type=jnp.float32
    )
    row_dot = jnp.sum(probs_again * grad_probs, axis=-1, keepdims=True)
    grad_scores = (probs_again * (grad_probs - row_dot)).astype(jnp.bfloat16)
    grad_query = (
        (
            jnp.einsum("kgij,jkd->ikgd", grad_scores, keys, preferred_element_type=jnp.float32)
            * score_scale
        )
        .astype(jnp.bfloat16)
        .reshape(seq_len, q_heads * head_dim)
    )
    grad_keys = (
        (
            jnp.einsum("kgij,ikgd->jkd", grad_scores, query, preferred_element_type=jnp.float32)
            * score_scale
        )
        .astype(jnp.bfloat16)
        .reshape(seq_len, kv_heads * head_dim)
    )
    grad_values = (
        jnp.einsum(
            "kgij,ikgd->jkd",
            probs_again.astype(jnp.bfloat16),
            grad_attended,
            preferred_element_type=jnp.float32,
        )
        .astype(jnp.bfloat16)
        .reshape(seq_len, kv_heads * head_dim)
    )

    grad_qkv = jnp.concatenate([grad_query, grad_keys, grad_values], axis=1)
    grad_w_qkv = dot_rows(normed_one, grad_qkv).astype(jnp.bfloat16).reshape(16, -1, grad_qkv.shape[1])
    attn_back_part = jnp.einsum(
        "sa,da->sd", grad_query, w_query, preferred_element_type=jnp.float32
    )
    attn_back_part = attn_back_part + jnp.einsum(
        "sa,da->sd", grad_keys, w_key, preferred_element_type=jnp.float32
    )
    attn_back_part = attn_back_part + jnp.einsum(
        "sa,da->sd", grad_values, w_value, preferred_element_type=jnp.float32
    )
    normed_grad_one = lax.psum(attn_back_part.astype(jnp.bfloat16), "tensor").astype(jnp.float32)
    grad_input_norm, grad_norm_attn = norm_backward(
        normed_grad_one, norm_attn, factor_one, scaled_one
    )
    grad_tokens = (grad_hidden + grad_input_norm).astype(jnp.bfloat16)

    gains = jnp.concatenate([grad_norm_attn, grad_norm_ffn]).reshape(8, -1)
    grad_w_qkv, grad_w_out, gains = reduce_grads(
        grad_w_qkv, grad_w_out.astype(jnp.bfloat16).reshape(16, -1, width), gains
    )
    grad_w_qkv = grad_w_qkv.reshape(width, -1).astype(jnp.float32)
    at = (q_heads * head_dim, (q_heads + kv_heads) * head_dim)
    gains = gains.reshape(2, -1)
    return (
        output, grad_tokens, gains[0], grad_w_qkv[:, : at[0]], grad_w_qkv[:, at[0] : at[1]], grad_w_qkv[:, at[1] :],
        grad_w_out.reshape(-1, width).astype(jnp.float32), gains[1], grad_shared_gate, grad_shared_up, grad_shared_down,
        grad_expert_gate, grad_expert_up, grad_expert_down,
    )


def shards(
    tokens,
    doc_lens,
    routes,
    gate_weights,
    norm_attn,
    w_query,
    w_key,
    w_value,
    w_out,
    norm_ffn,
    shared_gate,
    shared_up,
    shared_down,
    expert_gate,
    expert_up,
    expert_down,
    cotangent,
):
    seq_len, width = tokens.shape
    head_dim = DH
    kv_heads = w_key.shape[1] // head_dim
    q_heads = w_query.shape[1] // head_dim
    group_size = q_heads // kv_heads
    score_scale = head_dim ** (-0.5)
    expert_count = lax.axis_size("dp") * expert_gate.shape[0]
    capacity = 3 * seq_len * routes.shape[1] // (2 * expert_count)
    positions = jnp.arange(seq_len, dtype=jnp.int32)
    doc_ends = jnp.cumsum(doc_lens[0])
    doc_index = jnp.sum((positions[:, None] >= doc_ends[None, :]).astype(jnp.int32), axis=1)
    visible = (doc_index[:, None] == doc_index[None, :]) & (
        positions[None, :] <= positions[:, None]
    )
    inputs = tokens.astype(jnp.float32)
    factor_one = rms_factor(inputs)
    scaled_one = inputs * factor_one
    normed_one = (scaled_one * norm_attn).astype(jnp.bfloat16)
    query = (
        jnp.dot(normed_one, w_query, preferred_element_type=jnp.float32)
        .astype(jnp.bfloat16)
        .reshape(seq_len, kv_heads, group_size, head_dim)
    )
    keys = (
        jnp.dot(normed_one, w_key, preferred_element_type=jnp.float32)
        .astype(jnp.bfloat16)
        .reshape(seq_len, kv_heads, head_dim)
    )
    values = (
        jnp.dot(normed_one, w_value, preferred_element_type=jnp.float32)
        .astype(jnp.bfloat16)
        .reshape(seq_len, kv_heads, head_dim)
    )

    def score_block():
        raw = (
            jnp.einsum("ikgd,jkd->kgij", query, keys, preferred_element_type=jnp.float32)
            * score_scale
        )
        return jnp.where(visible, raw, masked_value)

    scores = score_block()
    row_max = jnp.max(scores, axis=-1, keepdims=True)
    log_total = row_max + jnp.log(jnp.sum(jnp.exp(scores - row_max), axis=-1, keepdims=True))
    probs_low = jnp.exp(scores - log_total).astype(jnp.bfloat16)
    attended = (
        jnp.einsum("kgij,jkd->ikgd", probs_low, values, preferred_element_type=jnp.float32)
        .astype(jnp.bfloat16)
        .reshape(seq_len, q_heads * head_dim)
    )
    attn_part = jnp.dot(attended, w_out, preferred_element_type=jnp.float32)
    hidden_state = inputs + lax.psum(attn_part, "tensor")
    factor_two = rms_factor(hidden_state)
    scaled_two = hidden_state * factor_two
    normed_two = (scaled_two * norm_ffn).astype(jnp.bfloat16)
    shared_gated = jnp.dot(normed_two, shared_gate, preferred_element_type=jnp.float32)
    shared_upward = jnp.dot(normed_two, shared_up, preferred_element_type=jnp.float32)
    shared_hidden = (shared_gated * jax.nn.sigmoid(shared_gated) * shared_upward).astype(
        jnp.bfloat16
    )
    shared_part = jnp.dot(shared_hidden, shared_down, preferred_element_type=jnp.float32)
    position = slot_positions(routes, expert_count)
    owners = jnp.repeat(positions, routes.shape[1])
    slot_rows = (
        jnp.full((expert_count, capacity), seq_len, jnp.int32)
        .at[routes.reshape(-1), position.reshape(-1)]
        .set(owners)
    )
    padded = jnp.concatenate([normed_two, jnp.zeros((1, width), jnp.bfloat16)], axis=0)
    dispatched = to_experts(padded[slot_rows])
    local_rows = dispatched.reshape(-1, width)
    expert_gated = jnp.dot(local_rows, expert_gate[0], preferred_element_type=jnp.float32)
    expert_upward = jnp.dot(local_rows, expert_up[0], preferred_element_type=jnp.float32)
    expert_hidden = (expert_gated * jax.nn.sigmoid(expert_gated) * expert_upward).astype(
        jnp.bfloat16
    )
    expert_part = jnp.dot(
        expert_hidden, expert_down[0], preferred_element_type=jnp.float32
    ).reshape(dispatched.shape)
    returned = from_experts(expert_part)
    mixture = jnp.sum(gate_weights[:, :, None] * returned[routes, position], axis=1)
    branches = lax.psum(shared_part.astype(jnp.bfloat16), "tensor").astype(jnp.float32) + mixture
    output = (hidden_state + branches).astype(jnp.bfloat16)
    grad_result = cotangent.astype(jnp.float32)
    grad_shared_down = jnp.einsum(
        "sf,sd->fd", shared_hidden, cotangent, preferred_element_type=jnp.float32
    )
    grad_shared_hidden = jnp.einsum(
        "sd,fd->sf", cotangent, shared_down, preferred_element_type=jnp.float32
    )
    grad_sg, grad_su = swish_grads(shared_gated, shared_upward, grad_shared_hidden)
    grad_shared_gate = jnp.einsum(
        "sd,sf->df", normed_two, grad_sg, preferred_element_type=jnp.float32
    )
    grad_shared_up = jnp.einsum(
        "sd,sf->df", normed_two, grad_su, preferred_element_type=jnp.float32
    )
    shared_back_part = jnp.einsum(
        "sf,df->sd", grad_sg, shared_gate, preferred_element_type=jnp.float32
    ) + jnp.einsum("sf,df->sd", grad_su, shared_up, preferred_element_type=jnp.float32)
    routed_grad = (gate_weights[:, :, None] * grad_result[:, None, :]).astype(jnp.bfloat16)
    back_buffer = (
        jnp.zeros((expert_count, capacity, width), jnp.bfloat16)
        .at[routes, position]
        .set(routed_grad)
    )
    arrived_grad = to_experts(back_buffer).reshape(-1, width)
    grad_expert_down = jnp.einsum(
        "rf,rd->fd", expert_hidden, arrived_grad, preferred_element_type=jnp.float32
    )[None]
    grad_expert_hidden = jnp.einsum(
        "rd,fd->rf", arrived_grad, expert_down[0], preferred_element_type=jnp.float32
    )
    grad_eg, grad_eu = swish_grads(expert_gated, expert_upward, grad_expert_hidden)
    grad_expert_gate = jnp.einsum(
        "rd,rf->df", local_rows, grad_eg, preferred_element_type=jnp.float32
    )[None]
    grad_expert_up = jnp.einsum(
        "rd,rf->df", local_rows, grad_eu, preferred_element_type=jnp.float32
    )[None]
    expert_back_part = (
        jnp.einsum("rf,df->rd", grad_eg, expert_gate[0], preferred_element_type=jnp.float32)
        + jnp.einsum("rf,df->rd", grad_eu, expert_up[0], preferred_element_type=jnp.float32)
    ).reshape(dispatched.shape)
    returned_grad = from_experts(expert_back_part)
    routed_back = jnp.sum(returned_grad[routes, position], axis=1)
    normed_grad = (
        lax.psum(shared_back_part.astype(jnp.bfloat16), "tensor").astype(jnp.float32) + routed_back
    )
    grad_hidden_norm, grad_norm_ffn = norm_backward(normed_grad, norm_ffn, factor_two, scaled_two)
    grad_hidden = grad_result + grad_hidden_norm
    grad_attn = grad_hidden.astype(jnp.bfloat16)
    grad_w_out = jnp.einsum("sa,sd->ad", attended, grad_attn, preferred_element_type=jnp.float32)
    grad_attended = (
        jnp.einsum("sd,ad->sa", grad_attn, w_out, preferred_element_type=jnp.float32)
        .astype(jnp.bfloat16)
        .reshape(seq_len, kv_heads, group_size, head_dim)
    )
    probs_again = jnp.exp(score_block() - log_total)
    grad_probs = jnp.einsum(
        "ikgd,jkd->kgij", grad_attended, values, preferred_element_type=jnp.float32
    )
    row_dot = jnp.sum(probs_again * grad_probs, axis=-1, keepdims=True)
    grad_scores = (probs_again * (grad_probs - row_dot)).astype(jnp.bfloat16)
    grad_query = (
        (
            jnp.einsum("kgij,jkd->ikgd", grad_scores, keys, preferred_element_type=jnp.float32)
            * score_scale
        )
        .astype(jnp.bfloat16)
        .reshape(seq_len, q_heads * head_dim)
    )
    grad_keys = (
        (
            jnp.einsum("kgij,ikgd->jkd", grad_scores, query, preferred_element_type=jnp.float32)
            * score_scale
        )
        .astype(jnp.bfloat16)
        .reshape(seq_len, kv_heads * head_dim)
    )
    grad_values = (
        jnp.einsum(
            "kgij,ikgd->jkd",
            probs_again.astype(jnp.bfloat16),
            grad_attended,
            preferred_element_type=jnp.float32,
        )
        .astype(jnp.bfloat16)
        .reshape(seq_len, kv_heads * head_dim)
    )
    grad_w_query = jnp.einsum(
        "sd,sa->da", normed_one, grad_query, preferred_element_type=jnp.float32
    )
    grad_w_key = jnp.einsum("sd,sa->da", normed_one, grad_keys, preferred_element_type=jnp.float32)
    grad_w_value = jnp.einsum(
        "sd,sa->da", normed_one, grad_values, preferred_element_type=jnp.float32
    )
    attn_back_part = jnp.einsum(
        "sa,da->sd", grad_query, w_query, preferred_element_type=jnp.float32
    )
    attn_back_part = attn_back_part + jnp.einsum(
        "sa,da->sd", grad_keys, w_key, preferred_element_type=jnp.float32
    )
    attn_back_part = attn_back_part + jnp.einsum(
        "sa,da->sd", grad_values, w_value, preferred_element_type=jnp.float32
    )
    normed_grad_one = lax.psum(attn_back_part.astype(jnp.bfloat16), "tensor").astype(jnp.float32)
    grad_input_norm, grad_norm_attn = norm_backward(
        normed_grad_one, norm_attn, factor_one, scaled_one
    )
    grad_tokens = (grad_hidden + grad_input_norm).astype(jnp.bfloat16)
    summed = lax.psum(
        (
            grad_norm_attn,
            grad_w_query,
            grad_w_key,
            grad_w_value,
            grad_w_out,
            grad_norm_ffn,
            grad_shared_gate,
            grad_shared_up,
            grad_shared_down,
        ),
        "dp",
    )
    return (
        output,
        grad_tokens,
        summed[0],
        summed[1],
        summed[2],
        summed[3],
        summed[4],
        summed[5],
        summed[6],
        summed[7],
        summed[8],
        grad_expert_gate,
        grad_expert_up,
        grad_expert_down,
    )


def solution(mesh):
    fast = mesh.shape["dp"] == 16 and mesh.shape["tensor"] == 2
    return jax.shard_map(
        shards_fast if fast else shards,
        mesh=mesh,
        in_specs=(
            P("dp", None),
            P("dp", None),
            P("dp", None),
            P("dp", None),
            P(),
            P(None, "tensor"),
            P(None, "tensor"),
            P(None, "tensor"),
            P("tensor", None),
            P(),
            P(None, "tensor"),
            P(None, "tensor"),
            P("tensor", None),
            P("dp", None, "tensor"),
            P("dp", None, "tensor"),
            P("dp", "tensor", None),
            P("dp", None),
        ),
        out_specs=(
            P("dp", None),
            P("dp", None),
            P(),
            P(None, "tensor"),
            P(None, "tensor"),
            P(None, "tensor"),
            P("tensor", None),
            P(),
            P(None, "tensor"),
            P(None, "tensor"),
            P("tensor", None),
            P("dp", None, "tensor"),
            P("dp", None, "tensor"),
            P("dp", "tensor", None),
        ),
        check_vma=False,
    )
```

```python
import functools
import jax
import jax.numpy as jnp
from jax import lax
from jax.experimental import pallas as pl
from jax.experimental.pallas import tpu as pltpu
from jax.sharding import PartitionSpec as P

DH = 128


epsilon = 1e-05
masked_value = -1e30


def rms_factor(values):
    return lax.rsqrt(jnp.mean(values * values, axis=-1, keepdims=True) + epsilon)


def norm_backward(grad_normed, gain_vector, factor, scaled):
    grad_scaled = grad_normed * gain_vector
    inner_mean = jnp.mean(grad_scaled * scaled, axis=-1, keepdims=True)
    return (factor * (grad_scaled - scaled * inner_mean), jnp.sum(grad_normed * scaled, axis=0))


def swish_grads(gated, upward, grad_hidden):
    sigma = jax.nn.sigmoid(gated)
    grad_gated = grad_hidden * upward * sigma * (1.0 + gated * (1.0 - sigma))
    grad_upward = grad_hidden * gated * sigma
    return (grad_gated.astype(jnp.bfloat16), grad_upward.astype(jnp.bfloat16))


def slot_positions(routes, expert_count):
    flat_routes = routes.reshape(-1)
    onehot = (flat_routes[:, None] == jnp.arange(expert_count, dtype=jnp.int32)[None, :]).astype(
        jnp.int32
    )
    earlier = jnp.cumsum(onehot, axis=0) - onehot
    return jnp.sum(earlier * onehot, axis=1).reshape(routes.shape)


def to_experts(buffer):
    return lax.all_to_all(buffer, "dp", split_axis=0, concat_axis=0, tiled=True)


def from_experts(partial_value):
    own_part = lax.psum_scatter(
        partial_value.astype(jnp.bfloat16), "tensor", scatter_dimension=1, tiled=True
    ).astype(jnp.float32)
    joined = lax.all_gather(own_part.astype(jnp.bfloat16), "tensor", axis=1, tiled=True).astype(
        own_part.dtype
    )
    return lax.all_to_all(
        joined.astype(jnp.bfloat16), "dp", split_axis=0, concat_axis=0, tiled=True
    ).astype(joined.dtype)


MESH = pl.DeviceIdType.MESH
ANY = pl.BlockSpec(memory_space=pl.ANY)
VMEM = pl.BlockSpec(memory_space=pltpu.VMEM)
DMA = pltpu.SemaphoreType.DMA
bf16, f32 = jnp.bfloat16, jnp.float32


def dot(first, second):
    return jnp.dot(first, second, preferred_element_type=f32)


def dot_t(first, second):
    return lax.dot_general(first, second, (((1,), (1,)), ((), ())), preferred_element_type=f32)


def dot_rows(first, second):
    return lax.dot_general(first, second, (((0,), (0,)), ((), ())), preferred_element_type=f32)


class Place:
    def __init__(self):
        self.dp = lax.axis_index("dp")
        self.t = lax.axis_index("tensor")
        self.x, self.y, self.z = self.dp % 2, (self.dp // 2) % 2, self.dp // 4
        digits = [0xE4, 0xE1, 0x1E, 0x1B]
        code = sum(jnp.where(self.z == i, d, 0) for i, d in enumerate(digits))
        self.near = lambda n: (code // (4**n if isinstance(n, int) else jnp.where(n == 0, 1, jnp.where(n == 1, 4, jnp.where(n == 2, 16, 64))))) % 4

    def flip(self, dx, dy, z):
        return z * 4 + (self.y + dy) % 2 * 2 + (self.x + dx) % 2

    def rel(self, da, db, z):
        t = self.t
        return self.flip((1 - t) * da + t * db, t * da + (1 - t) * db, z)

    def core(self):
        return (self.dp, 1 - self.t)

    def a(self):
        return (self.rel(1, 0, self.z), self.t)

    def b(self):
        return (self.rel(0, 1, self.z), self.t)

    def at_z(self, z):
        return (self.rel(0, 0, z), self.t)


def greet(place):
    barrier = pltpu.get_barrier_semaphore()
    partners = [place.core(), place.a(), place.b()] + [place.at_z((place.z + k) % 4) for k in (1, 2, 3)]
    for partner in partners:
        pl.semaphore_signal(barrier, inc=1, device_id=partner, device_id_type=MESH)
    pl.semaphore_wait(barrier, len(partners))


def remote(src, dst, send, recv, device):
    return pltpu.make_async_remote_copy(
        src_ref=src, dst_ref=dst, send_sem=send, recv_sem=recv, device_id=device, device_id_type=MESH
    )


class Gather:
    def __init__(self, place, part, sems, swap):
        self.p, self.part, self.swap = place, part, swap
        self.us, self.ds, self.zr, self.as_, self.ar, self.bs, self.br = sems[:7]
        if swap:
            self.cs, self.cr = sems[7:9]

    def copy(self, j, send, recv, device):
        return remote(self.part(j), self.part(j), send, recv, device)

    def up(self, z):
        p = self.p
        return self.copy(p.rel(0, 0, z), self.us.at[z], self.zr.at[z], p.at_z((p.z + 1) % 4))

    def down(self, z):
        p = self.p
        return self.copy(p.rel(0, 0, z), self.ds.at[z], self.zr.at[z], p.at_z((p.z + 3) % 4))

    def to_a(self, z):
        return self.copy(self.p.rel(0, 0, z), self.as_.at[z], self.ar.at[z], self.p.a())

    def from_a(self, z):
        return self.copy(self.p.rel(1, 0, z), self.as_.at[z], self.ar.at[z], self.p.a())

    def to_b(self, da, z):
        return self.copy(self.p.rel(da, 0, z), self.bs.at[da, z], self.br.at[da, z], self.p.b())

    def from_b(self, da, z):
        return self.copy(self.p.rel(da, 1, z), self.bs.at[da, z], self.br.at[da, z], self.p.b())

    def to_core(self, j):
        return self.copy(j, self.cs.at[j], self.cr.at[j], self.p.core())

    def ups(self, z):
        return jnp.logical_and(z <= self.p.z, self.p.z < 3)

    def downs(self, z):
        return jnp.logical_and(z >= self.p.z, self.p.z > 0)

    def spread(self, z):
        pl.when(self.ups(z))(lambda: self.up(z).start())
        pl.when(self.downs(z))(lambda: self.down(z).start())
        self.to_b(0, z).start()
        self.to_a(z).start()

    def start(self):
        self.spread(self.p.z)

    def got_z(self, n):
        z = self.p.near(n)
        self.up(z).wait_recv()
        self.spread(z)
        if self.swap:
            self.to_core(self.p.rel(0, 0, z)).start()

    def got_a(self, n):
        z = self.p.near(n)
        self.from_a(z).wait_recv()
        self.to_b(1, z).start()
        if self.swap:
            self.to_core(self.p.rel(1, 0, z)).start()

    def got_b(self, da, n):
        z = self.p.near(n)
        self.from_b(da, z).wait_recv()
        if self.swap:
            self.to_core(self.p.rel(da, 1, z)).start()

    def wait_core(self, j):
        self.to_core(j).wait_recv()

    def finish(self):
        def ends(z, _):
            pl.when(self.ups(z))(lambda: self.up(z).wait_send())
            pl.when(self.downs(z))(lambda: self.down(z).wait_send())
            self.to_a(z).wait_send()
            self.to_b(0, z).wait_send()
            self.to_b(1, z).wait_send()
            return 0

        lax.fori_loop(0, 4, ends, 0)
        if self.swap:

            def swaps(i, _):
                self.to_core((self.p.dp + 1 + i) % 16).wait_send()
                return 0

            lax.fori_loop(0, 15, swaps, 0)


def gather_sems(swap):
    return [DMA(kind) for kind in [(4,)] * 5 + [(2, 4)] * 2 + [(16,)] * (2 * swap)]


def add_into(dst, src):
    def step(i, _):
        at = pl.ds(pl.multiple_of(i * 16, 16), 16)
        dst[at, :] = dst[at, :] + src[at, :]
        return 0

    lax.fori_loop(0, dst.shape[0] // 16, step, 0)


class Scatter:
    def __init__(self, place, own, land, sems):
        self.p, self.own = place, own
        self.rb, self.ra, self.rz = land
        self.bs, self.br, self.as_, self.ar, self.zs, self.zr = sems

    def to_b(self, da, z):
        j = self.p.rel(da, 1, z)
        return remote(self.own.at[j], self.rb.at[da, z], self.bs.at[da, z], self.br.at[da, z], self.p.b())

    def to_a(self, z):
        j = self.p.rel(1, 0, z)
        return remote(self.own.at[j], self.ra.at[z], self.as_.at[z], self.ar.at[z], self.p.a())

    def to_z(self, k):
        z = (self.p.z + k) % 4
        return remote(self.own.at[self.p.rel(0, 0, z)], self.rz.at[k - 1], self.zs.at[k - 1], self.zr.at[k - 1], self.p.at_z(z))

    def got_b(self, da, z):
        self.to_b(da, z).wait_recv()
        add_into(self.own.at[self.p.rel(da, 0, z)], self.rb.at[da, z])

    def got_a(self, z):
        self.to_a(z).wait_recv()
        add_into(self.own.at[self.p.rel(0, 0, z)], self.ra.at[z])

    def far(self, k):
        z = (self.p.z + k) % 4
        self.got_b(1, z)
        self.to_a(z).start()

    def close(self, k):
        z = (self.p.z + k) % 4
        self.got_b(0, z)
        self.got_a(z)
        pl.when(k != 0)(lambda: self.to_z(k).start())

    def total(self, put):
        for k in (1, 2, 3):
            self.to_z(k).wait_recv()
        mine = self.own.at[self.p.dp]

        def step(i, _):
            at = pl.ds(pl.multiple_of(i * 16, 16), 16)
            total = mine[at, :].astype(f32)
            for k in range(3):
                total = total + self.rz[k, at, :].astype(f32)
            put(at, total)
            return 0

        lax.fori_loop(0, mine.shape[0] // 16, step, 0)

    def finish(self):
        def ends(z, _):
            self.to_a(z).wait_send()
            self.to_b(0, z).wait_send()
            self.to_b(1, z).wait_send()
            return 0

        lax.fori_loop(0, 4, ends, 0)
        for k in (1, 2, 3):
            self.to_z(k).wait_send()


def scatter_land(rows, cols):
    return [pltpu.VMEM((2, 4, rows, cols), bf16), pltpu.VMEM((4, rows, cols), bf16), pltpu.VMEM((3, rows, cols), bf16)]


def scatter_sems():
    return [DMA(kind) for kind in [(2, 4), (2, 4), (4,), (4,), (3,), (3,)]]


def row_mean(values):
    return jnp.sum(values, axis=1, keepdims=True) * (1.0 / values.shape[1])


def factor_of(values):
    return lax.rsqrt(row_mean(values * values) + epsilon)


def visible_in(lens, seq):
    rows = lax.broadcasted_iota(jnp.int32, (seq, seq), 0)
    cols = lax.broadcasted_iota(jnp.int32, (seq, seq), 1)
    first, second = lens[0, 0], lens[0, 0] + lens[0, 1]

    def doc(i):
        return (i >= first).astype(jnp.int32) + (i >= second).astype(jnp.int32)

    return jnp.logical_and(doc(rows) == doc(cols), cols <= rows)


def group_rows(values, g, heads):
    cols = [values[:, (heads * g + h) * DH : (heads * g + h + 1) * DH] for h in range(heads)]
    return jnp.concatenate(cols, axis=0)


def group_probs(query, keys, visible):
    seq = keys.shape[0]
    scores = dot_t(query, keys) * DH ** (-0.5)
    scores = jnp.where(visible[None], scores.reshape(-1, seq, seq), masked_value).reshape(scores.shape)
    top = jnp.max(scores, axis=1, keepdims=True)
    exps = jnp.exp(scores - top)
    return exps / jnp.sum(exps, axis=1, keepdims=True)


def swish_all(gated, upward, grad):
    sigma = jax.nn.sigmoid(gated)
    active = gated * sigma
    grad_gated = grad * upward * (sigma * (1.0 + gated * (1.0 - sigma)))
    return active * upward, grad_gated.astype(bf16), (grad * active).astype(bf16)


def place_of(p, i):
    n = jnp.where(i < 4, i, jnp.where(i < 12, (i - 4) // 2, i - 12))
    dx = jnp.where(i < 4, 0, jnp.where(i < 12, (i + 1) % 2, 1))
    dy = jnp.where(i < 4, 0, jnp.where(i < 12, i % 2, 1))
    return dx, dy, p.near(n)


def front_kernel(
    tokens, lens, gates, gain1, gain2, cot,
    hq, hk, hv, ho, heg, heu, hed, hsg, hsu, hsd,
    n2_all, cot_all, qkv, attended, hidden, mix_all, acts_all, grad2,
    wq, wk, wv, wo, weg, weu, wed, wsg, wsu, wsd, wsem,
    n2v, gall, apart, cbuf, mstage, astage, dstage, own, came, rb, ra, rz, res,
    asem, csem, msem, ksem, dsem, dcame, credit, lsem, fsem, *sems
):
    p = Place()
    nc = 9
    n2g = Gather(p, lambda j: n2v.at[j, :, pl.ds(pl.multiple_of(p.t * 768, 768), 768)], sems[:nc], True)
    ctg = Gather(p, lambda j: cot_all.at[j, :, pl.ds(pl.multiple_of(p.t * 768, 768), 768)], sems[nc : 2 * nc], True)
    gtg = Gather(p, lambda j: gall.at[j], sems[2 * nc : 2 * nc + 7], False)
    sct = Scatter(p, own, (rb, ra, rz), sems[2 * nc + 7 :])
    mine = pl.multiple_of(p.t * 768, 768)
    other = pl.multiple_of((1 - p.t) * 768, 768)

    own_cot = pltpu.make_async_copy(cot, cot_all.at[p.dp], lsem.at[0])
    own_cot.start()
    pairs = list(zip((hq, hk, hv, ho, heg, heu, hed, hsg, hsu, hsd), (wq, wk, wv, wo, weg, weu, wed, wsg, wsu, wsd)))
    loads = [pltpu.make_async_copy(s, d, wsem.at[i]) for i, (s, d) in enumerate(pairs)]
    for load in loads[:4]:
        load.start()
    gall[p.dp] = gates[...]
    greet(p)
    own_cot.wait()
    ctg.start()
    gtg.start()
    for load in loads[4:]:
        load.start()

    def both_z(n):
        ctg.got_z(n)
        gtg.got_z(n)

    def both_a(n):
        ctg.got_a(n)
        gtg.got_a(n)

    def both_b(da, n):
        ctg.got_b(da, n)
        gtg.got_b(da, n)

    inputs = tokens[...].astype(f32)
    n1 = (inputs * factor_of(inputs) * gain1[...]).astype(bf16)
    for load in loads[:4]:
        load.wait()
    qkv[:, :768] = dot(n1, wq[...]).astype(bf16)
    both_z(1)
    qkv[:, 768:1024] = dot(n1, wk[...]).astype(bf16)
    qkv[:, 1024:] = dot(n1, wv[...]).astype(bf16)
    visible = visible_in(lens, 256)
    for g in range(2):
        query = group_rows(qkv[:, :768], g, 3)
        probs = group_probs(query, qkv[:, 768 + g * DH : 768 + (g + 1) * DH], visible).astype(bf16)
        out = dot(probs, qkv[:, 1024 + g * DH : 1024 + (g + 1) * DH]).astype(bf16)
        for h in range(3):
            attended[:, (3 * g + h) * DH : (3 * g + h + 1) * DH] = out[h * 256 : (h + 1) * 256, :]
        if g == 0:
            both_z(2)
            both_a(0)
    apart[...] = dot(attended[...], wo[...])
    swap_a = remote(apart, hidden, asem.at[0], asem.at[1], p.core())
    swap_a.start()
    both_z(3)
    both_a(1)
    swap_a.wait()
    hidden[...] = tokens[...].astype(f32) + (apart[...] + hidden[...])
    state = hidden[...]
    n2v[p.dp] = (state * factor_of(state) * gain2[...]).astype(bf16)
    n2g.start()
    for load in loads[4:]:
        load.wait()

    def cot_load(i):
        dx, dy, z = place_of(p, i)
        return pltpu.make_async_copy(cot_all.at[p.flip(dx, dy, z)], cbuf.at[i % 2], csem.at[i % 2])

    def mix_out(i):
        dx, dy, z = place_of(p, i)
        return pltpu.make_async_copy(mstage.at[i % 2], mix_all.at[p.flip(dx, dy, z)], msem.at[i % 2])

    def acts_out(i):
        dx, dy, z = place_of(p, i)
        return pltpu.make_async_copy(astage.at[i % 2], acts_all.at[p.flip(dx, dy, z)], ksem.at[i % 2])

    def swap_d(i):
        return remote(dstage.at[i % 2, :, pl.ds(other, 768)], came.at[i % 4], dsem.at[i % 2], dcame.at[i % 4], p.core())

    def paired(i):
        dx, dy, z = place_of(p, i)
        j = p.flip(dx, dy, z)
        swap_d(i).wait_recv()
        add_into(own.at[j], came.at[i % 4])
        pl.when(i < 12)(lambda: pl.semaphore_signal(credit, inc=1, device_id=p.core(), device_id_type=MESH))
        da = (1 - p.t) * dx + p.t * dy
        db = (1 - p.t) * dy + p.t * dx
        pl.when(db == 1)(lambda: sct.to_b(da, z).start())

    cot_load(0).start()

    def step(i, _):
        dx, dy, z = place_of(p, i)
        j = p.flip(dx, dy, z)

        @pl.when(jnp.logical_and(i >= 1, i < 3))
        def _():
            both_a(i + 1)

        pl.when(jnp.logical_and(i >= 1, i < 4))(lambda: n2g.got_z(i))
        pl.when(jnp.logical_and(i >= 3, i < 7))(lambda: n2g.got_a(i - 3))
        pl.when(i < 4)(lambda: both_b(0, i))
        pl.when(jnp.logical_and(i >= 3, i < 7))(lambda: n2g.got_b(0, i - 3))
        pl.when(jnp.logical_and(i >= 6, i < 10))(lambda: both_b(1, i - 6))
        pl.when(jnp.logical_and(i >= 9, i < 13))(lambda: n2g.got_b(1, i - 9))
        cot_load(i).wait()

        @pl.when(i < 15)
        def _():
            dx, dy, z = place_of(p, i + 1)
            ctg.wait_core(p.flip(dx, dy, z))
            cot_load(i + 1).start()

        pl.when(i > 0)(lambda: n2g.wait_core(j))

        @pl.when(i >= 2)
        def _():
            mix_out(i - 2).wait()
            acts_out(i - 2).wait()
            swap_d(i - 2).wait_send()

        slot = i % 2
        rows, cots = n2v.at[j], cbuf.at[slot]
        gate = jnp.transpose(jnp.broadcast_to(gall[j, pl.ds(p.dp, 1), :], (128, 256)))[:, :1]
        gated, upward = dot(rows[...], weg[...]), dot(rows[...], weu[...])
        hid, dg, du = swish_all(gated, upward, dot_t(cots[...], wed[...]) * gate)
        hid = (gate * hid).astype(bf16)
        astage[slot, :, 0:256] = dg
        astage[slot, :, 256:512] = du
        astage[slot, :, 1536:1792] = hid
        mstage[slot] = dot(hid, wed[...]).astype(bf16)
        dstage[slot] = (dot_t(dg, weg[...]) + dot_t(du, weu[...])).astype(bf16)
        gated, upward = dot(rows[...], wsg[...]), dot(rows[...], wsu[...])
        hid, dg, du = swish_all(gated, upward, dot_t(cots[...], wsd[...]))
        astage[slot, :, 512:1024] = dg
        astage[slot, :, 1024:1536] = du
        astage[slot, :, 1792:] = hid.astype(bf16)

        @pl.when(i == 0)
        def _():
            mstage[slot] = (mstage[slot].astype(f32) + dot(astage[slot, :, 1792:], wsd[...])).astype(bf16)
            back = dot_t(astage[slot, :, 512:1024], wsg[...]) + dot_t(astage[slot, :, 1024:1536], wsu[...])
            dstage[slot] = (dstage[slot].astype(f32) + back).astype(bf16)

        mix_out(i).start()
        acts_out(i).start()
        pl.when(i >= 4)(lambda: pl.semaphore_wait(credit, 1))
        swap_d(i).start()
        own[j] = dstage[slot, :, pl.ds(mine, 768)]
        pl.when(i > 0)(lambda: paired(i - 1))
        return 0

    lax.fori_loop(0, 16, step, 0)
    paired(15)
    n2_out = pltpu.make_async_copy(n2v, n2_all, lsem.at[0])
    n2_out.start()

    def far(k, _):
        sct.far(k)
        return 0

    def close(i, _):
        sct.close((i + 1) % 4)
        return 0

    lax.fori_loop(0, 4, far, 0)
    lax.fori_loop(0, 4, close, 0)

    def put(at, total):
        res[at, :] = total

    sct.total(put)
    swap_r = remote(res, grad2.at[:, pl.ds(mine, 768)], fsem.at[0], fsem.at[1], p.core())
    keep_r = pltpu.make_async_copy(res, grad2.at[:, pl.ds(mine, 768)], fsem.at[2])
    swap_r.start()
    keep_r.start()
    for i in (14, 15):
        mix_out(i).wait()
        acts_out(i).wait()
        swap_d(i).wait_send()
    n2g.finish()
    ctg.finish()
    gtg.finish()
    sct.finish()
    n2_out.wait()
    keep_r.wait()
    swap_r.wait()


def front(tokens, lens, gates, gain1, gain2, cot, *weights):
    big = (16, 256, 1536)
    half = (16, 256, 768)
    sds = jax.ShapeDtypeStruct
    scratch = [pltpu.VMEM(w.shape, bf16) for w in weights] + [DMA((10,))]
    scratch += [
        pltpu.VMEM(big, bf16), pltpu.VMEM((16, 16, 256), f32), pltpu.VMEM((256, 1536), f32),
        pltpu.VMEM((2, 256, 1536), bf16), pltpu.VMEM((2, 256, 1536), bf16), pltpu.VMEM((2, 256, 2304), bf16),
        pltpu.VMEM((2, 256, 1536), bf16), pltpu.VMEM(half, bf16), pltpu.VMEM((4, 256, 768), bf16),
    ]
    scratch += scatter_land(256, 768) + [pltpu.VMEM((256, 768), f32)]
    scratch += [DMA((2,)), DMA((2,)), DMA((2,)), DMA((2,)), DMA((2,)), DMA((4,)), pltpu.SemaphoreType.REGULAR, DMA((1,)), DMA((3,))]
    scratch += gather_sems(True) + gather_sems(True) + gather_sems(False) + scatter_sems()
    return pl.pallas_call(
        front_kernel,
        out_shape=(
            sds(big, bf16), sds(big, bf16), sds((256, 1280), bf16), sds((256, 768), bf16), sds((256, 1536), f32),
            sds(big, bf16), sds((16, 256, 2304), bf16), sds((256, 1536), f32),
        ),
        in_specs=[VMEM, pl.BlockSpec(memory_space=pltpu.SMEM), VMEM, VMEM, VMEM, ANY] + [ANY] * 10,
        out_specs=(ANY, ANY, VMEM, VMEM, VMEM, ANY, ANY, ANY),
        scratch_shapes=scratch,
        compiler_params=pltpu.CompilerParams(collective_id=1, has_side_effects=True, vmem_limit_bytes=63 << 20),
    )(tokens, lens, gates, gain1, gain2, cot, *weights)


def back_kernel(
    grad2, hidden, tokens, cot, gain1, gain2, qkv, attended, lens,
    hq, hk, hv, ho, mix_all,
    output, grad_tokens, sum_a, sum_b, sum_n,
    wq, wk, wv, wo, wsem, mown, mcame, mrb, mra, mrz, mres, mother,
    ga, gb, arb, ara, arz, brb, bra, brz, blk_a, blk_b, gain_all, dqkv, dpart, dcame,
    msem, mcs, mcr, dsem, fsem, lsem, *sems
):
    p = Place()
    mix = Scatter(p, mown, (mrb, mra, mrz), sems[:6])
    sa = Scatter(p, ga, (arb, ara, arz), sems[6:12])
    sb = Scatter(p, gb, (brb, bra, brz), sems[12:18])
    gga = Gather(p, lambda j: sum_a.at[j], sems[18:25], False)
    ggb = Gather(p, lambda j: sum_b.at[j], sems[25:32], False)
    ggn = Gather(p, lambda j: gain_all.at[j], sems[32:39], False)
    mine = pl.multiple_of(p.t * 768, 768)
    other = pl.multiple_of((1 - p.t) * 768, 768)
    loads = [pltpu.make_async_copy(s, d, wsem.at[i]) for i, (s, d) in enumerate(zip((hq, hk, hv, ho), (wq, wk, wv, wo)))]
    for load in reversed(loads):
        load.start()

    def swap(j):
        return remote(mix_all.at[j, :, pl.ds(other, 768)], mcame.at[j], mcs.at[j], mcr.at[j], p.core())

    def load_mix(j):
        return pltpu.make_async_copy(mix_all.at[j, :, pl.ds(mine, 768)], mown.at[j], msem.at[j])

    def paired(da, db):
        def pair(z, _):
            j = p.rel(da, db, z)
            load_mix(j).wait()
            swap(j).wait_recv()
            add_into(mown.at[j], mcame.at[j])
            if db:
                mix.to_b(da, z).start()
            return 0

        lax.fori_loop(0, 4, pair, 0)

    greet(p)
    for da, db in ((1, 1), (1, 0), (0, 1), (0, 0)):

        def begin(z, _, da=da, db=db):
            swap(p.rel(da, db, z)).start()
            load_mix(p.rel(db, da, z)).start()
            return 0

        lax.fori_loop(0, 4, begin, 0)

    state = hidden[...]
    factor = factor_of(state)
    scaled = state * factor
    normed_grad = grad2[...]
    gain_sum2 = jnp.sum(normed_grad * scaled, axis=0, keepdims=True)
    weighted = normed_grad * gain2[...]
    grad_hidden = cot[...].astype(f32) + factor * (weighted - scaled * row_mean(weighted * scaled))
    dpart[...] = grad_hidden
    grad_attn = grad_hidden.astype(bf16)
    paired(1, 1)
    loads[3].wait()
    for c in range(0, 1536, 512):
        rows = dot_rows(attended[...], grad_attn[:, c : c + 512]).astype(bf16)
        gb[:, :, c : c + 512] = rows.reshape(16, 48, 512)
    for da in (1, 0):

        def send_b(z, _, da=da):
            sb.to_b(da, z).start()
            return 0

        lax.fori_loop(0, 4, send_b, 0)
    paired(0, 1)
    grad_att = dot_t(grad_attn, wo[...]).astype(bf16)
    paired(1, 0)
    paired(0, 0)

    def mix_far(k, _):
        mix.far(k)
        return 0

    visible = visible_in(lens, 256)
    for g in range(2):
        query = group_rows(qkv[:, :768], g, 3)
        keys, values = qkv[:, 768 + g * DH : 768 + (g + 1) * DH], qkv[:, 1024 + g * DH : 1024 + (g + 1) * DH]
        probs = group_probs(query, keys, visible)
        grad_out = group_rows(grad_att, g, 3)
        grad_probs = dot_t(grad_out, values)
        row_dot = jnp.sum(probs * grad_probs, axis=1, keepdims=True)
        grad_scores = (probs * (grad_probs - row_dot)).astype(bf16)
        grad_query = (dot(grad_scores, keys) * DH ** (-0.5)).astype(bf16)
        for h in range(3):
            dqkv[:, (3 * g + h) * DH : (3 * g + h + 1) * DH] = grad_query[h * 256 : (h + 1) * 256, :]
        dqkv[:, 768 + g * DH : 768 + (g + 1) * DH] = (dot_rows(grad_scores, query) * DH ** (-0.5)).astype(bf16)
        dqkv[:, 1024 + g * DH : 1024 + (g + 1) * DH] = dot_rows(probs.astype(bf16), grad_out).astype(bf16)
        if g == 0:
            lax.fori_loop(0, 2, mix_far, 0)
        else:
            lax.fori_loop(2, 4, mix_far, 0)
    inputs = tokens[...].astype(f32)
    factor_one = factor_of(inputs)
    n1 = (inputs * factor_one * gain1[...]).astype(bf16)
    for c in range(0, 1280, 256):
        rows = dot_rows(n1, dqkv[:, c : c + 256]).astype(bf16)
        ga[:, :, c : c + 256] = rows.reshape(16, 96, 256)
    for da in (1, 0):

        def send_a(z, _, da=da):
            sa.to_b(da, z).start()
            return 0

        lax.fori_loop(0, 4, send_a, 0)
    for load in loads[:3]:
        load.wait()
    mres[...] = jnp.zeros_like(mres)
    back = dot_t(dqkv[:, :768], wq[...]) + dot_t(dqkv[:, 768:1024], wk[...]) + dot_t(dqkv[:, 1024:], wv[...])
    dcame[0] = back
    swap_d = remote(dcame.at[0], dcame.at[1], dsem.at[0], dsem.at[1], p.core())
    swap_d.start()

    def mix_close(i, _):
        mix.close((i + 1) % 4)
        return 0

    def far_b(k, _):
        sb.far(k)
        return 0

    def far_a(k, _):
        sa.far(k)
        return 0

    lax.fori_loop(0, 4, far_b, 0)
    lax.fori_loop(0, 4, mix_close, 0)
    swap_d.wait()
    normed_grad = dcame[0] + dcame[1]
    scaled = inputs * factor_one
    gain_sum1 = jnp.sum(normed_grad * scaled, axis=0, keepdims=True)
    weighted = normed_grad * gain1[...]
    grad_tokens[...] = (dpart[...] + factor_one * (weighted - scaled * row_mean(weighted * scaled))).astype(bf16)
    for i in range(4):
        gain_all[p.dp, i : i + 1, :] = gain_sum1[:, i * 384 : (i + 1) * 384]
        gain_all[p.dp, 4 + i : 5 + i, :] = gain_sum2[:, i * 384 : (i + 1) * 384]
    ggn.start()
    lax.fori_loop(0, 4, far_a, 0)

    def put_mix(at, total):
        mres[at, :] = total

    mix.total(put_mix)
    swap_r = remote(mres, mother, fsem.at[0], fsem.at[1], p.core())
    swap_r.start()

    def close_b(i, _):
        sb.close((i + 1) % 4)
        return 0

    def close_a(i, _):
        sa.close((i + 1) % 4)
        return 0

    lax.fori_loop(0, 4, close_b, 0)
    lax.fori_loop(0, 4, close_a, 0)
    for n in (1, 2, 3):
        ggn.got_z(n)

    def put_b(at, total):
        blk_b[at, :] = total.astype(bf16)

    def put_a(at, total):
        blk_a[at, :] = total.astype(bf16)

    sb.total(put_b)
    own_b = pltpu.make_async_copy(blk_b, sum_b.at[p.dp], lsem.at[0])
    own_b.start()
    own_b.wait()
    ggb.start()
    sa.total(put_a)
    own_a = pltpu.make_async_copy(blk_a, sum_a.at[p.dp], lsem.at[1])
    own_a.start()
    own_a.wait()
    gga.start()
    swap_r.wait()
    low = pl.multiple_of(p.t, 1)
    left = jnp.where(low == 0, mres[...], mother[...])
    right = jnp.where(low == 0, mother[...], mres[...])
    output[:, :768] = (hidden[:, :768] + left).astype(bf16)
    output[:, 768:] = (hidden[:, 768:] + right).astype(bf16)
    for n in range(4):
        ggn.got_a(n)

    for n in (1, 2, 3):
        ggb.got_z(n)
        gga.got_z(n)
    for n in range(4):
        ggb.got_a(n)
        gga.got_a(n)
    for da in (0, 1):

        def lasts(n, _, da=da):
            ggn.got_b(da, n)
            ggb.got_b(da, n)
            gga.got_b(da, n)
            return 0

        lax.fori_loop(0, 4, lasts, 0)
    total = gain_all[0]
    for j in range(1, 16):
        total = total + gain_all[j]
    sum_n[...] = total

    def ends(j, _):
        swap(j).wait_send()
        return 0

    lax.fori_loop(0, 16, ends, 0)
    for plan in (mix, sa, sb, gga, ggb, ggn):
        plan.finish()


def back(grad2, hidden, tokens, cot, gain1, gain2, qkv, attended, lens, wq, wk, wv, wo, mix_all):
    sds = jax.ShapeDtypeStruct
    half = (16, 256, 768)
    a, b = (16, 96, 1280), (16, 48, 1536)
    scratch = [pltpu.VMEM(w.shape, bf16) for w in (wq, wk, wv, wo)] + [DMA((4,))]
    scratch += [pltpu.VMEM(half, bf16), pltpu.VMEM(half, bf16)] + scatter_land(256, 768)
    scratch += [pltpu.VMEM((256, 768), f32), pltpu.VMEM((256, 768), f32), pltpu.VMEM(a, bf16), pltpu.VMEM(b, bf16)]
    scratch += scatter_land(*a[1:]) + scatter_land(*b[1:])
    scratch += [
        pltpu.VMEM(a[1:], bf16), pltpu.VMEM(b[1:], bf16), pltpu.VMEM((16, 8, 384), f32), pltpu.VMEM((256, 1280), bf16),
        pltpu.VMEM((256, 1536), f32), pltpu.VMEM((2, 256, 1536), f32),
    ]
    scratch += [DMA((16,)), DMA((16,)), DMA((16,)), DMA((2,)), DMA((2,)), DMA((2,))]
    scratch += scatter_sems() * 3 + gather_sems(False) * 3
    return pl.pallas_call(
        back_kernel,
        out_shape=(sds((256, 1536), bf16), sds((256, 1536), bf16), sds(a, bf16), sds(b, bf16), sds((8, 384), f32)),
        in_specs=[VMEM] * 8 + [pl.BlockSpec(memory_space=pltpu.SMEM)] + [ANY] * 5,
        out_specs=(VMEM, VMEM, ANY, ANY, VMEM),
        scratch_shapes=scratch,
        compiler_params=pltpu.CompilerParams(collective_id=2, has_side_effects=True, vmem_limit_bytes=63 << 20),
    )(grad2, hidden, tokens, cot, gain1, gain2, qkv, attended, lens, wq, wk, wv, wo, mix_all)


def shards_fast(
    tokens, doc_lens, routes, gate_weights, norm_attn, w_query, w_key, w_value, w_out, norm_ffn,
    shared_gate, shared_up, shared_down, expert_gate, expert_up, expert_down, cotangent,
):
    width = tokens.shape[1]
    experts = jnp.arange(lax.axis_size("dp"), dtype=jnp.int32)
    named = (routes[None, :, :] == experts[:, None, None]).astype(f32)
    gates = jnp.sum(gate_weights[None, :, :] * named, axis=2)
    gain1, gain2 = norm_attn[None], norm_ffn[None]
    n2_all, cot_all, qkv, attended, hidden, mix_all, acts, grad2 = front(
        tokens, doc_lens, gates, gain1, gain2, cotangent, w_query, w_key, w_value, w_out,
        expert_gate[0], expert_up[0], expert_down[0], shared_gate, shared_up, shared_down,
    )
    output, grad_tokens, sum_a, sum_b, gains = back(
        grad2, hidden, tokens, cotangent, gain1, gain2, qkv, attended, doc_lens, w_query, w_key, w_value, w_out, mix_all
    )
    n2_all, cot_all, acts = n2_all.reshape(-1, width), cot_all.reshape(-1, width), acts.reshape(-1, acts.shape[2])
    fe, fs = expert_up.shape[2], shared_up.shape[1]
    cuts = [0, fe, 2 * fe, 2 * fe + fs, 2 * fe + 2 * fs]
    gate_e, up_e, gate_s, up_s = [dot_rows(n2_all, acts[:, lo:hi]) for lo, hi in zip(cuts, cuts[1:])]
    down_e = dot_rows(acts[:, cuts[4] : cuts[4] + fe], cot_all)
    down_s = dot_rows(acts[:, cuts[4] + fe :], cot_all)
    sum_a = sum_a.reshape(width, -1).astype(f32)
    at = (w_query.shape[1], w_query.shape[1] + w_key.shape[1])
    gains = gains.reshape(2, -1)
    return (
        output, grad_tokens, gains[0], sum_a[:, : at[0]], sum_a[:, at[0] : at[1]], sum_a[:, at[1] :],
        sum_b.reshape(-1, width).astype(f32), gains[1], gate_s, up_s, down_s, gate_e[None], up_e[None], down_e[None],
    )


def shards(
    tokens,
    doc_lens,
    routes,
    gate_weights,
    norm_attn,
    w_query,
    w_key,
    w_value,
    w_out,
    norm_ffn,
    shared_gate,
    shared_up,
    shared_down,
    expert_gate,
    expert_up,
    expert_down,
    cotangent,
):
    seq_len, width = tokens.shape
    head_dim = DH
    kv_heads = w_key.shape[1] // head_dim
    q_heads = w_query.shape[1] // head_dim
    group_size = q_heads // kv_heads
    score_scale = head_dim ** (-0.5)
    expert_count = lax.axis_size("dp") * expert_gate.shape[0]
    capacity = 3 * seq_len * routes.shape[1] // (2 * expert_count)
    positions = jnp.arange(seq_len, dtype=jnp.int32)
    doc_ends = jnp.cumsum(doc_lens[0])
    doc_index = jnp.sum((positions[:, None] >= doc_ends[None, :]).astype(jnp.int32), axis=1)
    visible = (doc_index[:, None] == doc_index[None, :]) & (
        positions[None, :] <= positions[:, None]
    )
    inputs = tokens.astype(jnp.float32)
    factor_one = rms_factor(inputs)
    scaled_one = inputs * factor_one
    normed_one = (scaled_one * norm_attn).astype(jnp.bfloat16)
    query = (
        jnp.dot(normed_one, w_query, preferred_element_type=jnp.float32)
        .astype(jnp.bfloat16)
        .reshape(seq_len, kv_heads, group_size, head_dim)
    )
    keys = (
        jnp.dot(normed_one, w_key, preferred_element_type=jnp.float32)
        .astype(jnp.bfloat16)
        .reshape(seq_len, kv_heads, head_dim)
    )
    values = (
        jnp.dot(normed_one, w_value, preferred_element_type=jnp.float32)
        .astype(jnp.bfloat16)
        .reshape(seq_len, kv_heads, head_dim)
    )

    def score_block():
        raw = (
            jnp.einsum("ikgd,jkd->kgij", query, keys, preferred_element_type=jnp.float32)
            * score_scale
        )
        return jnp.where(visible, raw, masked_value)

    scores = score_block()
    row_max = jnp.max(scores, axis=-1, keepdims=True)
    log_total = row_max + jnp.log(jnp.sum(jnp.exp(scores - row_max), axis=-1, keepdims=True))
    probs_low = jnp.exp(scores - log_total).astype(jnp.bfloat16)
    attended = (
        jnp.einsum("kgij,jkd->ikgd", probs_low, values, preferred_element_type=jnp.float32)
        .astype(jnp.bfloat16)
        .reshape(seq_len, q_heads * head_dim)
    )
    attn_part = jnp.dot(attended, w_out, preferred_element_type=jnp.float32)
    hidden_state = inputs + lax.psum(attn_part, "tensor")
    factor_two = rms_factor(hidden_state)
    scaled_two = hidden_state * factor_two
    normed_two = (scaled_two * norm_ffn).astype(jnp.bfloat16)
    shared_gated = jnp.dot(normed_two, shared_gate, preferred_element_type=jnp.float32)
    shared_upward = jnp.dot(normed_two, shared_up, preferred_element_type=jnp.float32)
    shared_hidden = (shared_gated * jax.nn.sigmoid(shared_gated) * shared_upward).astype(
        jnp.bfloat16
    )
    shared_part = jnp.dot(shared_hidden, shared_down, preferred_element_type=jnp.float32)
    position = slot_positions(routes, expert_count)
    owners = jnp.repeat(positions, routes.shape[1])
    slot_rows = (
        jnp.full((expert_count, capacity), seq_len, jnp.int32)
        .at[routes.reshape(-1), position.reshape(-1)]
        .set(owners)
    )
    padded = jnp.concatenate([normed_two, jnp.zeros((1, width), jnp.bfloat16)], axis=0)
    dispatched = to_experts(padded[slot_rows])
    local_rows = dispatched.reshape(-1, width)
    expert_gated = jnp.dot(local_rows, expert_gate[0], preferred_element_type=jnp.float32)
    expert_upward = jnp.dot(local_rows, expert_up[0], preferred_element_type=jnp.float32)
    expert_hidden = (expert_gated * jax.nn.sigmoid(expert_gated) * expert_upward).astype(
        jnp.bfloat16
    )
    expert_part = jnp.dot(
        expert_hidden, expert_down[0], preferred_element_type=jnp.float32
    ).reshape(dispatched.shape)
    returned = from_experts(expert_part)
    mixture = jnp.sum(gate_weights[:, :, None] * returned[routes, position], axis=1)
    branches = lax.psum(shared_part.astype(jnp.bfloat16), "tensor").astype(jnp.float32) + mixture
    output = (hidden_state + branches).astype(jnp.bfloat16)
    grad_result = cotangent.astype(jnp.float32)
    grad_shared_down = jnp.einsum(
        "sf,sd->fd", shared_hidden, cotangent, preferred_element_type=jnp.float32
    )
    grad_shared_hidden = jnp.einsum(
        "sd,fd->sf", cotangent, shared_down, preferred_element_type=jnp.float32
    )
    grad_sg, grad_su = swish_grads(shared_gated, shared_upward, grad_shared_hidden)
    grad_shared_gate = jnp.einsum(
        "sd,sf->df", normed_two, grad_sg, preferred_element_type=jnp.float32
    )
    grad_shared_up = jnp.einsum(
        "sd,sf->df", normed_two, grad_su, preferred_element_type=jnp.float32
    )
    shared_back_part = jnp.einsum(
        "sf,df->sd", grad_sg, shared_gate, preferred_element_type=jnp.float32
    ) + jnp.einsum("sf,df->sd", grad_su, shared_up, preferred_element_type=jnp.float32)
    routed_grad = (gate_weights[:, :, None] * grad_result[:, None, :]).astype(jnp.bfloat16)
    back_buffer = (
        jnp.zeros((expert_count, capacity, width), jnp.bfloat16)
        .at[routes, position]
        .set(routed_grad)
    )
    arrived_grad = to_experts(back_buffer).reshape(-1, width)
    grad_expert_down = jnp.einsum(
        "rf,rd->fd", expert_hidden, arrived_grad, preferred_element_type=jnp.float32
    )[None]
    grad_expert_hidden = jnp.einsum(
        "rd,fd->rf", arrived_grad, expert_down[0], preferred_element_type=jnp.float32
    )
    grad_eg, grad_eu = swish_grads(expert_gated, expert_upward, grad_expert_hidden)
    grad_expert_gate = jnp.einsum(
        "rd,rf->df", local_rows, grad_eg, preferred_element_type=jnp.float32
    )[None]
    grad_expert_up = jnp.einsum(
        "rd,rf->df", local_rows, grad_eu, preferred_element_type=jnp.float32
    )[None]
    expert_back_part = (
        jnp.einsum("rf,df->rd", grad_eg, expert_gate[0], preferred_element_type=jnp.float32)
        + jnp.einsum("rf,df->rd", grad_eu, expert_up[0], preferred_element_type=jnp.float32)
    ).reshape(dispatched.shape)
    returned_grad = from_experts(expert_back_part)
    routed_back = jnp.sum(returned_grad[routes, position], axis=1)
    normed_grad = (
        lax.psum(shared_back_part.astype(jnp.bfloat16), "tensor").astype(jnp.float32) + routed_back
    )
    grad_hidden_norm, grad_norm_ffn = norm_backward(normed_grad, norm_ffn, factor_two, scaled_two)
    grad_hidden = grad_result + grad_hidden_norm
    grad_attn = grad_hidden.astype(jnp.bfloat16)
    grad_w_out = jnp.einsum("sa,sd->ad", attended, grad_attn, preferred_element_type=jnp.float32)
    grad_attended = (
        jnp.einsum("sd,ad->sa", grad_attn, w_out, preferred_element_type=jnp.float32)
        .astype(jnp.bfloat16)
        .reshape(seq_len, kv_heads, group_size, head_dim)
    )
    probs_again = jnp.exp(score_block() - log_total)
    grad_probs = jnp.einsum(
        "ikgd,jkd->kgij", grad_attended, values, preferred_element_type=jnp.float32
    )
    row_dot = jnp.sum(probs_again * grad_probs, axis=-1, keepdims=True)
    grad_scores = (probs_again * (grad_probs - row_dot)).astype(jnp.bfloat16)
    grad_query = (
        (
            jnp.einsum("kgij,jkd->ikgd", grad_scores, keys, preferred_element_type=jnp.float32)
            * score_scale
        )
        .astype(jnp.bfloat16)
        .reshape(seq_len, q_heads * head_dim)
    )
    grad_keys = (
        (
            jnp.einsum("kgij,ikgd->jkd", grad_scores, query, preferred_element_type=jnp.float32)
            * score_scale
        )
        .astype(jnp.bfloat16)
        .reshape(seq_len, kv_heads * head_dim)
    )
    grad_values = (
        jnp.einsum(
            "kgij,ikgd->jkd",
            probs_again.astype(jnp.bfloat16),
            grad_attended,
            preferred_element_type=jnp.float32,
        )
        .astype(jnp.bfloat16)
        .reshape(seq_len, kv_heads * head_dim)
    )
    grad_w_query = jnp.einsum(
        "sd,sa->da", normed_one, grad_query, preferred_element_type=jnp.float32
    )
    grad_w_key = jnp.einsum("sd,sa->da", normed_one, grad_keys, preferred_element_type=jnp.float32)
    grad_w_value = jnp.einsum(
        "sd,sa->da", normed_one, grad_values, preferred_element_type=jnp.float32
    )
    attn_back_part = jnp.einsum(
        "sa,da->sd", grad_query, w_query, preferred_element_type=jnp.float32
    )
    attn_back_part = attn_back_part + jnp.einsum(
        "sa,da->sd", grad_keys, w_key, preferred_element_type=jnp.float32
    )
    attn_back_part = attn_back_part + jnp.einsum(
        "sa,da->sd", grad_values, w_value, preferred_element_type=jnp.float32
    )
    normed_grad_one = lax.psum(attn_back_part.astype(jnp.bfloat16), "tensor").astype(jnp.float32)
    grad_input_norm, grad_norm_attn = norm_backward(
        normed_grad_one, norm_attn, factor_one, scaled_one
    )
    grad_tokens = (grad_hidden + grad_input_norm).astype(jnp.bfloat16)
    summed = lax.psum(
        (
            grad_norm_attn,
            grad_w_query,
            grad_w_key,
            grad_w_value,
            grad_w_out,
            grad_norm_ffn,
            grad_shared_gate,
            grad_shared_up,
            grad_shared_down,
        ),
        "dp",
    )
    return (
        output,
        grad_tokens,
        summed[0],
        summed[1],
        summed[2],
        summed[3],
        summed[4],
        summed[5],
        summed[6],
        summed[7],
        summed[8],
        grad_expert_gate,
        grad_expert_up,
        grad_expert_down,
    )


def solution(mesh):
    fast = mesh.shape["dp"] == 16 and mesh.shape["tensor"] == 2
    return jax.shard_map(
        shards_fast if fast else shards,
        mesh=mesh,
        in_specs=(
            P("dp", None),
            P("dp", None),
            P("dp", None),
            P("dp", None),
            P(),
            P(None, "tensor"),
            P(None, "tensor"),
            P(None, "tensor"),
            P("tensor", None),
            P(),
            P(None, "tensor"),
            P(None, "tensor"),
            P("tensor", None),
            P("dp", None, "tensor"),
            P("dp", None, "tensor"),
            P("dp", "tensor", None),
            P("dp", None),
        ),
        out_specs=(
            P("dp", None),
            P("dp", None),
            P(),
            P(None, "tensor"),
            P(None, "tensor"),
            P(None, "tensor"),
            P("tensor", None),
            P(),
            P(None, "tensor"),
            P(None, "tensor"),
            P("tensor", None),
            P("dp", None, "tensor"),
            P("dp", None, "tensor"),
            P("dp", "tensor", None),
        ),
        check_vma=False,
    )
```

```python
import functools
import jax
import jax.numpy as jnp
from jax import lax
from jax.experimental import pallas as pl
from jax.experimental.pallas import tpu as pltpu
from jax.sharding import PartitionSpec as P

DH = 128


epsilon = 1e-05
masked_value = -1e30


def rms_factor(values):
    return lax.rsqrt(jnp.mean(values * values, axis=-1, keepdims=True) + epsilon)


def norm_backward(grad_normed, gain_vector, factor, scaled):
    grad_scaled = grad_normed * gain_vector
    inner_mean = jnp.mean(grad_scaled * scaled, axis=-1, keepdims=True)
    return (factor * (grad_scaled - scaled * inner_mean), jnp.sum(grad_normed * scaled, axis=0))


def swish_grads(gated, upward, grad_hidden):
    sigma = jax.nn.sigmoid(gated)
    grad_gated = grad_hidden * upward * sigma * (1.0 + gated * (1.0 - sigma))
    grad_upward = grad_hidden * gated * sigma
    return (grad_gated.astype(jnp.bfloat16), grad_upward.astype(jnp.bfloat16))


def slot_positions(routes, expert_count):
    flat_routes = routes.reshape(-1)
    onehot = (flat_routes[:, None] == jnp.arange(expert_count, dtype=jnp.int32)[None, :]).astype(
        jnp.int32
    )
    earlier = jnp.cumsum(onehot, axis=0) - onehot
    return jnp.sum(earlier * onehot, axis=1).reshape(routes.shape)


def to_experts(buffer):
    return lax.all_to_all(buffer, "dp", split_axis=0, concat_axis=0, tiled=True)


def from_experts(partial_value):
    own_part = lax.psum_scatter(
        partial_value.astype(jnp.bfloat16), "tensor", scatter_dimension=1, tiled=True
    ).astype(jnp.float32)
    joined = lax.all_gather(own_part.astype(jnp.bfloat16), "tensor", axis=1, tiled=True).astype(
        own_part.dtype
    )
    return lax.all_to_all(
        joined.astype(jnp.bfloat16), "dp", split_axis=0, concat_axis=0, tiled=True
    ).astype(joined.dtype)


MESH = pl.DeviceIdType.MESH
ANY = pl.BlockSpec(memory_space=pl.ANY)
VMEM = pl.BlockSpec(memory_space=pltpu.VMEM)
DMA = pltpu.SemaphoreType.DMA
bf16, f32 = jnp.bfloat16, jnp.float32


def dot(first, second):
    return jnp.dot(first, second, preferred_element_type=f32)


def dot_t(first, second):
    return lax.dot_general(first, second, (((1,), (1,)), ((), ())), preferred_element_type=f32)


def dot_rows(first, second):
    return lax.dot_general(first, second, (((0,), (0,)), ((), ())), preferred_element_type=f32)


class Place:
    def __init__(self):
        self.dp = lax.axis_index("dp")
        self.t = lax.axis_index("tensor")
        self.x, self.y, self.z = self.dp % 2, (self.dp // 2) % 2, self.dp // 4
        digits = [0xE4, 0xE1, 0x1E, 0x1B]
        code = sum(jnp.where(self.z == i, d, 0) for i, d in enumerate(digits))
        self.near = lambda n: (code // (4**n if isinstance(n, int) else jnp.where(n == 0, 1, jnp.where(n == 1, 4, jnp.where(n == 2, 16, 64))))) % 4

    def flip(self, dx, dy, z):
        return z * 4 + (self.y + dy) % 2 * 2 + (self.x + dx) % 2

    def rel(self, da, db, z):
        t = self.t
        return self.flip((1 - t) * da + t * db, t * da + (1 - t) * db, z)

    def core(self):
        return (self.dp, 1 - self.t)

    def a(self):
        return (self.rel(1, 0, self.z), self.t)

    def b(self):
        return (self.rel(0, 1, self.z), self.t)

    def at_z(self, z):
        return (self.rel(0, 0, z), self.t)


def greet(place):
    barrier = pltpu.get_barrier_semaphore()
    partners = [place.core(), place.a(), place.b()] + [place.at_z((place.z + k) % 4) for k in (1, 2, 3)]
    for partner in partners:
        pl.semaphore_signal(barrier, inc=1, device_id=partner, device_id_type=MESH)
    pl.semaphore_wait(barrier, len(partners))


def remote(src, dst, send, recv, device):
    return pltpu.make_async_remote_copy(
        src_ref=src, dst_ref=dst, send_sem=send, recv_sem=recv, device_id=device, device_id_type=MESH
    )


class Gather:
    def __init__(self, place, part, sems, swap, zfirst):
        self.p, self.part, self.swap, self.zfirst = place, part, swap, zfirst
        self.us, self.ds, self.zr, self.as_, self.ar, self.bs, self.br = sems[:7]
        if swap:
            self.cs, self.cr = sems[7:9]

    def copy(self, j, send, recv, device):
        return remote(self.part(j), self.part(j), send, recv, device)

    def up(self, da, z):
        p = self.p
        return self.copy(p.rel(da, 0, z), self.us.at[da, z], self.zr.at[da, z], p.at_z((p.z + 1) % 4))

    def down(self, da, z):
        p = self.p
        return self.copy(p.rel(da, 0, z), self.ds.at[da, z], self.zr.at[da, z], p.at_z((p.z + 3) % 4))

    def to_a(self, z):
        return self.copy(self.p.rel(0, 0, z), self.as_.at[z], self.ar.at[z], self.p.a())

    def from_a(self, z):
        return self.copy(self.p.rel(1, 0, z), self.as_.at[z], self.ar.at[z], self.p.a())

    def to_b(self, da, z):
        return self.copy(self.p.rel(da, 0, z), self.bs.at[da, z], self.br.at[da, z], self.p.b())

    def from_b(self, da, z):
        return self.copy(self.p.rel(da, 1, z), self.bs.at[da, z], self.br.at[da, z], self.p.b())

    def to_core(self, j):
        return self.copy(j, self.cs.at[j], self.cr.at[j], self.p.core())

    def ups(self, z):
        return jnp.logical_and(z <= self.p.z, self.p.z < 3)

    def downs(self, z):
        return jnp.logical_and(z >= self.p.z, self.p.z > 0)

    def along_z(self, da, z):
        pl.when(self.ups(z))(lambda: self.up(da, z).start())
        pl.when(self.downs(z))(lambda: self.down(da, z).start())

    def other_core(self, da, db, z):
        if self.swap:
            self.to_core(self.p.rel(da, db, z)).start()

    def start(self):
        if not self.zfirst:
            self.to_a(self.p.z).start()
        self.along_z(0, self.p.z)
        if self.zfirst:
            self.to_a(self.p.z).start()
        self.to_b(0, self.p.z).start()

    def got_z(self, n, da=0):
        z = self.p.near(n)
        self.up(da, z).wait_recv()
        self.along_z(da, z)
        if self.zfirst:
            self.to_a(z).start()
        self.to_b(da, z).start()
        self.other_core(da, 0, z)

    def got_a(self, n):
        z = self.p.near(n)
        self.from_a(z).wait_recv()
        if not self.zfirst:
            self.along_z(1, z)
        self.to_b(1, z).start()
        self.other_core(1, 0, z)

    def got_b(self, da, n):
        z = self.p.near(n)
        self.from_b(da, z).wait_recv()
        self.other_core(da, 1, z)

    def wait_core(self, j):
        self.to_core(j).wait_recv()

    def finish(self):
        def ends(z, _):
            for da in (0,) if self.zfirst else (0, 1):
                pl.when(self.ups(z))(lambda: self.up(da, z).wait_send())
                pl.when(self.downs(z))(lambda: self.down(da, z).wait_send())
            if self.zfirst:
                self.to_a(z).wait_send()
            self.to_b(0, z).wait_send()
            self.to_b(1, z).wait_send()
            return 0

        lax.fori_loop(0, 4, ends, 0)
        if not self.zfirst:
            self.to_a(self.p.z).wait_send()
        if self.swap:

            def swaps(i, _):
                self.to_core((self.p.dp + 1 + i) % 16).wait_send()
                return 0

            lax.fori_loop(0, 15, swaps, 0)


def gather_sems(swap):
    kinds = [(2, 4)] * 3 + [(4,)] * 2 + [(2, 4)] * 2 + [(16,)] * (2 * swap)
    return [DMA(kind) for kind in kinds]


def add_into(dst, src):
    dst[...] = dst[...] + src[...]


class Scatter:
    def __init__(self, place, part, land, sems, zlast):
        self.p, self.part, self.zlast = place, part, zlast
        self.rb, self.ra, self.rz = land
        self.bs, self.br, self.as_, self.ar, self.zs, self.zr = sems

    def order(self, m):
        return self.p.near(3 - m)

    def to_b(self, da, z):
        return remote(self.part(self.p.rel(da, 1, z)), self.rb.at[da, z], self.bs.at[da, z], self.br.at[da, z], self.p.b())

    def to_a(self, z):
        slot = z if self.zlast else 0
        return remote(self.part(self.p.rel(1, 0, z)), self.ra.at[slot], self.as_.at[slot], self.ar.at[slot], self.p.a())

    def up(self, da, t):
        p = self.p
        return remote(self.part(p.rel(da, 0, t)), self.rz.at[da, t], self.zs.at[da, t], self.zr.at[da, t], p.at_z((p.z + 1) % 4))

    def down(self, da, t):
        p = self.p
        slot = jnp.where(t == p.z - 1, 4, t)
        return remote(self.part(p.rel(da, 0, t)), self.rz.at[da, slot], self.zs.at[da, t], self.zr.at[da, slot], p.at_z((p.z + 3) % 4))

    def landed(self, da, slot):
        p = self.p
        piece = self.rz.at[da, slot]
        remote(piece, piece, self.zs.at[da, 0], self.zr.at[da, slot], p.at_z((p.z + 1) % 4)).wait_recv()

    def send_b(self):
        def sends(i, _):
            self.to_b(1 - i // 4, self.order(i % 4)).start()
            return 0

        lax.fori_loop(0, 8, sends, 0)

    def got_b(self, da, z):
        self.to_b(da, z).wait_recv()
        add_into(self.part(self.p.rel(da, 0, z)), self.rb.at[da, z])

    def pass_z(self, da, t):
        p = self.p

        @pl.when(jnp.logical_or(jnp.logical_and(t > p.z, p.z > 0), jnp.logical_and(t < p.z, p.z < 3)))
        def _():
            self.landed(da, t)
            add_into(self.part(p.rel(da, 0, t)), self.rz.at[da, t])

        pl.when(t > p.z)(lambda: self.up(da, t).start())
        pl.when(t < p.z)(lambda: self.down(da, t).start())

    def end_z(self, da):
        p = self.p

        @pl.when(p.z > 0)
        def _():
            self.landed(da, p.z)
            add_into(self.part(p.rel(da, 0, p.z)), self.rz.at[da, p.z])

        @pl.when(p.z < 3)
        def _():
            self.landed(da, 4)
            add_into(self.part(p.rel(da, 0, p.z)), self.rz.at[da, 4])

    def far(self, m):
        z = self.order(m)
        self.got_b(1, z)
        if self.zlast:
            self.to_a(z).start()
        else:
            pl.when(m < 3)(lambda: self.pass_z(1, z))

    def turn(self):
        if not self.zlast:
            self.end_z(1)
            self.to_a(self.p.z).start()

    def close(self, m):
        z = self.order(m)
        self.got_b(0, z)
        if self.zlast:
            self.to_a(z).wait_recv()
            add_into(self.part(self.p.rel(0, 0, z)), self.ra.at[z])
        pl.when(m < 3)(lambda: self.pass_z(0, z))

    def total(self):
        self.end_z(0)
        if not self.zlast:
            self.to_a(self.p.z).wait_recv()
            add_into(self.part(self.p.dp), self.ra.at[0])

    def finish(self):
        def ends(z, _):
            for da in (0,) if self.zlast else (0, 1):
                pl.when(z != self.p.z)(lambda: self.up(da, z).wait_send())
            if self.zlast:
                self.to_a(z).wait_send()
            self.to_b(0, z).wait_send()
            self.to_b(1, z).wait_send()
            return 0

        lax.fori_loop(0, 4, ends, 0)
        if not self.zlast:
            self.to_a(self.p.z).wait_send()


def scatter_land(rows, cols, zlast):
    kinds = [(2, 4), (4 if zlast else 1,), (1 if zlast else 2, 5)]
    return [pltpu.VMEM(kind + (rows, cols), bf16) for kind in kinds]


def scatter_sems():
    return [DMA(kind) for kind in [(2, 4), (2, 4), (4,), (4,), (2, 4), (2, 5)]]


class Both:
    def __init__(self, *members):
        self.members = members

    def __getattr__(self, name):
        def call(*args):
            for member in self.members:
                getattr(member, name)(*args)

        return call


def row_mean(values):
    return jnp.sum(values, axis=1, keepdims=True) * (1.0 / values.shape[1])


def factor_of(values):
    return lax.rsqrt(row_mean(values * values) + epsilon)


def visible_in(lens, seq):
    rows = lax.broadcasted_iota(jnp.int32, (seq, seq), 0)
    cols = lax.broadcasted_iota(jnp.int32, (seq, seq), 1)
    first, second = lens[0, 0], lens[0, 0] + lens[0, 1]

    def doc(i):
        return (i >= first).astype(jnp.int32) + (i >= second).astype(jnp.int32)

    return jnp.logical_and(doc(rows) == doc(cols), cols <= rows)


def group_rows(values, g, heads):
    cols = [values[:, (heads * g + h) * DH : (heads * g + h + 1) * DH] for h in range(heads)]
    return jnp.concatenate(cols, axis=0)


def group_probs(query, keys, visible):
    seq = keys.shape[0]
    scores = dot_t(query, keys) * DH ** (-0.5)
    scores = jnp.where(visible[None], scores.reshape(-1, seq, seq), masked_value).reshape(scores.shape)
    top = jnp.max(scores, axis=1, keepdims=True)
    exps = jnp.exp(scores - top)
    return exps / jnp.sum(exps, axis=1, keepdims=True)


def swish_all(gated, upward, grad):
    sigma = jax.nn.sigmoid(gated)
    active = gated * sigma
    grad_gated = grad * upward * (sigma * (1.0 + gated * (1.0 - sigma)))
    return active * upward, grad_gated.astype(bf16), (grad * active).astype(bf16)


def place_of(p, i):
    n = jnp.where(i < 4, i, jnp.where(i < 12, (i - 4) // 2, i - 12))
    dx = jnp.where(i < 4, 0, jnp.where(i < 12, (i + 1) % 2, 1))
    dy = jnp.where(i < 4, 0, jnp.where(i < 12, i % 2, 1))
    return dx, dy, p.near(n)


def front_kernel(
    tokens, lens, gates, gain1, gain2, cot,
    hq, hk, hv, ho, heg, heu, hed, hsg, hsu, hsd,
    n2_out, cot_out, qkv, attended, hidden, mix_all, acts_a, acts_b, grad2,
    wk, wv, weg, weu, wed, wsg, wsu, wsd, wsem,
    n2v, cotv, gall, apart, mstage, astage, dstage, own, came, rb1, ra1, rz1, rb2, ra2, rz2,
    asem, msem, dsem, dcame, credit, lsem, fsem, *sems
):
    p = Place()
    half = pl.ds(pl.multiple_of(p.t * 768, 768), 768)
    cut = 96
    top, low = pl.ds(0, cut), pl.ds(cut, 256 - cut)

    def block(j, first=0, rows=256):
        return own.at[pl.ds(pl.multiple_of(j * 256 + first, 16), rows)]

    n2p = Gather(p, lambda j: n2v.at[j, top, half], sems[:9], True, True)
    n2q = Gather(p, lambda j: n2v.at[j, low, half], sems[9:18], True, False)
    ctp = Gather(p, lambda j: cotv.at[j, top, half], sems[18:27], True, True)
    ctq = Gather(p, lambda j: cotv.at[j, low, half], sems[27:36], True, False)
    gtg = Gather(p, lambda j: gall.at[j], sems[36:43], False, True)
    scp = Scatter(p, lambda j: block(j, 0, cut), (rb1, ra1, rz1), sems[43:49], True)
    scq = Scatter(p, lambda j: block(j, cut, 256 - cut), (rb2, ra2, rz2), sems[49:55], False)
    n2g, ctg, sct = Both(n2p, n2q), Both(ctp, ctq), Both(scp, scq)
    cog = Both(ctp, gtg)
    mine = pl.multiple_of(p.t * 768, 768)
    other = pl.multiple_of((1 - p.t) * 768, 768)

    own_cot = pltpu.make_async_copy(cot, cotv.at[p.dp], lsem.at[0])
    own_cot.start()
    wq, wo = own.at[pl.ds(0, 1536)], [own.at[pl.ds(1536 + 768 * i, 768)] for i in range(2)]
    pairs = [(hq, wq), (hk, wk), (hv, wv)] + [(ho.at[:, pl.ds(768 * i, 768)], wo[i]) for i in range(2)]
    pairs += list(zip((heg, heu, hed, hsg, hsu, hsd), (weg, weu, wed, wsg, wsu, wsd)))
    loads = [pltpu.make_async_copy(s, d, wsem.at[i]) for i, (s, d) in enumerate(pairs)]
    for load in loads[:5]:
        load.start()
    gall[p.dp] = gates[...]
    greet(p)
    own_cot.wait()
    ctg.start()
    gtg.start()
    for load in loads[5:]:
        load.start()

    def arrive(first, second, n):
        first.got_z(n)
        if n == 1:
            second.got_a(0)
        second.got_z(n)
        if n > 1:
            first.got_a(n - 2)
            second.got_z(n - 1, 1)

    inputs = tokens[...].astype(f32)
    n1 = (inputs * factor_of(inputs) * gain1[...]).astype(bf16)
    for load in loads[:5]:
        load.wait()
    qkv[:, :768] = dot(n1, wq[...]).astype(bf16)
    arrive(cog, ctq, 1)
    qkv[:, 768:1024] = dot(n1, wk[...]).astype(bf16)
    qkv[:, 1024:] = dot(n1, wv[...]).astype(bf16)
    visible = visible_in(lens, 256)
    for g in range(2):
        query = group_rows(qkv[:, :768], g, 3)
        probs = group_probs(query, qkv[:, 768 + g * DH : 768 + (g + 1) * DH], visible).astype(bf16)
        out = dot(probs, qkv[:, 1024 + g * DH : 1024 + (g + 1) * DH]).astype(bf16)
        for h in range(3):
            attended[:, (3 * g + h) * DH : (3 * g + h + 1) * DH] = out[h * 256 : (h + 1) * 256, :]
        if g == 0:
            arrive(cog, ctq, 2)
    for i in range(2):
        apart[:, 768 * i : 768 * (i + 1)] = dot(attended[...], wo[i][...])
    swap_a = remote(apart, hidden, asem.at[0], asem.at[1], p.core())
    swap_a.start()
    arrive(cog, ctq, 3)
    swap_a.wait()
    hidden[...] = tokens[...].astype(f32) + (apart[...] + hidden[...])
    state = hidden[...]
    n2v[p.dp] = (state * factor_of(state) * gain2[...]).astype(bf16)
    n2g.start()
    for load in loads[5:]:
        load.wait()

    def outs(i):
        dx, dy, z = place_of(p, i)
        j, slot = p.flip(dx, dy, z), i % 2
        cols = [pl.ds(0, 768), pl.ds(768, 768)]
        copies = [(mstage.at[slot, :, cols[h]], mix_all.at[h, j]) for h in range(2)]
        copies += [(astage.at[slot, :, pl.ds(0, 1536)], acts_a.at[j]), (astage.at[slot, :, pl.ds(1536, 768)], acts_b.at[j])]
        return [pltpu.make_async_copy(src, dst, msem.at[slot, k]) for k, (src, dst) in enumerate(copies)]

    def swap_d(i):
        return remote(dstage.at[i % 2, :, pl.ds(other, 768)], came.at[i % 4], dsem.at[i % 2], dcame.at[i % 4], p.core())

    def paired(i):
        dx, dy, z = place_of(p, i)
        j = p.flip(dx, dy, z)
        swap_d(i).wait_recv()
        add_into(block(j), came.at[i % 4])
        pl.when(i < 12)(lambda: pl.semaphore_signal(credit, inc=1, device_id=p.core(), device_id_type=MESH))
        da = (1 - p.t) * dx + p.t * dy
        db = (1 - p.t) * dy + p.t * dx

        @pl.when(db == 1)
        def _():
            scp.to_b(da, z).start()
            scq.to_b(da, z).start()

    def step(i, _):
        dx, dy, z = place_of(p, i)
        j = p.flip(dx, dy, z)

        def window(first, count, event):
            pl.when(jnp.logical_and(i >= first, i < first + count))(lambda: event(i - first))

        @pl.when(i == 1)
        def _():
            cog.got_a(2)
            ctq.got_z(3, 1)
            n2p.got_z(1)
            n2q.got_a(0)

        @pl.when(i == 2)
        def _():
            cog.got_a(3)

        window(2, 2, lambda n: n2p.got_z(n + 2))
        window(1, 3, lambda n: n2q.got_z(n + 1))
        window(2, 4, n2p.got_a)
        window(2, 3, lambda n: n2q.got_z(n + 1, 1))
        window(0, 4, lambda n: cog.got_b(0, n))
        window(0, 4, lambda n: ctq.got_b(0, n))
        window(3, 4, lambda n: n2g.got_b(0, n))
        window(6, 4, lambda n: cog.got_b(1, n))
        window(6, 4, lambda n: ctq.got_b(1, n))
        window(9, 4, lambda n: n2g.got_b(1, n))
        @pl.when(i > 0)
        def _():
            ctg.wait_core(j)
            n2g.wait_core(j)

        @pl.when(i >= 2)
        def _():
            for copy in outs(i - 2):
                copy.wait()
            swap_d(i - 2).wait_send()

        slot = i % 2
        rows, cots = n2v.at[j], cotv.at[j]
        gate = jnp.transpose(jnp.broadcast_to(gall[j, pl.ds(p.dp, 1), :], (128, 256)))[:, :1]
        gated, upward = dot(rows[...], weg[...]), dot(rows[...], weu[...])
        hid, dg, du = swish_all(gated, upward, dot_t(cots[...], wed[...]) * gate)
        hid = (gate * hid).astype(bf16)
        astage[slot, :, 0:256] = dg
        astage[slot, :, 256:512] = du
        astage[slot, :, 1536:1792] = hid
        mstage[slot] = dot(hid, wed[...]).astype(bf16)
        dstage[slot] = (dot_t(dg, weg[...]) + dot_t(du, weu[...])).astype(bf16)
        gated, upward = dot(rows[...], wsg[...]), dot(rows[...], wsu[...])
        hid, dg, du = swish_all(gated, upward, dot_t(cots[...], wsd[...]))
        astage[slot, :, 512:1024] = dg
        astage[slot, :, 1024:1536] = du
        astage[slot, :, 1792:] = hid.astype(bf16)

        @pl.when(i == 0)
        def _():
            mstage[slot] = (mstage[slot].astype(f32) + dot(astage[slot, :, 1792:], wsd[...])).astype(bf16)
            back = dot_t(astage[slot, :, 512:1024], wsg[...]) + dot_t(astage[slot, :, 1024:1536], wsu[...])
            dstage[slot] = (dstage[slot].astype(f32) + back).astype(bf16)

        for copy in outs(i):
            copy.start()
        pl.when(i >= 4)(lambda: pl.semaphore_wait(credit, 1))
        swap_d(i).start()
        block(j)[...] = dstage[slot, :, pl.ds(mine, 768)]
        pl.when(i > 0)(lambda: paired(i - 1))
        return 0

    lax.fori_loop(0, 16, step, 0)
    paired(15)
    ends = [pltpu.make_async_copy(n2v.at[:, :, pl.ds(768 * h, 768)], n2_out.at[h], lsem.at[h]) for h in range(2)]
    ends.append(pltpu.make_async_copy(cotv, cot_out, lsem.at[2]))
    for copy in ends:
        copy.start()

    def far(m, _):
        sct.far(m)
        return 0

    def close(m, _):
        sct.close(m)
        return 0

    lax.fori_loop(0, 4, far, 0)
    scq.turn()
    lax.fori_loop(0, 4, close, 0)
    sct.total()
    res = apart.at[:, pl.ds(0, 768)]
    res[...] = block(p.dp)[...].astype(f32)
    swap_r = remote(res, grad2.at[:, pl.ds(mine, 768)], fsem.at[0], fsem.at[1], p.core())
    keep_r = pltpu.make_async_copy(res, grad2.at[:, pl.ds(mine, 768)], fsem.at[2])
    swap_r.start()
    keep_r.start()
    for i in (14, 15):
        for copy in outs(i):
            copy.wait()
        swap_d(i).wait_send()
    n2g.finish()
    ctg.finish()
    gtg.finish()
    sct.finish()
    for copy in ends:
        copy.wait()
    keep_r.wait()
    swap_r.wait()


def front(tokens, lens, gates, gain1, gain2, cot, *weights):
    big = (16, 256, 1536)
    sds = jax.ShapeDtypeStruct
    scratch = [pltpu.VMEM(w.shape, bf16) for w in weights[1:3] + weights[4:]] + [DMA((11,))]
    scratch += [
        pltpu.VMEM(big, bf16), pltpu.VMEM(big, bf16), pltpu.VMEM((16, 16, 256), f32), pltpu.VMEM((256, 1536), f32),
        pltpu.VMEM((2, 256, 1536), bf16), pltpu.VMEM((2, 256, 2304), bf16),
        pltpu.VMEM((2, 256, 1536), bf16), pltpu.VMEM((4096, 768), bf16), pltpu.VMEM((4, 256, 768), bf16),
    ]
    scratch += scatter_land(96, 768, True) + scatter_land(160, 768, False)
    scratch += [DMA((2,)), DMA((2, 4)), DMA((2,)), DMA((4,)), pltpu.SemaphoreType.REGULAR, DMA((3,)), DMA((3,))]
    scratch += gather_sems(True) * 4 + gather_sems(False) + scatter_sems() * 2
    return pl.pallas_call(
        front_kernel,
        out_shape=(
            sds((2, 16, 256, 768), bf16), sds(big, bf16), sds((256, 1280), bf16), sds((256, 768), bf16),
            sds((256, 1536), f32), sds((2, 16, 256, 768), bf16), sds(big, bf16), sds((16, 256, 768), bf16),
            sds((256, 1536), f32),
        ),
        in_specs=[VMEM, pl.BlockSpec(memory_space=pltpu.SMEM), VMEM, VMEM, VMEM, ANY] + [ANY] * 10,
        out_specs=(ANY, ANY, VMEM, VMEM, VMEM, ANY, ANY, ANY, ANY),
        scratch_shapes=scratch,
        compiler_params=pltpu.CompilerParams(collective_id=1, has_side_effects=True, vmem_limit_bytes=63 << 20),
    )(tokens, lens, gates, gain1, gain2, cot, *weights)


def back_kernel(
    grad2, hidden, tokens, cot, gain1, gain2, qkv, attended, lens,
    hq, hk, hv, ho, mix_all, n2_all, cot_all, acts_a, acts_b,
    output, grad_tokens, sum_a, sum_b, sum_n, wide,
    wqkv, wo, wsem, mown, mcame, mb1, ma1, mz1, mb2, ma2, mz2, mres, mother,
    ga, gb, arb, ara, arz, brb, bra, brz, gain_all, dqkv, acc, lhs, rhs,
    msem, mcs, mcr, dsem, fsem, lsem, tsem, osem, *sems
):
    p = Place()
    cut = 96
    mxp = Scatter(p, lambda j: mown.at[j, pl.ds(0, cut)], (mb1, ma1, mz1), sems[:6], True)
    mxq = Scatter(p, lambda j: mown.at[j, pl.ds(cut, 256 - cut)], (mb2, ma2, mz2), sems[6:12], False)
    mix = Both(mxp, mxq)
    sa = Scatter(p, lambda j: ga.at[j], (arb, ara, arz), sems[12:18], False)
    sb = Scatter(p, lambda j: gb.at[j], (brb, bra, brz), sems[18:24], True)
    gga = Gather(p, lambda j: wqkv.at[pl.ds(pl.multiple_of(96 * j, 96), 96)], sems[24:31], False, False)
    ggb = Gather(p, lambda j: wo.at[pl.ds(pl.multiple_of(48 * j, 48), 48)], sems[31:38], False, True)
    ggn = Gather(p, lambda j: gain_all.at[j], sems[38:45], False, True)
    dpart, dcame = acc.at[pl.ds(512, 256)], [acc.at[pl.ds(0, 256)], acc.at[pl.ds(256, 256)]]
    pairs = [(hq, wqkv.at[:, pl.ds(0, 768)]), (hk, wqkv.at[:, pl.ds(768, 256)]), (hv, wqkv.at[:, pl.ds(1024, 256)]), (ho, wo)]
    loads = [pltpu.make_async_copy(s, d, wsem.at[i]) for i, (s, d) in enumerate(pairs)]
    for load in reversed(loads):
        load.start()

    def swap(j):
        return remote(mix_all.at[1 - p.t, j], mcame.at[j], mcs.at[j], mcr.at[j], p.core())

    def load_mix(j):
        return pltpu.make_async_copy(mix_all.at[p.t, j], mown.at[j], msem.at[j])

    def paired(da, db):
        def pair(m, _):
            z = mxp.order(m)
            j = p.rel(da, db, z)
            load_mix(j).wait()
            swap(j).wait_recv()
            add_into(mown.at[j], mcame.at[j])
            if db:
                mxp.to_b(da, z).start()
                mxq.to_b(da, z).start()
            return 0

        lax.fori_loop(0, 4, pair, 0)

    greet(p)
    for da, db in ((1, 1), (1, 0), (0, 1), (0, 0)):

        def begin(m, _, da=da, db=db):
            z = mxp.order(m)
            swap(p.rel(da, db, z)).start()
            load_mix(p.rel(db, da, z)).start()
            return 0

        lax.fori_loop(0, 4, begin, 0)

    state = hidden[...]
    factor = factor_of(state)
    scaled = state * factor
    normed_grad = grad2[...]
    gain_sum2 = jnp.sum(normed_grad * scaled, axis=0, keepdims=True)
    weighted = normed_grad * gain2[...]
    grad_hidden = cot[...].astype(f32) + factor * (weighted - scaled * row_mean(weighted * scaled))
    dpart[...] = grad_hidden
    grad_attn = grad_hidden.astype(bf16)
    paired(1, 1)
    loads[3].wait()
    for c in range(0, 1536, 512):
        rows = dot_rows(attended[...], grad_attn[:, c : c + 512]).astype(bf16)
        gb[:, :, c : c + 512] = rows.reshape(16, 48, 512)
    grad_att = dot_t(grad_attn, wo[...]).astype(bf16)
    sb.send_b()
    paired(0, 1)
    paired(1, 0)
    paired(0, 0)

    def mix_far(k, _):
        mix.far(k)
        return 0

    visible = visible_in(lens, 256)
    for g in range(2):
        query = group_rows(qkv[:, :768], g, 3)
        keys, values = qkv[:, 768 + g * DH : 768 + (g + 1) * DH], qkv[:, 1024 + g * DH : 1024 + (g + 1) * DH]
        probs = group_probs(query, keys, visible)
        grad_out = group_rows(grad_att, g, 3)
        grad_probs = dot_t(grad_out, values)
        row_dot = jnp.sum(probs * grad_probs, axis=1, keepdims=True)
        grad_scores = (probs * (grad_probs - row_dot)).astype(bf16)
        grad_query = (dot(grad_scores, keys) * DH ** (-0.5)).astype(bf16)
        for h in range(3):
            dqkv[:, (3 * g + h) * DH : (3 * g + h + 1) * DH] = grad_query[h * 256 : (h + 1) * 256, :]
        dqkv[:, 768 + g * DH : 768 + (g + 1) * DH] = (dot_rows(grad_scores, query) * DH ** (-0.5)).astype(bf16)
        dqkv[:, 1024 + g * DH : 1024 + (g + 1) * DH] = dot_rows(probs.astype(bf16), grad_out).astype(bf16)
        if g == 0:
            lax.fori_loop(0, 2, mix_far, 0)
        else:
            lax.fori_loop(2, 4, mix_far, 0)
            mxq.turn()
    inputs = tokens[...].astype(f32)
    factor_one = factor_of(inputs)
    n1 = (inputs * factor_one * gain1[...]).astype(bf16)
    for c in range(0, 1280, 256):
        rows = dot_rows(n1, dqkv[:, c : c + 256]).astype(bf16)
        ga[:, :, c : c + 256] = rows.reshape(16, 96, 256)
    for load in loads[:3]:
        load.wait()
    dcame[0][...] = dot_t(dqkv[...], wqkv[...])
    sa.send_b()
    swap_d = remote(dcame[0], dcame[1], dsem.at[0], dsem.at[1], p.core())
    swap_d.start()

    def mix_close(m, _):
        mix.close(m)
        return 0

    lax.fori_loop(0, 4, mix_close, 0)
    swap_d.wait()
    normed_grad = dcame[0][...] + dcame[1][...]
    scaled = inputs * factor_one
    gain_sum1 = jnp.sum(normed_grad * scaled, axis=0, keepdims=True)
    weighted = normed_grad * gain1[...]
    grad_tokens[...] = (dpart[...] + factor_one * (weighted - scaled * row_mean(weighted * scaled))).astype(bf16)
    for i in range(4):
        gain_all[p.dp, i : i + 1, :] = gain_sum1[:, i * 384 : (i + 1) * 384]
        gain_all[p.dp, 4 + i : 5 + i, :] = gain_sum2[:, i * 384 : (i + 1) * 384]
    ggn.start()
    mix.total()
    mres[...] = mown[p.dp].astype(f32)
    swap_r = remote(mres, mother, fsem.at[0], fsem.at[1], p.core())
    swap_r.start()

    def operands(u):
        tile, j = u // 16, u % 16
        slot = u % 2
        low = tile < 2
        return low, [
            (n2_all.at[jnp.minimum(tile, 1), j], acts_a.at[j]),
            (acts_b.at[j], cot_all.at[j]),
        ], slot

    def fetch(u):
        low, (first, second), slot = operands(u)

        @pl.when(low)
        def _():
            pltpu.make_async_copy(first[0], lhs.at[slot], tsem.at[0, slot]).start()
            pltpu.make_async_copy(first[1], rhs.at[slot], tsem.at[1, slot]).start()

        @pl.when(jnp.logical_not(low))
        def _():
            pltpu.make_async_copy(second[0], lhs.at[slot], tsem.at[0, slot]).start()
            pltpu.make_async_copy(second[1], rhs.at[slot], tsem.at[1, slot]).start()

    def tile_out(tile):
        return pltpu.make_async_copy(acc, wide.at[tile], osem.at[0])

    def work(u):
        slot = u % 2
        pltpu.make_async_copy(acts_b.at[0], lhs.at[slot], tsem.at[0, slot]).wait()
        pltpu.make_async_copy(acts_a.at[0], rhs.at[slot], tsem.at[1, slot]).wait()
        pl.when(u + 1 < 48)(lambda: fetch(u + 1))
        fresh = u % 16 == 0

        @pl.when(jnp.logical_and(fresh, u > 0))
        def _():
            tile_out(u // 16 - 1).wait()

        @pl.when(fresh)
        def _():
            acc[...] = jnp.zeros_like(acc)

        for c in range(0, 1536, 512):
            cols = slice(c, c + 512)
            acc[:, cols] = acc[:, cols] + dot_rows(lhs[slot], rhs[slot, :, cols])
        pl.when(u % 16 == 15)(lambda: tile_out(u // 16).start())

    fetch(0)

    def step(i, _):
        def window(first, count, event):
            pl.when(jnp.logical_and(i >= first, i < first + count))(lambda: event(i - first))

        def far(m):
            sb.far(m)
            sa.far(m)

        def close(m):
            sb.close(m)
            sa.close(m)

        window(0, 4, far)
        pl.when(i == 4)(sa.turn)
        window(4, 4, close)

        @pl.when(i == 8)
        def _():
            sb.total()
            ggb.part(p.dp)[...] = gb[p.dp]
            ggb.start()
            sa.total()
            gga.part(p.dp)[...] = ga[p.dp]
            gga.start()

        window(5, 3, lambda n: ggn.got_z(n + 1))
        window(8, 4, ggn.got_a)
        window(9, 3, lambda n: ggb.got_z(n + 1))
        pl.when(i == 9)(lambda: gga.got_a(0))
        window(9, 3, lambda n: gga.got_z(n + 1))
        window(10, 4, ggb.got_a)
        window(10, 3, lambda n: gga.got_z(n + 1, 1))
        for da in (0, 1):
            window(14 + 4 * da, 4, lambda n, da=da: ggb.got_b(da, n))
            window(14 + 4 * da, 4, lambda n, da=da: gga.got_b(da, n))
            window(14 + 4 * da, 4, lambda n, da=da: ggn.got_b(da, n))

        def two(h, _):
            work(2 * i + h)
            return 0

        lax.fori_loop(0, 2, two, 0)
        return 0

    lax.fori_loop(0, 24, step, 0)
    copies = [pltpu.make_async_copy(wqkv, sum_a, lsem.at[0]), pltpu.make_async_copy(wo, sum_b, lsem.at[1])]
    for copy in copies:
        copy.start()
    swap_r.wait()
    low = pl.multiple_of(p.t, 1)
    left = jnp.where(low == 0, mres[...], mother[...])
    right = jnp.where(low == 0, mother[...], mres[...])
    output[:, :768] = (hidden[:, :768] + left).astype(bf16)
    output[:, 768:] = (hidden[:, 768:] + right).astype(bf16)
    total = gain_all[0]
    for j in range(1, 16):
        total = total + gain_all[j]
    sum_n[...] = total

    def ends(j, _):
        swap(j).wait_send()
        return 0

    lax.fori_loop(0, 16, ends, 0)
    for plan in (mix, sa, sb, gga, ggb, ggn):
        plan.finish()
    tile_out(2).wait()
    for copy in copies:
        copy.wait()


def back(grad2, hidden, tokens, cot, gain1, gain2, qkv, attended, lens, wq, wk, wv, wo, *saved):
    sds = jax.ShapeDtypeStruct
    half = (16, 256, 768)
    a, b = (16, 96, 1280), (16, 48, 1536)
    scratch = [pltpu.VMEM((1536, 1280), bf16), pltpu.VMEM((768, 1536), bf16), DMA((4,))]
    scratch += [pltpu.VMEM(half, bf16), pltpu.VMEM(half, bf16)] + scatter_land(96, 768, True) + scatter_land(160, 768, False)
    scratch += [pltpu.VMEM((256, 768), f32), pltpu.VMEM((256, 768), f32), pltpu.VMEM(a, bf16), pltpu.VMEM(b, bf16)]
    scratch += scatter_land(*a[1:], False) + scatter_land(*b[1:], True)
    scratch += [
        pltpu.VMEM((16, 8, 384), f32), pltpu.VMEM((256, 1280), bf16),
        pltpu.VMEM((768, 1536), f32), pltpu.VMEM((2, 256, 768), bf16), pltpu.VMEM((2, 256, 1536), bf16),
    ]
    scratch += [DMA((16,)), DMA((16,)), DMA((16,)), DMA((2,)), DMA((2,)), DMA((2,)), DMA((2, 2)), DMA((1,))]
    scratch += scatter_sems() * 4 + gather_sems(False) * 3
    return pl.pallas_call(
        back_kernel,
        out_shape=(sds((256, 1536), bf16), sds((256, 1536), bf16), sds((1536, 1280), bf16), sds((768, 1536), bf16), sds((8, 384), f32), sds((3, 768, 1536), f32)),
        in_specs=[VMEM] * 8 + [pl.BlockSpec(memory_space=pltpu.SMEM)] + [ANY] * 9,
        out_specs=(VMEM, VMEM, ANY, ANY, VMEM, ANY),
        scratch_shapes=scratch,
        compiler_params=pltpu.CompilerParams(collective_id=2, has_side_effects=True, vmem_limit_bytes=63 << 20),
    )(grad2, hidden, tokens, cot, gain1, gain2, qkv, attended, lens, wq, wk, wv, wo, *saved)


def shards_fast(
    tokens, doc_lens, routes, gate_weights, norm_attn, w_query, w_key, w_value, w_out, norm_ffn,
    shared_gate, shared_up, shared_down, expert_gate, expert_up, expert_down, cotangent,
):
    width = tokens.shape[1]
    experts = jnp.arange(lax.axis_size("dp"), dtype=jnp.int32)
    named = (routes[None, :, :] == experts[:, None, None]).astype(f32)
    gates = jnp.sum(gate_weights[None, :, :] * named, axis=2)
    gain1, gain2 = norm_attn[None], norm_ffn[None]
    n2_all, cot_all, qkv, attended, hidden, mix_all, acts_a, acts_b, grad2 = front(
        tokens, doc_lens, gates, gain1, gain2, cotangent, w_query, w_key, w_value, w_out,
        expert_gate[0], expert_up[0], expert_down[0], shared_gate, shared_up, shared_down,
    )
    output, grad_tokens, sum_a, sum_b, gains, wide = back(
        grad2, hidden, tokens, cotangent, gain1, gain2, qkv, attended, doc_lens, w_query, w_key, w_value, w_out, mix_all,
        n2_all, cot_all, acts_a, acts_b,
    )
    fe, fs = expert_up.shape[2], shared_up.shape[1]
    ins = wide[:2].reshape(width, -1)
    cuts = [0, fe, 2 * fe, 2 * fe + fs, 2 * fe + 2 * fs]
    gate_e, up_e, gate_s, up_s = [ins[:, lo:hi] for lo, hi in zip(cuts, cuts[1:])]
    down_e, down_s = wide[2, :fe], wide[2, fe:]
    sum_a = sum_a.astype(f32)
    at = (w_query.shape[1], w_query.shape[1] + w_key.shape[1])
    gains = gains.reshape(2, -1)
    return (
        output, grad_tokens, gains[0], sum_a[:, : at[0]], sum_a[:, at[0] : at[1]], sum_a[:, at[1] :],
        sum_b.astype(f32), gains[1], gate_s, up_s, down_s, gate_e[None], up_e[None], down_e[None],
    )


def shards(
    tokens,
    doc_lens,
    routes,
    gate_weights,
    norm_attn,
    w_query,
    w_key,
    w_value,
    w_out,
    norm_ffn,
    shared_gate,
    shared_up,
    shared_down,
    expert_gate,
    expert_up,
    expert_down,
    cotangent,
):
    seq_len, width = tokens.shape
    head_dim = DH
    kv_heads = w_key.shape[1] // head_dim
    q_heads = w_query.shape[1] // head_dim
    group_size = q_heads // kv_heads
    score_scale = head_dim ** (-0.5)
    expert_count = lax.axis_size("dp") * expert_gate.shape[0]
    capacity = 3 * seq_len * routes.shape[1] // (2 * expert_count)
    positions = jnp.arange(seq_len, dtype=jnp.int32)
    doc_ends = jnp.cumsum(doc_lens[0])
    doc_index = jnp.sum((positions[:, None] >= doc_ends[None, :]).astype(jnp.int32), axis=1)
    visible = (doc_index[:, None] == doc_index[None, :]) & (
        positions[None, :] <= positions[:, None]
    )
    inputs = tokens.astype(jnp.float32)
    factor_one = rms_factor(inputs)
    scaled_one = inputs * factor_one
    normed_one = (scaled_one * norm_attn).astype(jnp.bfloat16)
    query = (
        jnp.dot(normed_one, w_query, preferred_element_type=jnp.float32)
        .astype(jnp.bfloat16)
        .reshape(seq_len, kv_heads, group_size, head_dim)
    )
    keys = (
        jnp.dot(normed_one, w_key, preferred_element_type=jnp.float32)
        .astype(jnp.bfloat16)
        .reshape(seq_len, kv_heads, head_dim)
    )
    values = (
        jnp.dot(normed_one, w_value, preferred_element_type=jnp.float32)
        .astype(jnp.bfloat16)
        .reshape(seq_len, kv_heads, head_dim)
    )

    def score_block():
        raw = (
            jnp.einsum("ikgd,jkd->kgij", query, keys, preferred_element_type=jnp.float32)
            * score_scale
        )
        return jnp.where(visible, raw, masked_value)

    scores = score_block()
    row_max = jnp.max(scores, axis=-1, keepdims=True)
    log_total = row_max + jnp.log(jnp.sum(jnp.exp(scores - row_max), axis=-1, keepdims=True))
    probs_low = jnp.exp(scores - log_total).astype(jnp.bfloat16)
    attended = (
        jnp.einsum("kgij,jkd->ikgd", probs_low, values, preferred_element_type=jnp.float32)
        .astype(jnp.bfloat16)
        .reshape(seq_len, q_heads * head_dim)
    )
    attn_part = jnp.dot(attended, w_out, preferred_element_type=jnp.float32)
    hidden_state = inputs + lax.psum(attn_part, "tensor")
    factor_two = rms_factor(hidden_state)
    scaled_two = hidden_state * factor_two
    normed_two = (scaled_two * norm_ffn).astype(jnp.bfloat16)
    shared_gated = jnp.dot(normed_two, shared_gate, preferred_element_type=jnp.float32)
    shared_upward = jnp.dot(normed_two, shared_up, preferred_element_type=jnp.float32)
    shared_hidden = (shared_gated * jax.nn.sigmoid(shared_gated) * shared_upward).astype(
        jnp.bfloat16
    )
    shared_part = jnp.dot(shared_hidden, shared_down, preferred_element_type=jnp.float32)
    position = slot_positions(routes, expert_count)
    owners = jnp.repeat(positions, routes.shape[1])
    slot_rows = (
        jnp.full((expert_count, capacity), seq_len, jnp.int32)
        .at[routes.reshape(-1), position.reshape(-1)]
        .set(owners)
    )
    padded = jnp.concatenate([normed_two, jnp.zeros((1, width), jnp.bfloat16)], axis=0)
    dispatched = to_experts(padded[slot_rows])
    local_rows = dispatched.reshape(-1, width)
    expert_gated = jnp.dot(local_rows, expert_gate[0], preferred_element_type=jnp.float32)
    expert_upward = jnp.dot(local_rows, expert_up[0], preferred_element_type=jnp.float32)
    expert_hidden = (expert_gated * jax.nn.sigmoid(expert_gated) * expert_upward).astype(
        jnp.bfloat16
    )
    expert_part = jnp.dot(
        expert_hidden, expert_down[0], preferred_element_type=jnp.float32
    ).reshape(dispatched.shape)
    returned = from_experts(expert_part)
    mixture = jnp.sum(gate_weights[:, :, None] * returned[routes, position], axis=1)
    branches = lax.psum(shared_part.astype(jnp.bfloat16), "tensor").astype(jnp.float32) + mixture
    output = (hidden_state + branches).astype(jnp.bfloat16)
    grad_result = cotangent.astype(jnp.float32)
    grad_shared_down = jnp.einsum(
        "sf,sd->fd", shared_hidden, cotangent, preferred_element_type=jnp.float32
    )
    grad_shared_hidden = jnp.einsum(
        "sd,fd->sf", cotangent, shared_down, preferred_element_type=jnp.float32
    )
    grad_sg, grad_su = swish_grads(shared_gated, shared_upward, grad_shared_hidden)
    grad_shared_gate = jnp.einsum(
        "sd,sf->df", normed_two, grad_sg, preferred_element_type=jnp.float32
    )
    grad_shared_up = jnp.einsum(
        "sd,sf->df", normed_two, grad_su, preferred_element_type=jnp.float32
    )
    shared_back_part = jnp.einsum(
        "sf,df->sd", grad_sg, shared_gate, preferred_element_type=jnp.float32
    ) + jnp.einsum("sf,df->sd", grad_su, shared_up, preferred_element_type=jnp.float32)
    routed_grad = (gate_weights[:, :, None] * grad_result[:, None, :]).astype(jnp.bfloat16)
    back_buffer = (
        jnp.zeros((expert_count, capacity, width), jnp.bfloat16)
        .at[routes, position]
        .set(routed_grad)
    )
    arrived_grad = to_experts(back_buffer).reshape(-1, width)
    grad_expert_down = jnp.einsum(
        "rf,rd->fd", expert_hidden, arrived_grad, preferred_element_type=jnp.float32
    )[None]
    grad_expert_hidden = jnp.einsum(
        "rd,fd->rf", arrived_grad, expert_down[0], preferred_element_type=jnp.float32
    )
    grad_eg, grad_eu = swish_grads(expert_gated, expert_upward, grad_expert_hidden)
    grad_expert_gate = jnp.einsum(
        "rd,rf->df", local_rows, grad_eg, preferred_element_type=jnp.float32
    )[None]
    grad_expert_up = jnp.einsum(
        "rd,rf->df", local_rows, grad_eu, preferred_element_type=jnp.float32
    )[None]
    expert_back_part = (
        jnp.einsum("rf,df->rd", grad_eg, expert_gate[0], preferred_element_type=jnp.float32)
        + jnp.einsum("rf,df->rd", grad_eu, expert_up[0], preferred_element_type=jnp.float32)
    ).reshape(dispatched.shape)
    returned_grad = from_experts(expert_back_part)
    routed_back = jnp.sum(returned_grad[routes, position], axis=1)
    normed_grad = (
        lax.psum(shared_back_part.astype(jnp.bfloat16), "tensor").astype(jnp.float32) + routed_back
    )
    grad_hidden_norm, grad_norm_ffn = norm_backward(normed_grad, norm_ffn, factor_two, scaled_two)
    grad_hidden = grad_result + grad_hidden_norm
    grad_attn = grad_hidden.astype(jnp.bfloat16)
    grad_w_out = jnp.einsum("sa,sd->ad", attended, grad_attn, preferred_element_type=jnp.float32)
    grad_attended = (
        jnp.einsum("sd,ad->sa", grad_attn, w_out, preferred_element_type=jnp.float32)
        .astype(jnp.bfloat16)
        .reshape(seq_len, kv_heads, group_size, head_dim)
    )
    probs_again = jnp.exp(score_block() - log_total)
    grad_probs = jnp.einsum(
        "ikgd,jkd->kgij", grad_attended, values, preferred_element_type=jnp.float32
    )
    row_dot = jnp.sum(probs_again * grad_probs, axis=-1, keepdims=True)
    grad_scores = (probs_again * (grad_probs - row_dot)).astype(jnp.bfloat16)
    grad_query = (
        (
            jnp.einsum("kgij,jkd->ikgd", grad_scores, keys, preferred_element_type=jnp.float32)
            * score_scale
        )
        .astype(jnp.bfloat16)
        .reshape(seq_len, q_heads * head_dim)
    )
    grad_keys = (
        (
            jnp.einsum("kgij,ikgd->jkd", grad_scores, query, preferred_element_type=jnp.float32)
            * score_scale
        )
        .astype(jnp.bfloat16)
        .reshape(seq_len, kv_heads * head_dim)
    )
    grad_values = (
        jnp.einsum(
            "kgij,ikgd->jkd",
            probs_again.astype(jnp.bfloat16),
            grad_attended,
            preferred_element_type=jnp.float32,
        )
        .astype(jnp.bfloat16)
        .reshape(seq_len, kv_heads * head_dim)
    )
    grad_w_query = jnp.einsum(
        "sd,sa->da", normed_one, grad_query, preferred_element_type=jnp.float32
    )
    grad_w_key = jnp.einsum("sd,sa->da", normed_one, grad_keys, preferred_element_type=jnp.float32)
    grad_w_value = jnp.einsum(
        "sd,sa->da", normed_one, grad_values, preferred_element_type=jnp.float32
    )
    attn_back_part = jnp.einsum(
        "sa,da->sd", grad_query, w_query, preferred_element_type=jnp.float32
    )
    attn_back_part = attn_back_part + jnp.einsum(
        "sa,da->sd", grad_keys, w_key, preferred_element_type=jnp.float32
    )
    attn_back_part = attn_back_part + jnp.einsum(
        "sa,da->sd", grad_values, w_value, preferred_element_type=jnp.float32
    )
    normed_grad_one = lax.psum(attn_back_part.astype(jnp.bfloat16), "tensor").astype(jnp.float32)
    grad_input_norm, grad_norm_attn = norm_backward(
        normed_grad_one, norm_attn, factor_one, scaled_one
    )
    grad_tokens = (grad_hidden + grad_input_norm).astype(jnp.bfloat16)
    summed = lax.psum(
        (
            grad_norm_attn,
            grad_w_query,
            grad_w_key,
            grad_w_value,
            grad_w_out,
            grad_norm_ffn,
            grad_shared_gate,
            grad_shared_up,
            grad_shared_down,
        ),
        "dp",
    )
    return (
        output,
        grad_tokens,
        summed[0],
        summed[1],
        summed[2],
        summed[3],
        summed[4],
        summed[5],
        summed[6],
        summed[7],
        summed[8],
        grad_expert_gate,
        grad_expert_up,
        grad_expert_down,
    )


def solution(mesh):
    fast = mesh.shape["dp"] == 16 and mesh.shape["tensor"] == 2
    return jax.shard_map(
        shards_fast if fast else shards,
        mesh=mesh,
        in_specs=(
            P("dp", None),
            P("dp", None),
            P("dp", None),
            P("dp", None),
            P(),
            P(None, "tensor"),
            P(None, "tensor"),
            P(None, "tensor"),
            P("tensor", None),
            P(),
            P(None, "tensor"),
            P(None, "tensor"),
            P("tensor", None),
            P("dp", None, "tensor"),
            P("dp", None, "tensor"),
            P("dp", "tensor", None),
            P("dp", None),
        ),
        out_specs=(
            P("dp", None),
            P("dp", None),
            P(),
            P(None, "tensor"),
            P(None, "tensor"),
            P(None, "tensor"),
            P("tensor", None),
            P(),
            P(None, "tensor"),
            P(None, "tensor"),
            P("tensor", None),
            P("dp", None, "tensor"),
            P("dp", None, "tensor"),
            P("dp", "tensor", None),
        ),
        check_vma=False,
    )
```

```python
import functools
import jax
import jax.numpy as jnp
from jax import lax
from jax.experimental import pallas as pl
from jax.experimental.pallas import tpu as pltpu
from jax.sharding import PartitionSpec as P

DH = 128


epsilon = 1e-05
masked_value = -1e30


def rms_factor(values):
    return lax.rsqrt(jnp.mean(values * values, axis=-1, keepdims=True) + epsilon)


def norm_backward(grad_normed, gain_vector, factor, scaled):
    grad_scaled = grad_normed * gain_vector
    inner_mean = jnp.mean(grad_scaled * scaled, axis=-1, keepdims=True)
    return (factor * (grad_scaled - scaled * inner_mean), jnp.sum(grad_normed * scaled, axis=0))


def swish_grads(gated, upward, grad_hidden):
    sigma = jax.nn.sigmoid(gated)
    grad_gated = grad_hidden * upward * sigma * (1.0 + gated * (1.0 - sigma))
    grad_upward = grad_hidden * gated * sigma
    return (grad_gated.astype(jnp.bfloat16), grad_upward.astype(jnp.bfloat16))


def slot_positions(routes, expert_count):
    flat_routes = routes.reshape(-1)
    onehot = (flat_routes[:, None] == jnp.arange(expert_count, dtype=jnp.int32)[None, :]).astype(
        jnp.int32
    )
    earlier = jnp.cumsum(onehot, axis=0) - onehot
    return jnp.sum(earlier * onehot, axis=1).reshape(routes.shape)


def to_experts(buffer):
    return lax.all_to_all(buffer, "dp", split_axis=0, concat_axis=0, tiled=True)


def from_experts(partial_value):
    own_part = lax.psum_scatter(
        partial_value.astype(jnp.bfloat16), "tensor", scatter_dimension=1, tiled=True
    ).astype(jnp.float32)
    joined = lax.all_gather(own_part.astype(jnp.bfloat16), "tensor", axis=1, tiled=True).astype(
        own_part.dtype
    )
    return lax.all_to_all(
        joined.astype(jnp.bfloat16), "dp", split_axis=0, concat_axis=0, tiled=True
    ).astype(joined.dtype)


MESH = pl.DeviceIdType.MESH
ANY = pl.BlockSpec(memory_space=pl.ANY)
VMEM = pl.BlockSpec(memory_space=pltpu.VMEM)
DMA = pltpu.SemaphoreType.DMA
bf16, f32 = jnp.bfloat16, jnp.float32


def dot(first, second):
    return jnp.dot(first, second, preferred_element_type=f32)


def dot_t(first, second):
    return lax.dot_general(first, second, (((1,), (1,)), ((), ())), preferred_element_type=f32)


def dot_rows(first, second):
    return lax.dot_general(first, second, (((0,), (0,)), ((), ())), preferred_element_type=f32)


class Place:
    def __init__(self):
        self.dp = lax.axis_index("dp")
        self.t = lax.axis_index("tensor")
        self.x, self.y, self.z = self.dp % 2, (self.dp // 2) % 2, self.dp // 4
        digits = [0xE4, 0xE1, 0x1E, 0x1B]
        code = sum(jnp.where(self.z == i, d, 0) for i, d in enumerate(digits))
        self.near = lambda n: (code // (4**n if isinstance(n, int) else jnp.where(n == 0, 1, jnp.where(n == 1, 4, jnp.where(n == 2, 16, 64))))) % 4

    def flip(self, dx, dy, z):
        return z * 4 + (self.y + dy) % 2 * 2 + (self.x + dx) % 2

    def rel(self, da, db, z):
        t = self.t
        return self.flip((1 - t) * da + t * db, t * da + (1 - t) * db, z)

    def core(self):
        return (self.dp, 1 - self.t)

    def a(self):
        return (self.rel(1, 0, self.z), self.t)

    def b(self):
        return (self.rel(0, 1, self.z), self.t)

    def at_z(self, z):
        return (self.rel(0, 0, z), self.t)


def greet(place):
    barrier = pltpu.get_barrier_semaphore()
    partners = [place.core(), place.a(), place.b()] + [place.at_z((place.z + k) % 4) for k in (1, 2, 3)]
    for partner in partners:
        pl.semaphore_signal(barrier, inc=1, device_id=partner, device_id_type=MESH)
    pl.semaphore_wait(barrier, len(partners))


def remote(src, dst, send, recv, device):
    return pltpu.make_async_remote_copy(
        src_ref=src, dst_ref=dst, send_sem=send, recv_sem=recv, device_id=device, device_id_type=MESH
    )


class Gather:
    def __init__(self, place, part, sems, swap, zfirst):
        self.p, self.part, self.swap, self.zfirst = place, part, swap, zfirst
        self.us, self.ds, self.zr, self.as_, self.ar, self.bs, self.br = sems[:7]
        if swap:
            self.cs, self.cr = sems[7:9]

    def copy(self, j, send, recv, device):
        return remote(self.part(j), self.part(j), send, recv, device)

    def up(self, da, z):
        p = self.p
        return self.copy(p.rel(da, 0, z), self.us.at[da, z], self.zr.at[da, z], p.at_z((p.z + 1) % 4))

    def down(self, da, z):
        p = self.p
        return self.copy(p.rel(da, 0, z), self.ds.at[da, z], self.zr.at[da, z], p.at_z((p.z + 3) % 4))

    def to_a(self, z):
        return self.copy(self.p.rel(0, 0, z), self.as_.at[z], self.ar.at[z], self.p.a())

    def from_a(self, z):
        return self.copy(self.p.rel(1, 0, z), self.as_.at[z], self.ar.at[z], self.p.a())

    def to_b(self, da, z):
        return self.copy(self.p.rel(da, 0, z), self.bs.at[da, z], self.br.at[da, z], self.p.b())

    def from_b(self, da, z):
        return self.copy(self.p.rel(da, 1, z), self.bs.at[da, z], self.br.at[da, z], self.p.b())

    def to_core(self, j):
        return self.copy(j, self.cs.at[j], self.cr.at[j], self.p.core())

    def ups(self, z):
        return jnp.logical_and(z <= self.p.z, self.p.z < 3)

    def downs(self, z):
        return jnp.logical_and(z >= self.p.z, self.p.z > 0)

    def along_z(self, da, z):
        pl.when(self.ups(z))(lambda: self.up(da, z).start())
        pl.when(self.downs(z))(lambda: self.down(da, z).start())

    def other_core(self, da, db, z):
        if self.swap:
            self.to_core(self.p.rel(da, db, z)).start()

    def start(self):
        if not self.zfirst:
            self.to_a(self.p.z).start()
        self.along_z(0, self.p.z)
        if self.zfirst:
            self.to_a(self.p.z).start()
        self.to_b(0, self.p.z).start()

    def got_z(self, n, da=0):
        z = self.p.near(n)
        self.up(da, z).wait_recv()
        self.along_z(da, z)
        if self.zfirst:
            self.to_a(z).start()
        self.to_b(da, z).start()
        self.other_core(da, 0, z)

    def got_a(self, n):
        z = self.p.near(n)
        self.from_a(z).wait_recv()
        if not self.zfirst:
            self.along_z(1, z)
        self.to_b(1, z).start()
        self.other_core(1, 0, z)

    def got_b(self, da, n):
        z = self.p.near(n)
        self.from_b(da, z).wait_recv()
        self.other_core(da, 1, z)

    def wait_core(self, j):
        self.to_core(j).wait_recv()

    def finish(self):
        def ends(z, _):
            for da in (0,) if self.zfirst else (0, 1):
                pl.when(self.ups(z))(lambda: self.up(da, z).wait_send())
                pl.when(self.downs(z))(lambda: self.down(da, z).wait_send())
            if self.zfirst:
                self.to_a(z).wait_send()
            self.to_b(0, z).wait_send()
            self.to_b(1, z).wait_send()
            return 0

        lax.fori_loop(0, 4, ends, 0)
        if not self.zfirst:
            self.to_a(self.p.z).wait_send()
        if self.swap:

            def swaps(i, _):
                self.to_core((self.p.dp + 1 + i) % 16).wait_send()
                return 0

            lax.fori_loop(0, 15, swaps, 0)


def gather_sems(swap):
    kinds = [(2, 4)] * 3 + [(4,)] * 2 + [(2, 4)] * 2 + [(16,)] * (2 * swap)
    return [DMA(kind) for kind in kinds]


def add_into(dst, src):
    dst[...] = dst[...] + src[...]


class Scatter:
    def __init__(self, place, part, land, sems, zlast):
        self.p, self.part, self.zlast = place, part, zlast
        self.rb, self.ra, self.rz = land
        self.bs, self.br, self.as_, self.ar, self.zs, self.zr = sems

    def order(self, m):
        return self.p.near(3 - m)

    def to_b(self, da, z):
        return remote(self.part(self.p.rel(da, 1, z)), self.rb.at[da, z], self.bs.at[da, z], self.br.at[da, z], self.p.b())

    def to_a(self, z):
        slot = z if self.zlast else 0
        return remote(self.part(self.p.rel(1, 0, z)), self.ra.at[slot], self.as_.at[slot], self.ar.at[slot], self.p.a())

    def up(self, da, t):
        p = self.p
        return remote(self.part(p.rel(da, 0, t)), self.rz.at[da, t], self.zs.at[da, t], self.zr.at[da, t], p.at_z((p.z + 1) % 4))

    def down(self, da, t):
        p = self.p
        slot = jnp.where(t == p.z - 1, 4, t)
        return remote(self.part(p.rel(da, 0, t)), self.rz.at[da, slot], self.zs.at[da, t], self.zr.at[da, slot], p.at_z((p.z + 3) % 4))

    def landed(self, da, slot):
        p = self.p
        piece = self.rz.at[da, slot]
        remote(piece, piece, self.zs.at[da, 0], self.zr.at[da, slot], p.at_z((p.z + 1) % 4)).wait_recv()

    def send_b(self):
        def sends(i, _):
            self.to_b(1 - i // 4, self.order(i % 4)).start()
            return 0

        lax.fori_loop(0, 8, sends, 0)

    def got_b(self, da, z):
        self.to_b(da, z).wait_recv()
        add_into(self.part(self.p.rel(da, 0, z)), self.rb.at[da, z])

    def pass_z(self, da, t):
        p = self.p

        @pl.when(jnp.logical_or(jnp.logical_and(t > p.z, p.z > 0), jnp.logical_and(t < p.z, p.z < 3)))
        def _():
            self.landed(da, t)
            add_into(self.part(p.rel(da, 0, t)), self.rz.at[da, t])

        pl.when(t > p.z)(lambda: self.up(da, t).start())
        pl.when(t < p.z)(lambda: self.down(da, t).start())

    def end_z(self, da):
        p = self.p

        @pl.when(p.z > 0)
        def _():
            self.landed(da, p.z)
            add_into(self.part(p.rel(da, 0, p.z)), self.rz.at[da, p.z])

        @pl.when(p.z < 3)
        def _():
            self.landed(da, 4)
            add_into(self.part(p.rel(da, 0, p.z)), self.rz.at[da, 4])

    def far(self, m):
        z = self.order(m)
        self.got_b(1, z)
        if self.zlast:
            self.to_a(z).start()
        else:
            pl.when(m < 3)(lambda: self.pass_z(1, z))

    def turn(self):
        if not self.zlast:
            self.end_z(1)
            self.to_a(self.p.z).start()

    def close(self, m):
        z = self.order(m)
        self.got_b(0, z)
        if self.zlast:
            self.to_a(z).wait_recv()
            add_into(self.part(self.p.rel(0, 0, z)), self.ra.at[z])
        pl.when(m < 3)(lambda: self.pass_z(0, z))

    def total(self):
        self.end_z(0)
        if not self.zlast:
            self.to_a(self.p.z).wait_recv()
            add_into(self.part(self.p.dp), self.ra.at[0])

    def finish(self):
        def ends(z, _):
            for da in (0,) if self.zlast else (0, 1):
                pl.when(z != self.p.z)(lambda: self.up(da, z).wait_send())
            if self.zlast:
                self.to_a(z).wait_send()
            self.to_b(0, z).wait_send()
            self.to_b(1, z).wait_send()
            return 0

        lax.fori_loop(0, 4, ends, 0)
        if not self.zlast:
            self.to_a(self.p.z).wait_send()


def scatter_land(rows, cols, zlast):
    kinds = [(2, 4), (4 if zlast else 1,), (1 if zlast else 2, 5)]
    return [pltpu.VMEM(kind + (rows, cols), bf16) for kind in kinds]


def scatter_sems():
    return [DMA(kind) for kind in [(2, 4), (2, 4), (4,), (4,), (2, 4), (2, 5)]]


class Both:
    def __init__(self, *members):
        self.members = members

    def __getattr__(self, name):
        def call(*args):
            for member in self.members:
                getattr(member, name)(*args)

        return call


def row_mean(values):
    return jnp.sum(values, axis=1, keepdims=True) * (1.0 / values.shape[1])


def factor_of(values):
    return lax.rsqrt(row_mean(values * values) + epsilon)


def visible_in(lens, seq):
    rows = lax.broadcasted_iota(jnp.int32, (seq, seq), 0)
    cols = lax.broadcasted_iota(jnp.int32, (seq, seq), 1)
    first, second = lens[0, 0], lens[0, 0] + lens[0, 1]

    def doc(i):
        return (i >= first).astype(jnp.int32) + (i >= second).astype(jnp.int32)

    return jnp.logical_and(doc(rows) == doc(cols), cols <= rows)


def group_rows(values, g, heads):
    cols = [values[:, (heads * g + h) * DH : (heads * g + h + 1) * DH] for h in range(heads)]
    return jnp.concatenate(cols, axis=0)


def group_probs(query, keys, visible):
    seq = keys.shape[0]
    scores = dot_t(query, keys) * DH ** (-0.5)
    scores = jnp.where(visible[None], scores.reshape(-1, seq, seq), masked_value).reshape(scores.shape)
    top = jnp.max(scores, axis=1, keepdims=True)
    exps = jnp.exp(scores - top)
    return exps / jnp.sum(exps, axis=1, keepdims=True)


def swish_all(gated, upward, grad):
    sigma = jax.nn.sigmoid(gated)
    active = gated * sigma
    grad_gated = grad * upward * (sigma * (1.0 + gated * (1.0 - sigma)))
    return active * upward, grad_gated.astype(bf16), (grad * active).astype(bf16)


def place_of(p, i):
    n = jnp.where(i < 4, i, jnp.where(i < 12, (i - 4) // 2, i - 12))
    dx = jnp.where(i < 4, 0, jnp.where(i < 12, (i + 1) % 2, 1))
    dy = jnp.where(i < 4, 0, jnp.where(i < 12, i % 2, 1))
    return dx, dy, p.near(n)


def front_kernel(
    tokens, lens, routes, weights, gain1_ref, gain2_ref, cot,
    hq, hk, hv, ho, heg, heu, hed, hsg, hsu, hsd,
    n2_out, cot_out, qkv, attended, hidden, mix_all, acts_a, acts_b, grad2,
    wk, wv, weg, weu, wed, wsg, wsu, wsd, wsem,
    n2v, cotv, gall, apart, mstage, astage, dstage, own, came, rb1, ra1, rz1, rb2, ra2, rz2,
    asem, msem, dsem, dcame, credit, lsem, fsem, *sems
):
    p = Place()
    half = pl.ds(pl.multiple_of(p.t * 768, 768), 768)
    cut = 96
    top, low = pl.ds(0, cut), pl.ds(cut, 256 - cut)

    def block(j, first=0, rows=256):
        return own.at[pl.ds(pl.multiple_of(j * 256 + first, 16), rows)]

    n2p = Gather(p, lambda j: n2v.at[j, top, half], sems[:9], True, True)
    n2q = Gather(p, lambda j: n2v.at[j, low, half], sems[9:18], True, False)
    ctp = Gather(p, lambda j: cotv.at[j, top, half], sems[18:27], True, True)
    ctq = Gather(p, lambda j: cotv.at[j, low, half], sems[27:36], True, False)
    gtg = Gather(p, lambda j: gall.at[j], sems[36:43], False, True)
    scp = Scatter(p, lambda j: block(j, 0, cut), (rb1, ra1, rz1), sems[43:49], True)
    scq = Scatter(p, lambda j: block(j, cut, 256 - cut), (rb2, ra2, rz2), sems[49:55], False)
    n2g, ctg, sct = Both(n2p, n2q), Both(ctp, ctq), Both(scp, scq)
    cog = Both(ctp, gtg)
    mine = pl.multiple_of(p.t * 768, 768)
    other = pl.multiple_of((1 - p.t) * 768, 768)

    own_cot = pltpu.make_async_copy(cot, cotv.at[p.dp], lsem.at[0])
    own_cot.start()
    wq, wo = own.at[pl.ds(0, 1536)], [own.at[pl.ds(1536 + 768 * i, 768)] for i in range(2)]
    pairs = [(hq, wq), (hk, wk), (hv, wv)] + [(ho.at[:, pl.ds(768 * i, 768)], wo[i]) for i in range(2)]
    pairs += list(zip((heg, heu, hed, hsg, hsu, hsd), (weg, weu, wed, wsg, wsu, wsd)))
    loads = [pltpu.make_async_copy(s, d, wsem.at[i]) for i, (s, d) in enumerate(pairs)]
    for load in loads[:5]:
        load.start()
    gain1, gain2 = gain1_ref[...].reshape(1, 1536), gain2_ref[...].reshape(1, 1536)
    experts = lax.broadcasted_iota(jnp.int32, (16, 256), 0)
    gates = jnp.zeros((16, 256), f32)
    for k in range(6):
        gates = gates + jnp.where(routes[k : k + 1, :] == experts, weights[k : k + 1, :], 0.0)
    gall[p.dp] = gates
    greet(p)
    own_cot.wait()
    ctg.start()
    gtg.start()
    for load in loads[5:]:
        load.start()

    def arrive(first, second, n):
        first.got_z(n)
        if n == 1:
            second.got_a(0)
        second.got_z(n)
        if n > 1:
            first.got_a(n - 2)
            second.got_z(n - 1, 1)

    inputs = tokens[...].astype(f32)
    n1 = (inputs * factor_of(inputs) * gain1).astype(bf16)
    for load in loads[:5]:
        load.wait()
    qkv[:, :768] = dot(n1, wq[...]).astype(bf16)
    arrive(cog, ctq, 1)
    qkv[:, 768:1024] = dot(n1, wk[...]).astype(bf16)
    qkv[:, 1024:] = dot(n1, wv[...]).astype(bf16)
    visible = visible_in(lens, 256)
    for g in range(2):
        query = group_rows(qkv[:, :768], g, 3)
        probs = group_probs(query, qkv[:, 768 + g * DH : 768 + (g + 1) * DH], visible).astype(bf16)
        out = dot(probs, qkv[:, 1024 + g * DH : 1024 + (g + 1) * DH]).astype(bf16)
        for h in range(3):
            attended[:, (3 * g + h) * DH : (3 * g + h + 1) * DH] = out[h * 256 : (h + 1) * 256, :]
        if g == 0:
            arrive(cog, ctq, 2)
    for i in range(2):
        apart[:, 768 * i : 768 * (i + 1)] = dot(attended[...], wo[i][...])
    swap_a = remote(apart, hidden, asem.at[0], asem.at[1], p.core())
    swap_a.start()
    arrive(cog, ctq, 3)
    swap_a.wait()
    hidden[...] = tokens[...].astype(f32) + (apart[...] + hidden[...])
    state = hidden[...]
    n2v[p.dp] = (state * factor_of(state) * gain2).astype(bf16)
    n2g.start()
    for load in loads[5:]:
        load.wait()

    def outs(i):
        dx, dy, z = place_of(p, i)
        j, slot = p.flip(dx, dy, z), i % 2
        cols = [pl.ds(0, 768), pl.ds(768, 768)]
        copies = [(mstage.at[slot, :, cols[h]], mix_all.at[h, j]) for h in range(2)]
        copies += [(astage.at[slot, :, pl.ds(0, 1536)], acts_a.at[j]), (astage.at[slot, :, pl.ds(1536, 768)], acts_b.at[j])]
        return [pltpu.make_async_copy(src, dst, msem.at[slot, k]) for k, (src, dst) in enumerate(copies)]

    def swap_d(i):
        return remote(dstage.at[i % 2, :, pl.ds(other, 768)], came.at[i % 4], dsem.at[i % 2], dcame.at[i % 4], p.core())

    def paired(i):
        dx, dy, z = place_of(p, i)
        j = p.flip(dx, dy, z)
        swap_d(i).wait_recv()
        add_into(block(j), came.at[i % 4])
        pl.when(i < 12)(lambda: pl.semaphore_signal(credit, inc=1, device_id=p.core(), device_id_type=MESH))
        da = (1 - p.t) * dx + p.t * dy
        db = (1 - p.t) * dy + p.t * dx

        @pl.when(db == 1)
        def _():
            scp.to_b(da, z).start()
            scq.to_b(da, z).start()

    def step(i, _):
        dx, dy, z = place_of(p, i)
        j = p.flip(dx, dy, z)

        def window(first, count, event):
            pl.when(jnp.logical_and(i >= first, i < first + count))(lambda: event(i - first))

        @pl.when(i == 1)
        def _():
            cog.got_a(2)
            ctq.got_z(3, 1)
            n2p.got_z(1)
            n2q.got_a(0)

        @pl.when(i == 2)
        def _():
            cog.got_a(3)

        window(2, 2, lambda n: n2p.got_z(n + 2))
        window(1, 3, lambda n: n2q.got_z(n + 1))
        window(2, 4, n2p.got_a)
        window(2, 3, lambda n: n2q.got_z(n + 1, 1))
        window(0, 4, lambda n: cog.got_b(0, n))
        window(0, 4, lambda n: ctq.got_b(0, n))
        window(3, 4, lambda n: n2g.got_b(0, n))
        window(6, 4, lambda n: cog.got_b(1, n))
        window(6, 4, lambda n: ctq.got_b(1, n))
        window(9, 4, lambda n: n2g.got_b(1, n))
        @pl.when(i > 0)
        def _():
            ctg.wait_core(j)
            n2g.wait_core(j)

        @pl.when(i >= 2)
        def _():
            for copy in outs(i - 2):
                copy.wait()
            swap_d(i - 2).wait_send()

        slot = i % 2
        rows, cots = n2v.at[j], cotv.at[j]
        gate = jnp.transpose(jnp.broadcast_to(gall[j, pl.ds(p.dp, 1), :], (128, 256)))[:, :1]
        gated, upward = dot(rows[...], weg[...]), dot(rows[...], weu[...])
        hid, dg, du = swish_all(gated, upward, dot_t(cots[...], wed[...]) * gate)
        hid = (gate * hid).astype(bf16)
        astage[slot, :, 0:256] = dg
        astage[slot, :, 256:512] = du
        astage[slot, :, 1536:1792] = hid
        mstage[slot] = dot(hid, wed[...]).astype(bf16)
        dstage[slot] = (dot_t(dg, weg[...]) + dot_t(du, weu[...])).astype(bf16)
        gated, upward = dot(rows[...], wsg[...]), dot(rows[...], wsu[...])
        hid, dg, du = swish_all(gated, upward, dot_t(cots[...], wsd[...]))
        astage[slot, :, 512:1024] = dg
        astage[slot, :, 1024:1536] = du
        astage[slot, :, 1792:] = hid.astype(bf16)

        @pl.when(i == 0)
        def _():
            mstage[slot] = (mstage[slot].astype(f32) + dot(astage[slot, :, 1792:], wsd[...])).astype(bf16)
            back = dot_t(astage[slot, :, 512:1024], wsg[...]) + dot_t(astage[slot, :, 1024:1536], wsu[...])
            dstage[slot] = (dstage[slot].astype(f32) + back).astype(bf16)

        for copy in outs(i):
            copy.start()
        pl.when(i >= 4)(lambda: pl.semaphore_wait(credit, 1))
        swap_d(i).start()
        block(j)[...] = dstage[slot, :, pl.ds(mine, 768)]
        pl.when(i > 0)(lambda: paired(i - 1))
        return 0

    lax.fori_loop(0, 16, step, 0)
    paired(15)
    ends = [pltpu.make_async_copy(n2v.at[:, :, pl.ds(768 * h, 768)], n2_out.at[h], lsem.at[h]) for h in range(2)]
    ends.append(pltpu.make_async_copy(cotv, cot_out, lsem.at[2]))
    for copy in ends:
        copy.start()

    def far(m, _):
        sct.far(m)
        return 0

    def close(m, _):
        sct.close(m)
        return 0

    lax.fori_loop(0, 4, far, 0)
    scq.turn()
    lax.fori_loop(0, 4, close, 0)
    sct.total()
    res = apart.at[:, pl.ds(0, 768)]
    res[...] = block(p.dp)[...].astype(f32)
    swap_r = remote(res, grad2.at[:, pl.ds(mine, 768)], fsem.at[0], fsem.at[1], p.core())
    keep_r = pltpu.make_async_copy(res, grad2.at[:, pl.ds(mine, 768)], fsem.at[2])
    swap_r.start()
    keep_r.start()
    for i in (14, 15):
        for copy in outs(i):
            copy.wait()
        swap_d(i).wait_send()
    n2g.finish()
    ctg.finish()
    gtg.finish()
    sct.finish()
    for copy in ends:
        copy.wait()
    keep_r.wait()
    swap_r.wait()


def front(tokens, lens, routes, gates, gain1, gain2, cot, *weights):
    big = (16, 256, 1536)
    sds = jax.ShapeDtypeStruct
    scratch = [pltpu.VMEM(w.shape, bf16) for w in weights[1:3] + weights[4:]] + [DMA((11,))]
    scratch += [
        pltpu.VMEM(big, bf16), pltpu.VMEM(big, bf16), pltpu.VMEM((16, 16, 256), f32), pltpu.VMEM((256, 1536), f32),
        pltpu.VMEM((2, 256, 1536), bf16), pltpu.VMEM((2, 256, 2304), bf16),
        pltpu.VMEM((2, 256, 1536), bf16), pltpu.VMEM((4096, 768), bf16), pltpu.VMEM((4, 256, 768), bf16),
    ]
    scratch += scatter_land(96, 768, True) + scatter_land(160, 768, False)
    scratch += [DMA((2,)), DMA((2, 4)), DMA((2,)), DMA((4,)), pltpu.SemaphoreType.REGULAR, DMA((3,)), DMA((3,))]
    scratch += gather_sems(True) * 4 + gather_sems(False) + scatter_sems() * 2
    return pl.pallas_call(
        front_kernel,
        out_shape=(
            sds((2, 16, 256, 768), bf16), sds(big, bf16), sds((256, 1280), bf16), sds((256, 768), bf16),
            sds((256, 1536), f32), sds((2, 16, 256, 768), bf16), sds(big, bf16), sds((16, 256, 768), bf16),
            sds((256, 1536), f32),
        ),
        in_specs=[VMEM, pl.BlockSpec(memory_space=pltpu.SMEM), VMEM, VMEM, VMEM, VMEM, ANY] + [ANY] * 10,
        out_specs=(ANY, ANY, VMEM, VMEM, VMEM, ANY, ANY, ANY, ANY),
        scratch_shapes=scratch,
        compiler_params=pltpu.CompilerParams(collective_id=1, has_side_effects=True, vmem_limit_bytes=63 << 20),
    )(tokens, lens, routes, gates, gain1, gain2, cot, *weights)


def back_kernel(
    grad2, hidden, tokens, cot, gain1_ref, gain2_ref, qkv, attended, lens,
    hq, hk, hv, ho, mix_all, n2_all, cot_all, acts_a, acts_b,
    output, grad_tokens, sum_a, sum_b, sum_n, wide,
    wqkv, wo, wsem, mown, mcame, mb1, ma1, mz1, mb2, ma2, mz2, mres, mother,
    ga, gb, arb, ara, arz, brb, bra, brz, gain_all, dqkv, acc, lhs, rhs,
    msem, mcs, mcr, dsem, fsem, lsem, tsem, osem, *sems
):
    p = Place()
    gain1, gain2 = gain1_ref[...].reshape(1, 1536), gain2_ref[...].reshape(1, 1536)
    cut = 96
    mxp = Scatter(p, lambda j: mown.at[j, pl.ds(0, cut)], (mb1, ma1, mz1), sems[:6], True)
    mxq = Scatter(p, lambda j: mown.at[j, pl.ds(cut, 256 - cut)], (mb2, ma2, mz2), sems[6:12], False)
    mix = Both(mxp, mxq)
    sa = Scatter(p, lambda j: ga.at[j], (arb, ara, arz), sems[12:18], False)
    sb = Scatter(p, lambda j: gb.at[j], (brb, bra, brz), sems[18:24], True)
    gga = Gather(p, lambda j: wqkv.at[pl.ds(pl.multiple_of(96 * j, 96), 96)], sems[24:31], False, False)
    ggb = Gather(p, lambda j: wo.at[pl.ds(pl.multiple_of(48 * j, 48), 48)], sems[31:38], False, True)
    ggn = Gather(p, lambda j: gain_all.at[j], sems[38:45], False, True)
    dpart, dcame = acc.at[pl.ds(512, 256)], [acc.at[pl.ds(0, 256)], acc.at[pl.ds(256, 256)]]
    pairs = [(hq, wqkv.at[:, pl.ds(0, 768)]), (hk, wqkv.at[:, pl.ds(768, 256)]), (hv, wqkv.at[:, pl.ds(1024, 256)]), (ho, wo)]
    loads = [pltpu.make_async_copy(s, d, wsem.at[i]) for i, (s, d) in enumerate(pairs)]
    for load in reversed(loads):
        load.start()

    def swap(j):
        return remote(mix_all.at[1 - p.t, j], mcame.at[j], mcs.at[j], mcr.at[j], p.core())

    def load_mix(j):
        return pltpu.make_async_copy(mix_all.at[p.t, j], mown.at[j], msem.at[j])

    def paired(da, db):
        def pair(m, _):
            z = mxp.order(m)
            j = p.rel(da, db, z)
            load_mix(j).wait()
            swap(j).wait_recv()
            add_into(mown.at[j], mcame.at[j])
            if db:
                mxp.to_b(da, z).start()
                mxq.to_b(da, z).start()
            return 0

        lax.fori_loop(0, 4, pair, 0)

    greet(p)
    for da, db in ((1, 1), (1, 0), (0, 1), (0, 0)):

        def begin(m, _, da=da, db=db):
            z = mxp.order(m)
            swap(p.rel(da, db, z)).start()
            load_mix(p.rel(db, da, z)).start()
            return 0

        lax.fori_loop(0, 4, begin, 0)

    state = hidden[...]
    factor = factor_of(state)
    scaled = state * factor
    normed_grad = grad2[...]
    gain_sum2 = jnp.sum(normed_grad * scaled, axis=0, keepdims=True)
    weighted = normed_grad * gain2
    grad_hidden = cot[...].astype(f32) + factor * (weighted - scaled * row_mean(weighted * scaled))
    dpart[...] = grad_hidden
    grad_attn = grad_hidden.astype(bf16)
    paired(1, 1)
    loads[3].wait()
    for c in range(0, 1536, 512):
        rows = dot_rows(attended[...], grad_attn[:, c : c + 512]).astype(bf16)
        gb[:, :, c : c + 512] = rows.reshape(16, 48, 512)
    grad_att = dot_t(grad_attn, wo[...]).astype(bf16)
    sb.send_b()
    paired(0, 1)
    paired(1, 0)
    paired(0, 0)

    def mix_far(k, _):
        mix.far(k)
        return 0

    visible = visible_in(lens, 256)
    for g in range(2):
        query = group_rows(qkv[:, :768], g, 3)
        keys, values = qkv[:, 768 + g * DH : 768 + (g + 1) * DH], qkv[:, 1024 + g * DH : 1024 + (g + 1) * DH]
        probs = group_probs(query, keys, visible)
        grad_out = group_rows(grad_att, g, 3)
        grad_probs = dot_t(grad_out, values)
        row_dot = jnp.sum(probs * grad_probs, axis=1, keepdims=True)
        grad_scores = (probs * (grad_probs - row_dot)).astype(bf16)
        grad_query = (dot(grad_scores, keys) * DH ** (-0.5)).astype(bf16)
        for h in range(3):
            dqkv[:, (3 * g + h) * DH : (3 * g + h + 1) * DH] = grad_query[h * 256 : (h + 1) * 256, :]
        dqkv[:, 768 + g * DH : 768 + (g + 1) * DH] = (dot_rows(grad_scores, query) * DH ** (-0.5)).astype(bf16)
        dqkv[:, 1024 + g * DH : 1024 + (g + 1) * DH] = dot_rows(probs.astype(bf16), grad_out).astype(bf16)
        if g == 0:
            lax.fori_loop(0, 2, mix_far, 0)
        else:
            lax.fori_loop(2, 4, mix_far, 0)
            mxq.turn()
    inputs = tokens[...].astype(f32)
    factor_one = factor_of(inputs)
    n1 = (inputs * factor_one * gain1).astype(bf16)
    for c in range(0, 1280, 256):
        rows = dot_rows(n1, dqkv[:, c : c + 256]).astype(bf16)
        ga[:, :, c : c + 256] = rows.reshape(16, 96, 256)
    for load in loads[:3]:
        load.wait()
    dcame[0][...] = dot_t(dqkv[...], wqkv[...])
    sa.send_b()
    swap_d = remote(dcame[0], dcame[1], dsem.at[0], dsem.at[1], p.core())
    swap_d.start()

    def mix_close(m, _):
        mix.close(m)
        return 0

    lax.fori_loop(0, 4, mix_close, 0)
    swap_d.wait()
    normed_grad = dcame[0][...] + dcame[1][...]
    scaled = inputs * factor_one
    gain_sum1 = jnp.sum(normed_grad * scaled, axis=0, keepdims=True)
    weighted = normed_grad * gain1
    grad_tokens[...] = (dpart[...] + factor_one * (weighted - scaled * row_mean(weighted * scaled))).astype(bf16)
    for i in range(4):
        gain_all[p.dp, i : i + 1, :] = gain_sum1[:, i * 384 : (i + 1) * 384]
        gain_all[p.dp, 4 + i : 5 + i, :] = gain_sum2[:, i * 384 : (i + 1) * 384]
    ggn.start()
    mix.total()
    mres[...] = mown[p.dp].astype(f32)
    swap_r = remote(mres, mother, fsem.at[0], fsem.at[1], p.core())
    swap_r.start()

    def operands(u):
        tile, j = u // 8, u % 8
        slot = u % 2
        low = tile < 2
        return low, [
            (n2_all.at[jnp.minimum(tile, 1), pl.ds(2 * j, 2)], acts_a.at[pl.ds(2 * j, 2)]),
            (acts_b.at[pl.ds(2 * j, 2)], cot_all.at[pl.ds(2 * j, 2)]),
        ], slot

    def fetch(u):
        low, (first, second), slot = operands(u)

        @pl.when(low)
        def _():
            pltpu.make_async_copy(first[0], lhs.at[slot], tsem.at[0, slot]).start()
            pltpu.make_async_copy(first[1], rhs.at[slot], tsem.at[1, slot]).start()

        @pl.when(jnp.logical_not(low))
        def _():
            pltpu.make_async_copy(second[0], lhs.at[slot], tsem.at[0, slot]).start()
            pltpu.make_async_copy(second[1], rhs.at[slot], tsem.at[1, slot]).start()

    def tile_out(tile):
        return pltpu.make_async_copy(acc, wide.at[tile], osem.at[0])

    def work(u):
        slot = u % 2
        pltpu.make_async_copy(acts_b.at[pl.ds(0, 2)], lhs.at[slot], tsem.at[0, slot]).wait()
        pltpu.make_async_copy(acts_a.at[pl.ds(0, 2)], rhs.at[slot], tsem.at[1, slot]).wait()
        pl.when(u + 1 < 24)(lambda: fetch(u + 1))
        fresh = u % 8 == 0

        @pl.when(jnp.logical_and(fresh, u > 0))
        def _():
            tile_out(u // 8 - 1).wait()

        @pl.when(fresh)
        def _():
            acc[...] = jnp.zeros_like(acc)

        for c in range(0, 1536, 512):
            cols = slice(c, c + 512)
            acc[:, cols] = acc[:, cols] + dot_rows(lhs[slot].reshape(512, 768), rhs[slot, :, :, cols].reshape(512, 512))
        pl.when(u % 8 == 7)(lambda: tile_out(u // 8).start())

    fetch(0)

    def step(i, _):
        def window(first, count, event):
            pl.when(jnp.logical_and(i >= first, i < first + count))(lambda: event(i - first))

        def far(m):
            sb.far(m)
            sa.far(m)

        def close(m):
            sb.close(m)
            sa.close(m)

        window(0, 4, far)
        pl.when(i == 4)(sa.turn)
        window(4, 4, close)

        @pl.when(i == 8)
        def _():
            sb.total()
            ggb.part(p.dp)[...] = gb[p.dp]
            ggb.start()
            sa.total()
            gga.part(p.dp)[...] = ga[p.dp]
            gga.start()

        window(5, 3, lambda n: ggn.got_z(n + 1))
        window(8, 4, ggn.got_a)
        window(9, 3, lambda n: ggb.got_z(n + 1))
        pl.when(i == 9)(lambda: gga.got_a(0))
        window(9, 3, lambda n: gga.got_z(n + 1))
        window(10, 4, ggb.got_a)
        window(10, 3, lambda n: gga.got_z(n + 1, 1))
        for da in (0, 1):
            window(14 + 4 * da, 4, lambda n, da=da: ggb.got_b(da, n))
            window(14 + 4 * da, 4, lambda n, da=da: gga.got_b(da, n))
            window(14 + 4 * da, 4, lambda n, da=da: ggn.got_b(da, n))

        def some(u, _):
            work(u)
            return 0

        def done(i):
            return jnp.minimum(jnp.where(i < 8, 2 * i, 16 + 1 * (i - 8)), 24)

        lax.fori_loop(done(i), done(i + 1), some, 0)
        return 0

    lax.fori_loop(0, 24, step, 0)
    copies = [pltpu.make_async_copy(wqkv, sum_a, lsem.at[0]), pltpu.make_async_copy(wo, sum_b, lsem.at[1])]
    for copy in copies:
        copy.start()
    swap_r.wait()
    low = pl.multiple_of(p.t, 1)
    left = jnp.where(low == 0, mres[...], mother[...])
    right = jnp.where(low == 0, mother[...], mres[...])
    output[:, :768] = (hidden[:, :768] + left).astype(bf16)
    output[:, 768:] = (hidden[:, 768:] + right).astype(bf16)
    total = gain_all[0]
    for j in range(1, 16):
        total = total + gain_all[j]
    sum_n[...] = total

    def ends(j, _):
        swap(j).wait_send()
        return 0

    lax.fori_loop(0, 16, ends, 0)
    for plan in (mix, sa, sb, gga, ggb, ggn):
        plan.finish()
    tile_out(2).wait()
    for copy in copies:
        copy.wait()


def back(grad2, hidden, tokens, cot, gain1, gain2, qkv, attended, lens, wq, wk, wv, wo, *saved):
    sds = jax.ShapeDtypeStruct
    half = (16, 256, 768)
    a, b = (16, 96, 1280), (16, 48, 1536)
    scratch = [pltpu.VMEM((1536, 1280), bf16), pltpu.VMEM((768, 1536), bf16), DMA((4,))]
    scratch += [pltpu.VMEM(half, bf16), pltpu.VMEM(half, bf16)] + scatter_land(96, 768, True) + scatter_land(160, 768, False)
    scratch += [pltpu.VMEM((256, 768), f32), pltpu.VMEM((256, 768), f32), pltpu.VMEM(a, bf16), pltpu.VMEM(b, bf16)]
    scratch += scatter_land(*a[1:], False) + scatter_land(*b[1:], True)
    scratch += [
        pltpu.VMEM((16, 8, 384), f32), pltpu.VMEM((256, 1280), bf16),
        pltpu.VMEM((768, 1536), f32), pltpu.VMEM((2, 2, 256, 768), bf16), pltpu.VMEM((2, 2, 256, 1536), bf16),
    ]
    scratch += [DMA((16,)), DMA((16,)), DMA((16,)), DMA((2,)), DMA((2,)), DMA((2,)), DMA((2, 2)), DMA((1,))]
    scratch += scatter_sems() * 4 + gather_sems(False) * 3
    return pl.pallas_call(
        back_kernel,
        out_shape=(sds((256, 1536), bf16), sds((256, 1536), bf16), sds((1536, 1280), bf16), sds((768, 1536), bf16), sds((8, 384), f32), sds((3, 768, 1536), f32)),
        in_specs=[VMEM] * 8 + [pl.BlockSpec(memory_space=pltpu.SMEM)] + [ANY] * 9,
        out_specs=(VMEM, VMEM, ANY, ANY, VMEM, ANY),
        scratch_shapes=scratch,
        compiler_params=pltpu.CompilerParams(collective_id=2, has_side_effects=True, vmem_limit_bytes=63 << 20),
    )(grad2, hidden, tokens, cot, gain1, gain2, qkv, attended, lens, wq, wk, wv, wo, *saved)


def finish_kernel(sum_a, sum_b, ins, downs, out_in, grad_in, gains, wq, wk, wv, wo, ge, ue, gs, us, de, ds, out, grad, g1, g2):
    i = pl.program_id(0)
    rows = sum_a[...].astype(f32)
    wq[...], wk[...], wv[...] = rows[:, :768], rows[:, 768:1024], rows[:, 1024:]
    wo[...] = sum_b[...].astype(f32)
    ge[0], ue[0] = ins[0, :, :256], ins[0, :, 256:512]
    gs[...], us[...] = ins[0, :, 512:1024], ins[0, :, 1024:]

    @pl.when(i < 4)
    def _():
        de[0] = downs[0]

    @pl.when(i >= 4)
    def _():
        ds[...] = downs[0]

    @pl.when(i < 8)
    def _():
        out[...] = out_in[...]
        grad[...] = grad_in[...]

    @pl.when(i == 0)
    def _():
        for ref, first in ((g1, 0), (g2, 4)):
            ref[...] = jnp.concatenate([gains[first + r : first + r + 1, :] for r in range(4)], axis=1).reshape(1536)


def finish(sum_a, sum_b, wide, output, grad_tokens, gains):
    sds, spec = jax.ShapeDtypeStruct, pl.BlockSpec

    def rows(n, cols):
        return spec((n, cols), lambda i: (i, 0))

    def expert(cols):
        return spec((1, 128, cols), lambda i: (0, i, 0))

    early = spec((32, 1536), lambda i: (jnp.minimum(i, 7), 0))
    return pl.pallas_call(
        finish_kernel,
        grid=(12,),
        out_shape=(
            sds((1536, 768), f32), sds((1536, 256), f32), sds((1536, 256), f32), sds((768, 1536), f32),
            sds((1, 1536, 256), f32), sds((1, 1536, 256), f32), sds((1536, 512), f32), sds((1536, 512), f32),
            sds((1, 256, 1536), f32), sds((512, 1536), f32), sds((256, 1536), bf16), sds((256, 1536), bf16),
            sds((1536,), f32), sds((1536,), f32),
        ),
        in_specs=[
            rows(128, 1280), rows(64, 1536), spec((1, 128, 1536), lambda i: (i // 6, i % 6, 0)),
            spec((1, 64, 1536), lambda i: (2, i, 0)), early, early, spec((8, 384), lambda i: (0, 0)),
        ],
        out_specs=(
            rows(128, 768), rows(128, 256), rows(128, 256), rows(64, 1536), expert(256), expert(256), rows(128, 512), rows(128, 512),
            spec((1, 64, 1536), lambda i: (0, jnp.minimum(i, 3), 0)), spec((64, 1536), lambda i: (jnp.maximum(i - 4, 0), 0)),
            early, early, spec((1536,), lambda i: (0,)), spec((1536,), lambda i: (0,)),
        ),
        compiler_params=pltpu.CompilerParams(vmem_limit_bytes=63 << 20),
    )(sum_a, sum_b, wide, wide, output, grad_tokens, gains)


def shards_fast(
    tokens, doc_lens, routes, gate_weights, norm_attn, w_query, w_key, w_value, w_out, norm_ffn,
    shared_gate, shared_up, shared_down, expert_gate, expert_up, expert_down, cotangent,
):
    n2_all, cot_all, qkv, attended, hidden, mix_all, acts_a, acts_b, grad2 = front(
        tokens, doc_lens, routes.T, gate_weights.T, norm_attn, norm_ffn, cotangent, w_query, w_key, w_value, w_out,
        expert_gate[0], expert_up[0], expert_down[0], shared_gate, shared_up, shared_down,
    )
    output, grad_tokens, sum_a, sum_b, gains, wide = back(
        grad2, hidden, tokens, cotangent, norm_attn, norm_ffn, qkv, attended, doc_lens, w_query, w_key, w_value, w_out, mix_all,
        n2_all, cot_all, acts_a, acts_b,
    )
    wq, wk, wv, wo, gate_e, up_e, gate_s, up_s, down_e, down_s, output, grad_tokens, gain1, gain2 = finish(
        sum_a, sum_b, wide, output, grad_tokens, gains
    )
    return output, grad_tokens, gain1, wq, wk, wv, wo, gain2, gate_s, up_s, down_s, gate_e, up_e, down_e


def shards(
    tokens,
    doc_lens,
    routes,
    gate_weights,
    norm_attn,
    w_query,
    w_key,
    w_value,
    w_out,
    norm_ffn,
    shared_gate,
    shared_up,
    shared_down,
    expert_gate,
    expert_up,
    expert_down,
    cotangent,
):
    seq_len, width = tokens.shape
    head_dim = DH
    kv_heads = w_key.shape[1] // head_dim
    q_heads = w_query.shape[1] // head_dim
    group_size = q_heads // kv_heads
    score_scale = head_dim ** (-0.5)
    expert_count = lax.axis_size("dp") * expert_gate.shape[0]
    capacity = 3 * seq_len * routes.shape[1] // (2 * expert_count)
    positions = jnp.arange(seq_len, dtype=jnp.int32)
    doc_ends = jnp.cumsum(doc_lens[0])
    doc_index = jnp.sum((positions[:, None] >= doc_ends[None, :]).astype(jnp.int32), axis=1)
    visible = (doc_index[:, None] == doc_index[None, :]) & (
        positions[None, :] <= positions[:, None]
    )
    inputs = tokens.astype(jnp.float32)
    factor_one = rms_factor(inputs)
    scaled_one = inputs * factor_one
    normed_one = (scaled_one * norm_attn).astype(jnp.bfloat16)
    query = (
        jnp.dot(normed_one, w_query, preferred_element_type=jnp.float32)
        .astype(jnp.bfloat16)
        .reshape(seq_len, kv_heads, group_size, head_dim)
    )
    keys = (
        jnp.dot(normed_one, w_key, preferred_element_type=jnp.float32)
        .astype(jnp.bfloat16)
        .reshape(seq_len, kv_heads, head_dim)
    )
    values = (
        jnp.dot(normed_one, w_value, preferred_element_type=jnp.float32)
        .astype(jnp.bfloat16)
        .reshape(seq_len, kv_heads, head_dim)
    )

    def score_block():
        raw = (
            jnp.einsum("ikgd,jkd->kgij", query, keys, preferred_element_type=jnp.float32)
            * score_scale
        )
        return jnp.where(visible, raw, masked_value)

    scores = score_block()
    row_max = jnp.max(scores, axis=-1, keepdims=True)
    log_total = row_max + jnp.log(jnp.sum(jnp.exp(scores - row_max), axis=-1, keepdims=True))
    probs_low = jnp.exp(scores - log_total).astype(jnp.bfloat16)
    attended = (
        jnp.einsum("kgij,jkd->ikgd", probs_low, values, preferred_element_type=jnp.float32)
        .astype(jnp.bfloat16)
        .reshape(seq_len, q_heads * head_dim)
    )
    attn_part = jnp.dot(attended, w_out, preferred_element_type=jnp.float32)
    hidden_state = inputs + lax.psum(attn_part, "tensor")
    factor_two = rms_factor(hidden_state)
    scaled_two = hidden_state * factor_two
    normed_two = (scaled_two * norm_ffn).astype(jnp.bfloat16)
    shared_gated = jnp.dot(normed_two, shared_gate, preferred_element_type=jnp.float32)
    shared_upward = jnp.dot(normed_two, shared_up, preferred_element_type=jnp.float32)
    shared_hidden = (shared_gated * jax.nn.sigmoid(shared_gated) * shared_upward).astype(
        jnp.bfloat16
    )
    shared_part = jnp.dot(shared_hidden, shared_down, preferred_element_type=jnp.float32)
    position = slot_positions(routes, expert_count)
    owners = jnp.repeat(positions, routes.shape[1])
    slot_rows = (
        jnp.full((expert_count, capacity), seq_len, jnp.int32)
        .at[routes.reshape(-1), position.reshape(-1)]
        .set(owners)
    )
    padded = jnp.concatenate([normed_two, jnp.zeros((1, width), jnp.bfloat16)], axis=0)
    dispatched = to_experts(padded[slot_rows])
    local_rows = dispatched.reshape(-1, width)
    expert_gated = jnp.dot(local_rows, expert_gate[0], preferred_element_type=jnp.float32)
    expert_upward = jnp.dot(local_rows, expert_up[0], preferred_element_type=jnp.float32)
    expert_hidden = (expert_gated * jax.nn.sigmoid(expert_gated) * expert_upward).astype(
        jnp.bfloat16
    )
    expert_part = jnp.dot(
        expert_hidden, expert_down[0], preferred_element_type=jnp.float32
    ).reshape(dispatched.shape)
    returned = from_experts(expert_part)
    mixture = jnp.sum(gate_weights[:, :, None] * returned[routes, position], axis=1)
    branches = lax.psum(shared_part.astype(jnp.bfloat16), "tensor").astype(jnp.float32) + mixture
    output = (hidden_state + branches).astype(jnp.bfloat16)
    grad_result = cotangent.astype(jnp.float32)
    grad_shared_down = jnp.einsum(
        "sf,sd->fd", shared_hidden, cotangent, preferred_element_type=jnp.float32
    )
    grad_shared_hidden = jnp.einsum(
        "sd,fd->sf", cotangent, shared_down, preferred_element_type=jnp.float32
    )
    grad_sg, grad_su = swish_grads(shared_gated, shared_upward, grad_shared_hidden)
    grad_shared_gate = jnp.einsum(
        "sd,sf->df", normed_two, grad_sg, preferred_element_type=jnp.float32
    )
    grad_shared_up = jnp.einsum(
        "sd,sf->df", normed_two, grad_su, preferred_element_type=jnp.float32
    )
    shared_back_part = jnp.einsum(
        "sf,df->sd", grad_sg, shared_gate, preferred_element_type=jnp.float32
    ) + jnp.einsum("sf,df->sd", grad_su, shared_up, preferred_element_type=jnp.float32)
    routed_grad = (gate_weights[:, :, None] * grad_result[:, None, :]).astype(jnp.bfloat16)
    back_buffer = (
        jnp.zeros((expert_count, capacity, width), jnp.bfloat16)
        .at[routes, position]
        .set(routed_grad)
    )
    arrived_grad = to_experts(back_buffer).reshape(-1, width)
    grad_expert_down = jnp.einsum(
        "rf,rd->fd", expert_hidden, arrived_grad, preferred_element_type=jnp.float32
    )[None]
    grad_expert_hidden = jnp.einsum(
        "rd,fd->rf", arrived_grad, expert_down[0], preferred_element_type=jnp.float32
    )
    grad_eg, grad_eu = swish_grads(expert_gated, expert_upward, grad_expert_hidden)
    grad_expert_gate = jnp.einsum(
        "rd,rf->df", local_rows, grad_eg, preferred_element_type=jnp.float32
    )[None]
    grad_expert_up = jnp.einsum(
        "rd,rf->df", local_rows, grad_eu, preferred_element_type=jnp.float32
    )[None]
    expert_back_part = (
        jnp.einsum("rf,df->rd", grad_eg, expert_gate[0], preferred_element_type=jnp.float32)
        + jnp.einsum("rf,df->rd", grad_eu, expert_up[0], preferred_element_type=jnp.float32)
    ).reshape(dispatched.shape)
    returned_grad = from_experts(expert_back_part)
    routed_back = jnp.sum(returned_grad[routes, position], axis=1)
    normed_grad = (
        lax.psum(shared_back_part.astype(jnp.bfloat16), "tensor").astype(jnp.float32) + routed_back
    )
    grad_hidden_norm, grad_norm_ffn = norm_backward(normed_grad, norm_ffn, factor_two, scaled_two)
    grad_hidden = grad_result + grad_hidden_norm
    grad_attn = grad_hidden.astype(jnp.bfloat16)
    grad_w_out = jnp.einsum("sa,sd->ad", attended, grad_attn, preferred_element_type=jnp.float32)
    grad_attended = (
        jnp.einsum("sd,ad->sa", grad_attn, w_out, preferred_element_type=jnp.float32)
        .astype(jnp.bfloat16)
        .reshape(seq_len, kv_heads, group_size, head_dim)
    )
    probs_again = jnp.exp(score_block() - log_total)
    grad_probs = jnp.einsum(
        "ikgd,jkd->kgij", grad_attended, values, preferred_element_type=jnp.float32
    )
    row_dot = jnp.sum(probs_again * grad_probs, axis=-1, keepdims=True)
    grad_scores = (probs_again * (grad_probs - row_dot)).astype(jnp.bfloat16)
    grad_query = (
        (
            jnp.einsum("kgij,jkd->ikgd", grad_scores, keys, preferred_element_type=jnp.float32)
            * score_scale
        )
        .astype(jnp.bfloat16)
        .reshape(seq_len, q_heads * head_dim)
    )
    grad_keys = (
        (
            jnp.einsum("kgij,ikgd->jkd", grad_scores, query, preferred_element_type=jnp.float32)
            * score_scale
        )
        .astype(jnp.bfloat16)
        .reshape(seq_len, kv_heads * head_dim)
    )
    grad_values = (
        jnp.einsum(
            "kgij,ikgd->jkd",
            probs_again.astype(jnp.bfloat16),
            grad_attended,
            preferred_element_type=jnp.float32,
        )
        .astype(jnp.bfloat16)
        .reshape(seq_len, kv_heads * head_dim)
    )
    grad_w_query = jnp.einsum(
        "sd,sa->da", normed_one, grad_query, preferred_element_type=jnp.float32
    )
    grad_w_key = jnp.einsum("sd,sa->da", normed_one, grad_keys, preferred_element_type=jnp.float32)
    grad_w_value = jnp.einsum(
        "sd,sa->da", normed_one, grad_values, preferred_element_type=jnp.float32
    )
    attn_back_part = jnp.einsum(
        "sa,da->sd", grad_query, w_query, preferred_element_type=jnp.float32
    )
    attn_back_part = attn_back_part + jnp.einsum(
        "sa,da->sd", grad_keys, w_key, preferred_element_type=jnp.float32
    )
    attn_back_part = attn_back_part + jnp.einsum(
        "sa,da->sd", grad_values, w_value, preferred_element_type=jnp.float32
    )
    normed_grad_one = lax.psum(attn_back_part.astype(jnp.bfloat16), "tensor").astype(jnp.float32)
    grad_input_norm, grad_norm_attn = norm_backward(
        normed_grad_one, norm_attn, factor_one, scaled_one
    )
    grad_tokens = (grad_hidden + grad_input_norm).astype(jnp.bfloat16)
    summed = lax.psum(
        (
            grad_norm_attn,
            grad_w_query,
            grad_w_key,
            grad_w_value,
            grad_w_out,
            grad_norm_ffn,
            grad_shared_gate,
            grad_shared_up,
            grad_shared_down,
        ),
        "dp",
    )
    return (
        output,
        grad_tokens,
        summed[0],
        summed[1],
        summed[2],
        summed[3],
        summed[4],
        summed[5],
        summed[6],
        summed[7],
        summed[8],
        grad_expert_gate,
        grad_expert_up,
        grad_expert_down,
    )


def solution(mesh):
    fast = mesh.shape["dp"] == 16 and mesh.shape["tensor"] == 2
    return jax.shard_map(
        shards_fast if fast else shards,
        mesh=mesh,
        in_specs=(
            P("dp", None),
            P("dp", None),
            P("dp", None),
            P("dp", None),
            P(),
            P(None, "tensor"),
            P(None, "tensor"),
            P(None, "tensor"),
            P("tensor", None),
            P(),
            P(None, "tensor"),
            P(None, "tensor"),
            P("tensor", None),
            P("dp", None, "tensor"),
            P("dp", None, "tensor"),
            P("dp", "tensor", None),
            P("dp", None),
        ),
        out_specs=(
            P("dp", None),
            P("dp", None),
            P(),
            P(None, "tensor"),
            P(None, "tensor"),
            P(None, "tensor"),
            P("tensor", None),
            P(),
            P(None, "tensor"),
            P(None, "tensor"),
            P("tensor", None),
            P("dp", None, "tensor"),
            P("dp", None, "tensor"),
            P("dp", "tensor", None),
        ),
        check_vma=False,
    )
```

```python
import functools
import jax
import jax.numpy as jnp
from jax import lax
from jax.experimental import pallas as pl
from jax.experimental.pallas import tpu as pltpu
from jax.sharding import PartitionSpec as P

DH = 128


epsilon = 1e-05
masked_value = -1e30


def rms_factor(values):
    return lax.rsqrt(jnp.mean(values * values, axis=-1, keepdims=True) + epsilon)


def norm_backward(grad_normed, gain_vector, factor, scaled):
    grad_scaled = grad_normed * gain_vector
    inner_mean = jnp.mean(grad_scaled * scaled, axis=-1, keepdims=True)
    return (factor * (grad_scaled - scaled * inner_mean), jnp.sum(grad_normed * scaled, axis=0))


def swish_grads(gated, upward, grad_hidden):
    sigma = jax.nn.sigmoid(gated)
    grad_gated = grad_hidden * upward * sigma * (1.0 + gated * (1.0 - sigma))
    grad_upward = grad_hidden * gated * sigma
    return (grad_gated.astype(jnp.bfloat16), grad_upward.astype(jnp.bfloat16))


def slot_positions(routes, expert_count):
    flat_routes = routes.reshape(-1)
    onehot = (flat_routes[:, None] == jnp.arange(expert_count, dtype=jnp.int32)[None, :]).astype(
        jnp.int32
    )
    earlier = jnp.cumsum(onehot, axis=0) - onehot
    return jnp.sum(earlier * onehot, axis=1).reshape(routes.shape)


def to_experts(buffer):
    return lax.all_to_all(buffer, "dp", split_axis=0, concat_axis=0, tiled=True)


def from_experts(partial_value):
    own_part = lax.psum_scatter(
        partial_value.astype(jnp.bfloat16), "tensor", scatter_dimension=1, tiled=True
    ).astype(jnp.float32)
    joined = lax.all_gather(own_part.astype(jnp.bfloat16), "tensor", axis=1, tiled=True).astype(
        own_part.dtype
    )
    return lax.all_to_all(
        joined.astype(jnp.bfloat16), "dp", split_axis=0, concat_axis=0, tiled=True
    ).astype(joined.dtype)


MESH = pl.DeviceIdType.MESH
ANY = pl.BlockSpec(memory_space=pl.ANY)
VMEM = pl.BlockSpec(memory_space=pltpu.VMEM)
DMA = pltpu.SemaphoreType.DMA
bf16, f32 = jnp.bfloat16, jnp.float32


def dot(first, second):
    return jnp.dot(first, second, preferred_element_type=f32)


def dot_t(first, second):
    return lax.dot_general(first, second, (((1,), (1,)), ((), ())), preferred_element_type=f32)


def dot_rows(first, second):
    return lax.dot_general(first, second, (((0,), (0,)), ((), ())), preferred_element_type=f32)


class Place:
    def __init__(self):
        self.dp = lax.axis_index("dp")
        self.t = lax.axis_index("tensor")
        self.x, self.y, self.z = self.dp % 2, (self.dp // 2) % 2, self.dp // 4
        digits = [0xE4, 0xE1, 0x1E, 0x1B]
        code = sum(jnp.where(self.z == i, d, 0) for i, d in enumerate(digits))
        self.near = lambda n: (code // (4**n if isinstance(n, int) else jnp.where(n == 0, 1, jnp.where(n == 1, 4, jnp.where(n == 2, 16, 64))))) % 4

    def flip(self, dx, dy, z):
        return z * 4 + (self.y + dy) % 2 * 2 + (self.x + dx) % 2

    def rel(self, da, db, z):
        t = self.t
        return self.flip((1 - t) * da + t * db, t * da + (1 - t) * db, z)

    def core(self):
        return (self.dp, 1 - self.t)

    def a(self):
        return (self.rel(1, 0, self.z), self.t)

    def b(self):
        return (self.rel(0, 1, self.z), self.t)

    def at_z(self, z):
        return (self.rel(0, 0, z), self.t)


def greet(place):
    barrier = pltpu.get_barrier_semaphore()
    partners = [place.core(), place.a(), place.b()] + [place.at_z((place.z + k) % 4) for k in (1, 2, 3)]
    for partner in partners:
        pl.semaphore_signal(barrier, inc=1, device_id=partner, device_id_type=MESH)
    pl.semaphore_wait(barrier, len(partners))


def remote(src, dst, send, recv, device):
    return pltpu.make_async_remote_copy(
        src_ref=src, dst_ref=dst, send_sem=send, recv_sem=recv, device_id=device, device_id_type=MESH
    )


class Gather:
    def __init__(self, place, part, sems, swap, zfirst):
        self.p, self.part, self.swap, self.zfirst = place, part, swap, zfirst
        self.us, self.ds, self.zr, self.as_, self.ar, self.bs, self.br = sems[:7]
        if swap:
            self.cs, self.cr = sems[7:9]

    def copy(self, j, send, recv, device):
        return remote(self.part(j), self.part(j), send, recv, device)

    def up(self, da, z):
        p = self.p
        return self.copy(p.rel(da, 0, z), self.us.at[da, z], self.zr.at[da, z], p.at_z((p.z + 1) % 4))

    def down(self, da, z):
        p = self.p
        return self.copy(p.rel(da, 0, z), self.ds.at[da, z], self.zr.at[da, z], p.at_z((p.z + 3) % 4))

    def to_a(self, z):
        return self.copy(self.p.rel(0, 0, z), self.as_.at[z], self.ar.at[z], self.p.a())

    def from_a(self, z):
        return self.copy(self.p.rel(1, 0, z), self.as_.at[z], self.ar.at[z], self.p.a())

    def to_b(self, da, z):
        return self.copy(self.p.rel(da, 0, z), self.bs.at[da, z], self.br.at[da, z], self.p.b())

    def from_b(self, da, z):
        return self.copy(self.p.rel(da, 1, z), self.bs.at[da, z], self.br.at[da, z], self.p.b())

    def to_core(self, j):
        return self.copy(j, self.cs.at[j], self.cr.at[j], self.p.core())

    def ups(self, z):
        return jnp.logical_and(z <= self.p.z, self.p.z < 3)

    def downs(self, z):
        return jnp.logical_and(z >= self.p.z, self.p.z > 0)

    def along_z(self, da, z):
        pl.when(self.ups(z))(lambda: self.up(da, z).start())
        pl.when(self.downs(z))(lambda: self.down(da, z).start())

    def other_core(self, da, db, z):
        if self.swap:
            self.to_core(self.p.rel(da, db, z)).start()

    def start(self):
        if not self.zfirst:
            self.to_a(self.p.z).start()
        self.along_z(0, self.p.z)
        if self.zfirst:
            self.to_a(self.p.z).start()
        self.to_b(0, self.p.z).start()

    def got_z(self, n, da=0):
        z = self.p.near(n)
        self.up(da, z).wait_recv()
        self.along_z(da, z)
        if self.zfirst:
            self.to_a(z).start()
        self.to_b(da, z).start()
        self.other_core(da, 0, z)

    def got_a(self, n):
        z = self.p.near(n)
        self.from_a(z).wait_recv()
        if not self.zfirst:
            self.along_z(1, z)
        self.to_b(1, z).start()
        self.other_core(1, 0, z)

    def got_b(self, da, n):
        z = self.p.near(n)
        self.from_b(da, z).wait_recv()
        self.other_core(da, 1, z)

    def wait_core(self, j):
        self.to_core(j).wait_recv()

    def finish(self):
        def ends(z, _):
            for da in (0,) if self.zfirst else (0, 1):
                pl.when(self.ups(z))(lambda: self.up(da, z).wait_send())
                pl.when(self.downs(z))(lambda: self.down(da, z).wait_send())
            if self.zfirst:
                self.to_a(z).wait_send()
            self.to_b(0, z).wait_send()
            self.to_b(1, z).wait_send()
            return 0

        lax.fori_loop(0, 4, ends, 0)
        if not self.zfirst:
            self.to_a(self.p.z).wait_send()
        if self.swap:

            def swaps(i, _):
                self.to_core((self.p.dp + 1 + i) % 16).wait_send()
                return 0

            lax.fori_loop(0, 15, swaps, 0)


def gather_sems(swap):
    kinds = [(2, 4)] * 3 + [(4,)] * 2 + [(2, 4)] * 2 + [(16,)] * (2 * swap)
    return [DMA(kind) for kind in kinds]


def add_into(dst, src):
    dst[...] = dst[...] + src[...]


class Scatter:
    def __init__(self, place, part, land, sems, zlast):
        self.p, self.part, self.zlast = place, part, zlast
        self.rb, self.ra, self.rz = land
        self.bs, self.br, self.as_, self.ar, self.zs, self.zr = sems

    def order(self, m):
        return self.p.near(3 - m)

    def to_b(self, da, z):
        return remote(self.part(self.p.rel(da, 1, z)), self.rb.at[da, z], self.bs.at[da, z], self.br.at[da, z], self.p.b())

    def to_a(self, z):
        slot = z if self.zlast else 0
        return remote(self.part(self.p.rel(1, 0, z)), self.ra.at[slot], self.as_.at[slot], self.ar.at[slot], self.p.a())

    def up(self, da, t):
        p = self.p
        return remote(self.part(p.rel(da, 0, t)), self.rz.at[da, t], self.zs.at[da, t], self.zr.at[da, t], p.at_z((p.z + 1) % 4))

    def down(self, da, t):
        p = self.p
        slot = jnp.where(t == p.z - 1, 4, t)
        return remote(self.part(p.rel(da, 0, t)), self.rz.at[da, slot], self.zs.at[da, t], self.zr.at[da, slot], p.at_z((p.z + 3) % 4))

    def landed(self, da, slot):
        p = self.p
        piece = self.rz.at[da, slot]
        remote(piece, piece, self.zs.at[da, 0], self.zr.at[da, slot], p.at_z((p.z + 1) % 4)).wait_recv()

    def send_b(self):
        def sends(i, _):
            self.to_b(1 - i // 4, self.order(i % 4)).start()
            return 0

        lax.fori_loop(0, 8, sends, 0)

    def got_b(self, da, z):
        self.to_b(da, z).wait_recv()
        add_into(self.part(self.p.rel(da, 0, z)), self.rb.at[da, z])

    def pass_z(self, da, t):
        p = self.p

        @pl.when(jnp.logical_or(jnp.logical_and(t > p.z, p.z > 0), jnp.logical_and(t < p.z, p.z < 3)))
        def _():
            self.landed(da, t)
            add_into(self.part(p.rel(da, 0, t)), self.rz.at[da, t])

        pl.when(t > p.z)(lambda: self.up(da, t).start())
        pl.when(t < p.z)(lambda: self.down(da, t).start())

    def end_z(self, da):
        p = self.p

        @pl.when(p.z > 0)
        def _():
            self.landed(da, p.z)
            add_into(self.part(p.rel(da, 0, p.z)), self.rz.at[da, p.z])

        @pl.when(p.z < 3)
        def _():
            self.landed(da, 4)
            add_into(self.part(p.rel(da, 0, p.z)), self.rz.at[da, 4])

    def far(self, m):
        z = self.order(m)
        self.got_b(1, z)
        if self.zlast:
            self.to_a(z).start()
        else:
            pl.when(m < 3)(lambda: self.pass_z(1, z))

    def turn(self):
        if not self.zlast:
            self.end_z(1)
            self.to_a(self.p.z).start()

    def got_a(self, z):
        self.to_a(z).wait_recv()
        add_into(self.part(self.p.rel(0, 0, z)), self.ra.at[z])

    def close(self, m):
        z = self.order(m)
        self.got_b(0, z)
        if self.zlast:
            self.got_a(z)
        pl.when(m < 3)(lambda: self.pass_z(0, z))

    def total(self):
        self.end_z(0)
        if not self.zlast:
            self.to_a(self.p.z).wait_recv()
            add_into(self.part(self.p.dp), self.ra.at[0])

    def finish(self):
        def ends(z, _):
            for da in (0,) if self.zlast else (0, 1):
                pl.when(z != self.p.z)(lambda: self.up(da, z).wait_send())
            if self.zlast:
                self.to_a(z).wait_send()
            self.to_b(0, z).wait_send()
            self.to_b(1, z).wait_send()
            return 0

        lax.fori_loop(0, 4, ends, 0)
        if not self.zlast:
            self.to_a(self.p.z).wait_send()


def scatter_land(rows, cols, zlast):
    kinds = [(2, 4), (4 if zlast else 1,), (1 if zlast else 2, 5)]
    return [pltpu.VMEM(kind + (rows, cols), bf16) for kind in kinds]


def scatter_sems():
    return [DMA(kind) for kind in [(2, 4), (2, 4), (4,), (4,), (2, 4), (2, 5)]]


class Both:
    def __init__(self, *members):
        self.members = members

    def __getattr__(self, name):
        def call(*args):
            for member in self.members:
                getattr(member, name)(*args)

        return call


def row_mean(values):
    return jnp.sum(values, axis=1, keepdims=True) * (1.0 / values.shape[1])


def factor_of(values):
    return lax.rsqrt(row_mean(values * values) + epsilon)


def visible_in(lens, seq):
    rows = lax.broadcasted_iota(jnp.int32, (seq, seq), 0)
    cols = lax.broadcasted_iota(jnp.int32, (seq, seq), 1)
    first, second = lens[0, 0], lens[0, 0] + lens[0, 1]

    def doc(i):
        return (i >= first).astype(jnp.int32) + (i >= second).astype(jnp.int32)

    return jnp.logical_and(doc(rows) == doc(cols), cols <= rows)


def group_rows(values, g, heads):
    cols = [values[:, (heads * g + h) * DH : (heads * g + h + 1) * DH] for h in range(heads)]
    return jnp.concatenate(cols, axis=0)


def group_probs(query, keys, visible):
    seq = keys.shape[0]
    scores = dot_t(query, keys) * DH ** (-0.5)
    scores = jnp.where(visible[None], scores.reshape(-1, seq, seq), masked_value).reshape(scores.shape)
    top = jnp.max(scores, axis=1, keepdims=True)
    exps = jnp.exp(scores - top)
    return exps / jnp.sum(exps, axis=1, keepdims=True)


def swish_all(gated, upward, grad):
    sigma = jax.nn.sigmoid(gated)
    active = gated * sigma
    grad_gated = grad * upward * (sigma * (1.0 + gated * (1.0 - sigma)))
    return active * upward, grad_gated.astype(bf16), (grad * active).astype(bf16)


def place_of(p, i):
    n = jnp.where(i < 4, i, jnp.where(i < 12, (i - 4) // 2, i - 12))
    dx = jnp.where(i < 4, 0, jnp.where(i < 12, (i + 1) % 2, 1))
    dy = jnp.where(i < 4, 0, jnp.where(i < 12, i % 2, 1))
    return dx, dy, p.near(n)


def front_kernel(
    tokens, lens, routes, weights, gain1_ref, gain2_ref, cot,
    hq, hk, hv, ho, heg, heu, hed, hsg, hsu, hsd,
    n2_out, cot_out, qkv, attended, hidden, mix_all, acts_a, acts_b, grad2,
    wk, wv, weg, weu, wed, wsg, wsu, wsd, wsem,
    n2v, cotv, gall, apart, mstage, astage, dstage, own, came, rb1, ra1, rz1, rb2, ra2, rz2,
    asem, msem, dsem, dcame, credit, lsem, fsem, *sems
):
    p = Place()
    half = pl.ds(pl.multiple_of(p.t * 768, 768), 768)
    cut = 96
    top, low = pl.ds(0, cut), pl.ds(cut, 256 - cut)

    def block(j, first=0, rows=256):
        return own.at[pl.ds(pl.multiple_of(j * 256 + first, 16), rows)]

    n2p = Gather(p, lambda j: n2v.at[j, top, half], sems[:9], True, True)
    n2q = Gather(p, lambda j: n2v.at[j, low, half], sems[9:18], True, False)
    ctp = Gather(p, lambda j: cotv.at[j, top, half], sems[18:27], True, True)
    ctq = Gather(p, lambda j: cotv.at[j, low, half], sems[27:36], True, False)
    gtg = Gather(p, lambda j: gall.at[j], sems[36:43], False, True)
    scp = Scatter(p, lambda j: block(j, 0, cut), (rb1, ra1, rz1), sems[43:49], True)
    scq = Scatter(p, lambda j: block(j, cut, 256 - cut), (rb2, ra2, rz2), sems[49:55], False)
    n2g, ctg, sct = Both(n2p, n2q), Both(ctp, ctq), Both(scp, scq)
    cog = Both(ctp, gtg)
    mine = pl.multiple_of(p.t * 768, 768)
    other = pl.multiple_of((1 - p.t) * 768, 768)

    own_cot = pltpu.make_async_copy(cot, cotv.at[p.dp], lsem.at[0])
    own_cot.start()
    wq, wo = own.at[pl.ds(0, 1536)], [own.at[pl.ds(1536 + 768 * i, 768)] for i in range(2)]
    pairs = [(hq, wq), (hk, wk), (hv, wv)] + [(ho.at[:, pl.ds(768 * i, 768)], wo[i]) for i in range(2)]
    pairs += list(zip((heg, heu, hed, hsg, hsu, hsd), (weg, weu, wed, wsg, wsu, wsd)))
    loads = [pltpu.make_async_copy(s, d, wsem.at[i]) for i, (s, d) in enumerate(pairs)]
    for load in loads[:5]:
        load.start()
    gain1, gain2 = gain1_ref[...].reshape(1, 1536), gain2_ref[...].reshape(1, 1536)
    experts = lax.broadcasted_iota(jnp.int32, (16, 256), 0)
    gates = jnp.zeros((16, 256), f32)
    for k in range(6):
        gates = gates + jnp.where(routes[k : k + 1, :] == experts, weights[k : k + 1, :], 0.0)
    gall[p.dp] = gates
    greet(p)
    own_cot.wait()
    ctg.start()
    gtg.start()
    for load in loads[5:]:
        load.start()

    def arrive(first, second, n):
        first.got_z(n)
        if n == 1:
            second.got_a(0)
        second.got_z(n)
        if n > 1:
            first.got_a(n - 2)
            second.got_z(n - 1, 1)

    inputs = tokens[...].astype(f32)
    n1 = (inputs * factor_of(inputs) * gain1).astype(bf16)
    for load in loads[:5]:
        load.wait()
    qkv[:, :768] = dot(n1, wq[...]).astype(bf16)
    arrive(cog, ctq, 1)
    qkv[:, 768:1024] = dot(n1, wk[...]).astype(bf16)
    qkv[:, 1024:] = dot(n1, wv[...]).astype(bf16)
    visible = visible_in(lens, 256)
    for g in range(2):
        query = group_rows(qkv[:, :768], g, 3)
        probs = group_probs(query, qkv[:, 768 + g * DH : 768 + (g + 1) * DH], visible).astype(bf16)
        out = dot(probs, qkv[:, 1024 + g * DH : 1024 + (g + 1) * DH]).astype(bf16)
        for h in range(3):
            attended[:, (3 * g + h) * DH : (3 * g + h + 1) * DH] = out[h * 256 : (h + 1) * 256, :]
        if g == 0:
            arrive(cog, ctq, 2)
    for i in range(2):
        apart[:, 768 * i : 768 * (i + 1)] = dot(attended[...], wo[i][...])
    swap_a = remote(apart, hidden, asem.at[0], asem.at[1], p.core())
    swap_a.start()
    arrive(cog, ctq, 3)
    swap_a.wait()
    hidden[...] = tokens[...].astype(f32) + (apart[...] + hidden[...])
    state = hidden[...]
    n2v[p.dp] = (state * factor_of(state) * gain2).astype(bf16)
    n2g.start()
    for load in loads[5:]:
        load.wait()

    def outs(i):
        dx, dy, z = place_of(p, i)
        j, slot = p.flip(dx, dy, z), i % 2
        cols = [pl.ds(0, 768), pl.ds(768, 768)]
        copies = [(mstage.at[slot, :, cols[h]], mix_all.at[h, j]) for h in range(2)]
        copies += [(astage.at[slot, :, pl.ds(0, 1536)], acts_a.at[j]), (astage.at[slot, :, pl.ds(1536, 768)], acts_b.at[j])]
        return [pltpu.make_async_copy(src, dst, msem.at[slot, k]) for k, (src, dst) in enumerate(copies)]

    def swap_d(i):
        return remote(dstage.at[i % 2, :, pl.ds(other, 768)], came.at[i % 4], dsem.at[i % 2], dcame.at[i % 4], p.core())

    def paired(i):
        dx, dy, z = place_of(p, i)
        j = p.flip(dx, dy, z)
        swap_d(i).wait_recv()
        add_into(block(j), came.at[i % 4])
        pl.when(i < 12)(lambda: pl.semaphore_signal(credit, inc=1, device_id=p.core(), device_id_type=MESH))
        da = (1 - p.t) * dx + p.t * dy
        db = (1 - p.t) * dy + p.t * dx

        @pl.when(db == 1)
        def _():
            scp.to_b(da, z).start()
            scq.to_b(da, z).start()

    def step(i, _):
        dx, dy, z = place_of(p, i)
        j = p.flip(dx, dy, z)

        def window(first, count, event):
            pl.when(jnp.logical_and(i >= first, i < first + count))(lambda: event(i - first))

        @pl.when(i == 1)
        def _():
            cog.got_a(2)
            ctq.got_z(3, 1)
            n2p.got_z(1)
            n2q.got_a(0)

        @pl.when(i == 2)
        def _():
            cog.got_a(3)

        window(2, 2, lambda n: n2p.got_z(n + 2))
        window(1, 3, lambda n: n2q.got_z(n + 1))
        window(2, 4, n2p.got_a)
        window(2, 3, lambda n: n2q.got_z(n + 1, 1))
        window(0, 4, lambda n: cog.got_b(0, n))
        window(0, 4, lambda n: ctq.got_b(0, n))
        window(3, 4, lambda n: n2g.got_b(0, n))
        window(6, 4, lambda n: cog.got_b(1, n))
        window(6, 4, lambda n: ctq.got_b(1, n))
        window(9, 4, lambda n: n2g.got_b(1, n))
        @pl.when(i > 0)
        def _():
            ctg.wait_core(j)
            n2g.wait_core(j)

        @pl.when(i >= 2)
        def _():
            for copy in outs(i - 2):
                copy.wait()
            swap_d(i - 2).wait_send()

        slot = i % 2
        rows, cots = n2v.at[j], cotv.at[j]
        gate = jnp.transpose(jnp.broadcast_to(gall[j, pl.ds(p.dp, 1), :], (128, 256)))[:, :1]
        gated, upward = dot(rows[...], weg[...]), dot(rows[...], weu[...])
        hid, dg, du = swish_all(gated, upward, dot_t(cots[...], wed[...]) * gate)
        hid = (gate * hid).astype(bf16)
        astage[slot, :, 0:256] = dg
        astage[slot, :, 256:512] = du
        astage[slot, :, 1536:1792] = hid
        mstage[slot] = dot(hid, wed[...]).astype(bf16)
        dstage[slot] = (dot_t(dg, weg[...]) + dot_t(du, weu[...])).astype(bf16)
        gated, upward = dot(rows[...], wsg[...]), dot(rows[...], wsu[...])
        hid, dg, du = swish_all(gated, upward, dot_t(cots[...], wsd[...]))
        astage[slot, :, 512:1024] = dg
        astage[slot, :, 1024:1536] = du
        astage[slot, :, 1792:] = hid.astype(bf16)

        @pl.when(i == 0)
        def _():
            mstage[slot] = (mstage[slot].astype(f32) + dot(astage[slot, :, 1792:], wsd[...])).astype(bf16)
            back = dot_t(astage[slot, :, 512:1024], wsg[...]) + dot_t(astage[slot, :, 1024:1536], wsu[...])
            dstage[slot] = (dstage[slot].astype(f32) + back).astype(bf16)

        for copy in outs(i):
            copy.start()
        pl.when(i >= 4)(lambda: pl.semaphore_wait(credit, 1))
        swap_d(i).start()
        block(j)[...] = dstage[slot, :, pl.ds(mine, 768)]
        pl.when(i > 0)(lambda: paired(i - 1))
        return 0

    lax.fori_loop(0, 16, step, 0)
    paired(15)
    ends = [pltpu.make_async_copy(n2v.at[:, :, pl.ds(768 * h, 768)], n2_out.at[h], lsem.at[h]) for h in range(2)]
    ends.append(pltpu.make_async_copy(cotv, cot_out, lsem.at[2]))
    for copy in ends:
        copy.start()

    def first(n, _):
        z = p.near(n)
        scp.got_b(0, z)
        scq.got_b(0, z)
        return 0

    lax.fori_loop(0, 4, first, 0)

    def pass_on(da):
        def run(m, _):
            scq.pass_z(da, scq.order(m))
            return 0

        lax.fori_loop(0, 3, run, 0)

    def second(n, _):
        z = p.near(n)
        scp.got_b(1, z)
        scp.to_a(z).start()
        scq.got_b(1, z)
        return 0

    def third(m, _):
        z = scp.order(m)
        scp.got_a(z)
        pl.when(m < 3)(lambda: scp.pass_z(0, z))
        return 0

    pass_on(0)
    lax.fori_loop(0, 4, second, 0)
    pass_on(1)
    scq.turn()
    lax.fori_loop(0, 4, third, 0)
    scp.total()
    scq.total()
    res = apart.at[:, pl.ds(0, 768)]
    res[...] = block(p.dp)[...].astype(f32)
    swap_r = remote(res, grad2.at[:, pl.ds(mine, 768)], fsem.at[0], fsem.at[1], p.core())
    keep_r = pltpu.make_async_copy(res, grad2.at[:, pl.ds(mine, 768)], fsem.at[2])
    swap_r.start()
    keep_r.start()
    for i in (14, 15):
        for copy in outs(i):
            copy.wait()
        swap_d(i).wait_send()
    n2g.finish()
    ctg.finish()
    gtg.finish()
    sct.finish()
    for copy in ends:
        copy.wait()
    keep_r.wait()
    swap_r.wait()


def front(tokens, lens, routes, gates, gain1, gain2, cot, *weights):
    big = (16, 256, 1536)
    sds = jax.ShapeDtypeStruct
    scratch = [pltpu.VMEM(w.shape, bf16) for w in weights[1:3] + weights[4:]] + [DMA((11,))]
    scratch += [
        pltpu.VMEM(big, bf16), pltpu.VMEM(big, bf16), pltpu.VMEM((16, 16, 256), f32), pltpu.VMEM((256, 1536), f32),
        pltpu.VMEM((2, 256, 1536), bf16), pltpu.VMEM((2, 256, 2304), bf16),
        pltpu.VMEM((2, 256, 1536), bf16), pltpu.VMEM((4096, 768), bf16), pltpu.VMEM((4, 256, 768), bf16),
    ]
    scratch += scatter_land(96, 768, True) + scatter_land(160, 768, False)
    scratch += [DMA((2,)), DMA((2, 4)), DMA((2,)), DMA((4,)), pltpu.SemaphoreType.REGULAR, DMA((3,)), DMA((3,))]
    scratch += gather_sems(True) * 4 + gather_sems(False) + scatter_sems() * 2
    return pl.pallas_call(
        front_kernel,
        out_shape=(
            sds((2, 16, 256, 768), bf16), sds(big, bf16), sds((256, 1280), bf16), sds((256, 768), bf16),
            sds((256, 1536), f32), sds((2, 16, 256, 768), bf16), sds(big, bf16), sds((16, 256, 768), bf16),
            sds((256, 1536), f32),
        ),
        in_specs=[VMEM, pl.BlockSpec(memory_space=pltpu.SMEM), VMEM, VMEM, VMEM, VMEM, ANY] + [ANY] * 10,
        out_specs=(ANY, ANY, VMEM, VMEM, VMEM, ANY, ANY, ANY, ANY),
        scratch_shapes=scratch,
        compiler_params=pltpu.CompilerParams(collective_id=1, has_side_effects=True, vmem_limit_bytes=63 << 20),
    )(tokens, lens, routes, gates, gain1, gain2, cot, *weights)


def back_kernel(
    grad2, hidden, tokens, cot, gain1_ref, gain2_ref, qkv, attended, lens,
    hq, hk, hv, ho, mix_all, n2_all, cot_all, acts_a, acts_b,
    output, grad_tokens, sum_a, sum_b, sum_n, wide,
    wqkv, wo, wsem, mown, mcame, mb1, ma1, mz1, mb2, ma2, mz2, mres, mother,
    ga, gb, arb, ara, arz, brb, bra, brz, gain_all, dqkv, acc, lhs, rhs,
    msem, mcs, mcr, dsem, fsem, lsem, tsem, osem, *sems
):
    p = Place()
    gain1, gain2 = gain1_ref[...].reshape(1, 1536), gain2_ref[...].reshape(1, 1536)
    cut = 96
    mxp = Scatter(p, lambda j: mown.at[j, pl.ds(0, cut)], (mb1, ma1, mz1), sems[:6], True)
    mxq = Scatter(p, lambda j: mown.at[j, pl.ds(cut, 256 - cut)], (mb2, ma2, mz2), sems[6:12], False)
    mix = Both(mxp, mxq)
    sa = Scatter(p, lambda j: ga.at[j], (arb, ara, arz), sems[12:18], False)
    sb = Scatter(p, lambda j: gb.at[j], (brb, bra, brz), sems[18:24], True)
    gga = Gather(p, lambda j: wqkv.at[pl.ds(pl.multiple_of(96 * j, 96), 96)], sems[24:31], False, False)
    ggb = Gather(p, lambda j: wo.at[pl.ds(pl.multiple_of(48 * j, 48), 48)], sems[31:38], False, True)
    ggn = Gather(p, lambda j: gain_all.at[j], sems[38:45], False, True)
    dpart, dcame = acc.at[pl.ds(512, 256)], [acc.at[pl.ds(0, 256)], acc.at[pl.ds(256, 256)]]
    pairs = [(hq, wqkv.at[:, pl.ds(0, 768)]), (hk, wqkv.at[:, pl.ds(768, 256)]), (hv, wqkv.at[:, pl.ds(1024, 256)]), (ho, wo)]
    loads = [pltpu.make_async_copy(s, d, wsem.at[i]) for i, (s, d) in enumerate(pairs)]
    for load in reversed(loads):
        load.start()

    def swap(j):
        return remote(mix_all.at[1 - p.t, j], mcame.at[j], mcs.at[j], mcr.at[j], p.core())

    def load_mix(j):
        return pltpu.make_async_copy(mix_all.at[p.t, j], mown.at[j], msem.at[j])

    def paired(da, db):
        def pair(m, _):
            z = mxp.order(m)
            j = p.rel(da, db, z)
            load_mix(j).wait()
            swap(j).wait_recv()
            add_into(mown.at[j], mcame.at[j])
            if db:
                mxp.to_b(da, z).start()
                mxq.to_b(da, z).start()
            return 0

        lax.fori_loop(0, 4, pair, 0)

    greet(p)
    for da, db in ((1, 1), (1, 0), (0, 1), (0, 0)):

        def begin(m, _, da=da, db=db):
            z = mxp.order(m)
            swap(p.rel(da, db, z)).start()
            load_mix(p.rel(db, da, z)).start()
            return 0

        lax.fori_loop(0, 4, begin, 0)

    state = hidden[...]
    factor = factor_of(state)
    scaled = state * factor
    normed_grad = grad2[...]
    gain_sum2 = jnp.sum(normed_grad * scaled, axis=0, keepdims=True)
    weighted = normed_grad * gain2
    grad_hidden = cot[...].astype(f32) + factor * (weighted - scaled * row_mean(weighted * scaled))
    dpart[...] = grad_hidden
    grad_attn = grad_hidden.astype(bf16)
    paired(1, 1)
    loads[3].wait()
    for c in range(0, 1536, 512):
        rows = dot_rows(attended[...], grad_attn[:, c : c + 512]).astype(bf16)
        gb[:, :, c : c + 512] = rows.reshape(16, 48, 512)
    grad_att = dot_t(grad_attn, wo[...]).astype(bf16)
    sb.send_b()
    paired(1, 0)
    paired(0, 0)

    def mix_far(k, _):
        mix.far(k)
        return 0

    visible = visible_in(lens, 256)
    for g in range(2):
        query = group_rows(qkv[:, :768], g, 3)
        keys, values = qkv[:, 768 + g * DH : 768 + (g + 1) * DH], qkv[:, 1024 + g * DH : 1024 + (g + 1) * DH]
        probs = group_probs(query, keys, visible)
        grad_out = group_rows(grad_att, g, 3)
        grad_probs = dot_t(grad_out, values)
        row_dot = jnp.sum(probs * grad_probs, axis=1, keepdims=True)
        grad_scores = (probs * (grad_probs - row_dot)).astype(bf16)
        grad_query = (dot(grad_scores, keys) * DH ** (-0.5)).astype(bf16)
        for h in range(3):
            dqkv[:, (3 * g + h) * DH : (3 * g + h + 1) * DH] = grad_query[h * 256 : (h + 1) * 256, :]
        dqkv[:, 768 + g * DH : 768 + (g + 1) * DH] = (dot_rows(grad_scores, query) * DH ** (-0.5)).astype(bf16)
        dqkv[:, 1024 + g * DH : 1024 + (g + 1) * DH] = dot_rows(probs.astype(bf16), grad_out).astype(bf16)
        if g == 0:
            lax.fori_loop(0, 2, mix_far, 0)
        else:
            lax.fori_loop(2, 4, mix_far, 0)
            mxq.turn()
    inputs = tokens[...].astype(f32)
    factor_one = factor_of(inputs)
    n1 = (inputs * factor_one * gain1).astype(bf16)
    for c in range(0, 1280, 256):
        rows = dot_rows(n1, dqkv[:, c : c + 256]).astype(bf16)
        ga[:, :, c : c + 256] = rows.reshape(16, 96, 256)
    for load in loads[:3]:
        load.wait()
    dcame[0][...] = dot_t(dqkv[...], wqkv[...])
    sa.send_b()
    paired(0, 1)
    swap_d = remote(dcame[0], dcame[1], dsem.at[0], dsem.at[1], p.core())
    swap_d.start()

    swap_d.wait()
    normed_grad = dcame[0][...] + dcame[1][...]
    scaled = inputs * factor_one
    gain_sum1 = jnp.sum(normed_grad * scaled, axis=0, keepdims=True)
    weighted = normed_grad * gain1
    grad_tokens[...] = (dpart[...] + factor_one * (weighted - scaled * row_mean(weighted * scaled))).astype(bf16)
    for i in range(4):
        gain_all[p.dp, i : i + 1, :] = gain_sum1[:, i * 384 : (i + 1) * 384]
        gain_all[p.dp, 4 + i : 5 + i, :] = gain_sum2[:, i * 384 : (i + 1) * 384]
    ggn.start()
    swap_r = remote(mres, mother, fsem.at[0], fsem.at[1], p.core())

    def operands(u):
        tile, j = u // 8, u % 8
        slot = u % 2
        low = tile < 2
        return low, [
            (n2_all.at[jnp.minimum(tile, 1), pl.ds(2 * j, 2)], acts_a.at[pl.ds(2 * j, 2)]),
            (acts_b.at[pl.ds(2 * j, 2)], cot_all.at[pl.ds(2 * j, 2)]),
        ], slot

    def fetch(u):
        low, (first, second), slot = operands(u)

        @pl.when(low)
        def _():
            pltpu.make_async_copy(first[0], lhs.at[slot], tsem.at[0, slot]).start()
            pltpu.make_async_copy(first[1], rhs.at[slot], tsem.at[1, slot]).start()

        @pl.when(jnp.logical_not(low))
        def _():
            pltpu.make_async_copy(second[0], lhs.at[slot], tsem.at[0, slot]).start()
            pltpu.make_async_copy(second[1], rhs.at[slot], tsem.at[1, slot]).start()

    def tile_out(tile):
        return pltpu.make_async_copy(acc, wide.at[tile], osem.at[0])

    def work(u):
        slot = u % 2
        pltpu.make_async_copy(acts_b.at[pl.ds(0, 2)], lhs.at[slot], tsem.at[0, slot]).wait()
        pltpu.make_async_copy(acts_a.at[pl.ds(0, 2)], rhs.at[slot], tsem.at[1, slot]).wait()
        pl.when(u + 1 < 24)(lambda: fetch(u + 1))
        fresh = u % 8 == 0

        @pl.when(jnp.logical_and(fresh, u > 0))
        def _():
            tile_out(u // 8 - 1).wait()

        @pl.when(fresh)
        def _():
            acc[...] = jnp.zeros_like(acc)

        for c in range(0, 1536, 512):
            cols = slice(c, c + 512)
            acc[:, cols] = acc[:, cols] + dot_rows(lhs[slot].reshape(512, 768), rhs[slot, :, :, cols].reshape(512, 512))
        pl.when(u % 8 == 7)(lambda: tile_out(u // 8).start())

    fetch(0)

    def step(i, _):
        def window(first, count, event):
            pl.when(jnp.logical_and(i >= first, i < first + count))(lambda: event(i - first))

        def far(m):
            sb.far(m)
            sa.far(m)

        def close(m):
            sb.close(m)
            sa.close(m)

        window(0, 4, far)
        pl.when(i == 4)(sa.turn)
        window(4, 4, close)

        @pl.when(i == 8)
        def _():
            sb.total()
            ggb.part(p.dp)[...] = gb[p.dp]
            ggb.start()
            sa.total()
            gga.part(p.dp)[...] = ga[p.dp]
            gga.start()

        window(5, 3, lambda n: ggn.got_z(n + 1))
        window(8, 4, ggn.got_a)
        window(9, 3, lambda n: ggb.got_z(n + 1))
        pl.when(i == 9)(lambda: gga.got_a(0))
        window(9, 3, lambda n: gga.got_z(n + 1))
        window(10, 4, ggb.got_a)
        window(10, 3, lambda n: gga.got_z(n + 1, 1))
        for da in (0, 1):
            window(14 + 4 * da, 4, lambda n, da=da: ggb.got_b(da, n))
            window(14 + 4 * da, 4, lambda n, da=da: gga.got_b(da, n))
            window(14 + 4 * da, 4, lambda n, da=da: ggn.got_b(da, n))

        window(10, 4, mix.close)

        @pl.when(i == 15)
        def _():
            mix.total()
            mres[...] = mown[p.dp].astype(f32)
            swap_r.start()

        def some(u, _):
            work(u)
            return 0

        def done(i):
            return jnp.minimum(jnp.where(i < 8, 2 * i, 16 + 1 * (i - 8)), 24)

        lax.fori_loop(done(i), done(i + 1), some, 0)
        return 0

    lax.fori_loop(0, 24, step, 0)
    copies = [pltpu.make_async_copy(wqkv, sum_a, lsem.at[0]), pltpu.make_async_copy(wo, sum_b, lsem.at[1])]
    for copy in copies:
        copy.start()
    swap_r.wait()
    low = pl.multiple_of(p.t, 1)
    left = jnp.where(low == 0, mres[...], mother[...])
    right = jnp.where(low == 0, mother[...], mres[...])
    output[:, :768] = (hidden[:, :768] + left).astype(bf16)
    output[:, 768:] = (hidden[:, 768:] + right).astype(bf16)
    total = gain_all[0]
    for j in range(1, 16):
        total = total + gain_all[j]
    sum_n[...] = total

    def ends(j, _):
        swap(j).wait_send()
        return 0

    lax.fori_loop(0, 16, ends, 0)
    for plan in (mix, sa, sb, gga, ggb, ggn):
        plan.finish()
    tile_out(2).wait()
    for copy in copies:
        copy.wait()


def back(grad2, hidden, tokens, cot, gain1, gain2, qkv, attended, lens, wq, wk, wv, wo, *saved):
    sds = jax.ShapeDtypeStruct
    half = (16, 256, 768)
    a, b = (16, 96, 1280), (16, 48, 1536)
    scratch = [pltpu.VMEM((1536, 1280), bf16), pltpu.VMEM((768, 1536), bf16), DMA((4,))]
    scratch += [pltpu.VMEM(half, bf16), pltpu.VMEM(half, bf16)] + scatter_land(96, 768, True) + scatter_land(160, 768, False)
    scratch += [pltpu.VMEM((256, 768), f32), pltpu.VMEM((256, 768), f32), pltpu.VMEM(a, bf16), pltpu.VMEM(b, bf16)]
    scratch += scatter_land(*a[1:], False) + scatter_land(*b[1:], True)
    scratch += [
        pltpu.VMEM((16, 8, 384), f32), pltpu.VMEM((256, 1280), bf16),
        pltpu.VMEM((768, 1536), f32), pltpu.VMEM((2, 2, 256, 768), bf16), pltpu.VMEM((2, 2, 256, 1536), bf16),
    ]
    scratch += [DMA((16,)), DMA((16,)), DMA((16,)), DMA((2,)), DMA((2,)), DMA((2,)), DMA((2, 2)), DMA((1,))]
    scratch += scatter_sems() * 4 + gather_sems(False) * 3
    return pl.pallas_call(
        back_kernel,
        out_shape=(sds((256, 1536), bf16), sds((256, 1536), bf16), sds((1536, 1280), bf16), sds((768, 1536), bf16), sds((8, 384), f32), sds((3, 768, 1536), f32)),
        in_specs=[VMEM] * 8 + [pl.BlockSpec(memory_space=pltpu.SMEM)] + [ANY] * 9,
        out_specs=(VMEM, VMEM, ANY, ANY, VMEM, ANY),
        scratch_shapes=scratch,
        compiler_params=pltpu.CompilerParams(collective_id=2, has_side_effects=True, vmem_limit_bytes=63 << 20),
    )(grad2, hidden, tokens, cot, gain1, gain2, qkv, attended, lens, wq, wk, wv, wo, *saved)


def finish_kernel(sum_a, sum_b, ins, downs, out_in, grad_in, gains, wq, wk, wv, wo, ge, ue, gs, us, de, ds, out, grad, g1, g2):
    i = pl.program_id(0)
    rows = sum_a[...].astype(f32)
    wq[...], wk[...], wv[...] = rows[:, :768], rows[:, 768:1024], rows[:, 1024:]
    wo[...] = sum_b[...].astype(f32)
    ge[0], ue[0] = ins[0, :, :256], ins[0, :, 256:512]
    gs[...], us[...] = ins[0, :, 512:1024], ins[0, :, 1024:]

    @pl.when(i < 4)
    def _():
        de[0] = downs[0]

    @pl.when(i >= 4)
    def _():
        ds[...] = downs[0]

    @pl.when(i < 8)
    def _():
        out[...] = out_in[...]
        grad[...] = grad_in[...]

    @pl.when(i == 0)
    def _():
        for ref, first in ((g1, 0), (g2, 4)):
            ref[...] = jnp.concatenate([gains[first + r : first + r + 1, :] for r in range(4)], axis=1).reshape(1536)


def finish(sum_a, sum_b, wide, output, grad_tokens, gains):
    sds, spec = jax.ShapeDtypeStruct, pl.BlockSpec

    def rows(n, cols):
        return spec((n, cols), lambda i: (i, 0))

    def expert(cols):
        return spec((1, 128, cols), lambda i: (0, i, 0))

    early = spec((32, 1536), lambda i: (jnp.minimum(i, 7), 0))
    return pl.pallas_call(
        finish_kernel,
        grid=(12,),
        out_shape=(
            sds((1536, 768), f32), sds((1536, 256), f32), sds((1536, 256), f32), sds((768, 1536), f32),
            sds((1, 1536, 256), f32), sds((1, 1536, 256), f32), sds((1536, 512), f32), sds((1536, 512), f32),
            sds((1, 256, 1536), f32), sds((512, 1536), f32), sds((256, 1536), bf16), sds((256, 1536), bf16),
            sds((1536,), f32), sds((1536,), f32),
        ),
        in_specs=[
            rows(128, 1280), rows(64, 1536), spec((1, 128, 1536), lambda i: (i // 6, i % 6, 0)),
            spec((1, 64, 1536), lambda i: (2, i, 0)), early, early, spec((8, 384), lambda i: (0, 0)),
        ],
        out_specs=(
            rows(128, 768), rows(128, 256), rows(128, 256), rows(64, 1536), expert(256), expert(256), rows(128, 512), rows(128, 512),
            spec((1, 64, 1536), lambda i: (0, jnp.minimum(i, 3), 0)), spec((64, 1536), lambda i: (jnp.maximum(i - 4, 0), 0)),
            early, early, spec((1536,), lambda i: (0,)), spec((1536,), lambda i: (0,)),
        ),
        compiler_params=pltpu.CompilerParams(vmem_limit_bytes=63 << 20),
    )(sum_a, sum_b, wide, wide, output, grad_tokens, gains)


def shards_fast(
    tokens, doc_lens, routes, gate_weights, norm_attn, w_query, w_key, w_value, w_out, norm_ffn,
    shared_gate, shared_up, shared_down, expert_gate, expert_up, expert_down, cotangent,
):
    n2_all, cot_all, qkv, attended, hidden, mix_all, acts_a, acts_b, grad2 = front(
        tokens, doc_lens, routes.T, gate_weights.T, norm_attn, norm_ffn, cotangent, w_query, w_key, w_value, w_out,
        expert_gate[0], expert_up[0], expert_down[0], shared_gate, shared_up, shared_down,
    )
    output, grad_tokens, sum_a, sum_b, gains, wide = back(
        grad2, hidden, tokens, cotangent, norm_attn, norm_ffn, qkv, attended, doc_lens, w_query, w_key, w_value, w_out, mix_all,
        n2_all, cot_all, acts_a, acts_b,
    )
    wq, wk, wv, wo, gate_e, up_e, gate_s, up_s, down_e, down_s, output, grad_tokens, gain1, gain2 = finish(
        sum_a, sum_b, wide, output, grad_tokens, gains
    )
    return output, grad_tokens, gain1, wq, wk, wv, wo, gain2, gate_s, up_s, down_s, gate_e, up_e, down_e


def shards(
    tokens,
    doc_lens,
    routes,
    gate_weights,
    norm_attn,
    w_query,
    w_key,
    w_value,
    w_out,
    norm_ffn,
    shared_gate,
    shared_up,
    shared_down,
    expert_gate,
    expert_up,
    expert_down,
    cotangent,
):
    seq_len, width = tokens.shape
    head_dim = DH
    kv_heads = w_key.shape[1] // head_dim
    q_heads = w_query.shape[1] // head_dim
    group_size = q_heads // kv_heads
    score_scale = head_dim ** (-0.5)
    expert_count = lax.axis_size("dp") * expert_gate.shape[0]
    capacity = 3 * seq_len * routes.shape[1] // (2 * expert_count)
    positions = jnp.arange(seq_len, dtype=jnp.int32)
    doc_ends = jnp.cumsum(doc_lens[0])
    doc_index = jnp.sum((positions[:, None] >= doc_ends[None, :]).astype(jnp.int32), axis=1)
    visible = (doc_index[:, None] == doc_index[None, :]) & (
        positions[None, :] <= positions[:, None]
    )
    inputs = tokens.astype(jnp.float32)
    factor_one = rms_factor(inputs)
    scaled_one = inputs * factor_one
    normed_one = (scaled_one * norm_attn).astype(jnp.bfloat16)
    query = (
        jnp.dot(normed_one, w_query, preferred_element_type=jnp.float32)
        .astype(jnp.bfloat16)
        .reshape(seq_len, kv_heads, group_size, head_dim)
    )
    keys = (
        jnp.dot(normed_one, w_key, preferred_element_type=jnp.float32)
        .astype(jnp.bfloat16)
        .reshape(seq_len, kv_heads, head_dim)
    )
    values = (
        jnp.dot(normed_one, w_value, preferred_element_type=jnp.float32)
        .astype(jnp.bfloat16)
        .reshape(seq_len, kv_heads, head_dim)
    )

    def score_block():
        raw = (
            jnp.einsum("ikgd,jkd->kgij", query, keys, preferred_element_type=jnp.float32)
            * score_scale
        )
        return jnp.where(visible, raw, masked_value)

    scores = score_block()
    row_max = jnp.max(scores, axis=-1, keepdims=True)
    log_total = row_max + jnp.log(jnp.sum(jnp.exp(scores - row_max), axis=-1, keepdims=True))
    probs_low = jnp.exp(scores - log_total).astype(jnp.bfloat16)
    attended = (
        jnp.einsum("kgij,jkd->ikgd", probs_low, values, preferred_element_type=jnp.float32)
        .astype(jnp.bfloat16)
        .reshape(seq_len, q_heads * head_dim)
    )
    attn_part = jnp.dot(attended, w_out, preferred_element_type=jnp.float32)
    hidden_state = inputs + lax.psum(attn_part, "tensor")
    factor_two = rms_factor(hidden_state)
    scaled_two = hidden_state * factor_two
    normed_two = (scaled_two * norm_ffn).astype(jnp.bfloat16)
    shared_gated = jnp.dot(normed_two, shared_gate, preferred_element_type=jnp.float32)
    shared_upward = jnp.dot(normed_two, shared_up, preferred_element_type=jnp.float32)
    shared_hidden = (shared_gated * jax.nn.sigmoid(shared_gated) * shared_upward).astype(
        jnp.bfloat16
    )
    shared_part = jnp.dot(shared_hidden, shared_down, preferred_element_type=jnp.float32)
    position = slot_positions(routes, expert_count)
    owners = jnp.repeat(positions, routes.shape[1])
    slot_rows = (
        jnp.full((expert_count, capacity), seq_len, jnp.int32)
        .at[routes.reshape(-1), position.reshape(-1)]
        .set(owners)
    )
    padded = jnp.concatenate([normed_two, jnp.zeros((1, width), jnp.bfloat16)], axis=0)
    dispatched = to_experts(padded[slot_rows])
    local_rows = dispatched.reshape(-1, width)
    expert_gated = jnp.dot(local_rows, expert_gate[0], preferred_element_type=jnp.float32)
    expert_upward = jnp.dot(local_rows, expert_up[0], preferred_element_type=jnp.float32)
    expert_hidden = (expert_gated * jax.nn.sigmoid(expert_gated) * expert_upward).astype(
        jnp.bfloat16
    )
    expert_part = jnp.dot(
        expert_hidden, expert_down[0], preferred_element_type=jnp.float32
    ).reshape(dispatched.shape)
    returned = from_experts(expert_part)
    mixture = jnp.sum(gate_weights[:, :, None] * returned[routes, position], axis=1)
    branches = lax.psum(shared_part.astype(jnp.bfloat16), "tensor").astype(jnp.float32) + mixture
    output = (hidden_state + branches).astype(jnp.bfloat16)
    grad_result = cotangent.astype(jnp.float32)
    grad_shared_down = jnp.einsum(
        "sf,sd->fd", shared_hidden, cotangent, preferred_element_type=jnp.float32
    )
    grad_shared_hidden = jnp.einsum(
        "sd,fd->sf", cotangent, shared_down, preferred_element_type=jnp.float32
    )
    grad_sg, grad_su = swish_grads(shared_gated, shared_upward, grad_shared_hidden)
    grad_shared_gate = jnp.einsum(
        "sd,sf->df", normed_two, grad_sg, preferred_element_type=jnp.float32
    )
    grad_shared_up = jnp.einsum(
        "sd,sf->df", normed_two, grad_su, preferred_element_type=jnp.float32
    )
    shared_back_part = jnp.einsum(
        "sf,df->sd", grad_sg, shared_gate, preferred_element_type=jnp.float32
    ) + jnp.einsum("sf,df->sd", grad_su, shared_up, preferred_element_type=jnp.float32)
    routed_grad = (gate_weights[:, :, None] * grad_result[:, None, :]).astype(jnp.bfloat16)
    back_buffer = (
        jnp.zeros((expert_count, capacity, width), jnp.bfloat16)
        .at[routes, position]
        .set(routed_grad)
    )
    arrived_grad = to_experts(back_buffer).reshape(-1, width)
    grad_expert_down = jnp.einsum(
        "rf,rd->fd", expert_hidden, arrived_grad, preferred_element_type=jnp.float32
    )[None]
    grad_expert_hidden = jnp.einsum(
        "rd,fd->rf", arrived_grad, expert_down[0], preferred_element_type=jnp.float32
    )
    grad_eg, grad_eu = swish_grads(expert_gated, expert_upward, grad_expert_hidden)
    grad_expert_gate = jnp.einsum(
        "rd,rf->df", local_rows, grad_eg, preferred_element_type=jnp.float32
    )[None]
    grad_expert_up = jnp.einsum(
        "rd,rf->df", local_rows, grad_eu, preferred_element_type=jnp.float32
    )[None]
    expert_back_part = (
        jnp.einsum("rf,df->rd", grad_eg, expert_gate[0], preferred_element_type=jnp.float32)
        + jnp.einsum("rf,df->rd", grad_eu, expert_up[0], preferred_element_type=jnp.float32)
    ).reshape(dispatched.shape)
    returned_grad = from_experts(expert_back_part)
    routed_back = jnp.sum(returned_grad[routes, position], axis=1)
    normed_grad = (
        lax.psum(shared_back_part.astype(jnp.bfloat16), "tensor").astype(jnp.float32) + routed_back
    )
    grad_hidden_norm, grad_norm_ffn = norm_backward(normed_grad, norm_ffn, factor_two, scaled_two)
    grad_hidden = grad_result + grad_hidden_norm
    grad_attn = grad_hidden.astype(jnp.bfloat16)
    grad_w_out = jnp.einsum("sa,sd->ad", attended, grad_attn, preferred_element_type=jnp.float32)
    grad_attended = (
        jnp.einsum("sd,ad->sa", grad_attn, w_out, preferred_element_type=jnp.float32)
        .astype(jnp.bfloat16)
        .reshape(seq_len, kv_heads, group_size, head_dim)
    )
    probs_again = jnp.exp(score_block() - log_total)
    grad_probs = jnp.einsum(
        "ikgd,jkd->kgij", grad_attended, values, preferred_element_type=jnp.float32
    )
    row_dot = jnp.sum(probs_again * grad_probs, axis=-1, keepdims=True)
    grad_scores = (probs_again * (grad_probs - row_dot)).astype(jnp.bfloat16)
    grad_query = (
        (
            jnp.einsum("kgij,jkd->ikgd", grad_scores, keys, preferred_element_type=jnp.float32)
            * score_scale
        )
        .astype(jnp.bfloat16)
        .reshape(seq_len, q_heads * head_dim)
    )
    grad_keys = (
        (
            jnp.einsum("kgij,ikgd->jkd", grad_scores, query, preferred_element_type=jnp.float32)
            * score_scale
        )
        .astype(jnp.bfloat16)
        .reshape(seq_len, kv_heads * head_dim)
    )
    grad_values = (
        jnp.einsum(
            "kgij,ikgd->jkd",
            probs_again.astype(jnp.bfloat16),
            grad_attended,
            preferred_element_type=jnp.float32,
        )
        .astype(jnp.bfloat16)
        .reshape(seq_len, kv_heads * head_dim)
    )
    grad_w_query = jnp.einsum(
        "sd,sa->da", normed_one, grad_query, preferred_element_type=jnp.float32
    )
    grad_w_key = jnp.einsum("sd,sa->da", normed_one, grad_keys, preferred_element_type=jnp.float32)
    grad_w_value = jnp.einsum(
        "sd,sa->da", normed_one, grad_values, preferred_element_type=jnp.float32
    )
    attn_back_part = jnp.einsum(
        "sa,da->sd", grad_query, w_query, preferred_element_type=jnp.float32
    )
    attn_back_part = attn_back_part + jnp.einsum(
        "sa,da->sd", grad_keys, w_key, preferred_element_type=jnp.float32
    )
    attn_back_part = attn_back_part + jnp.einsum(
        "sa,da->sd", grad_values, w_value, preferred_element_type=jnp.float32
    )
    normed_grad_one = lax.psum(attn_back_part.astype(jnp.bfloat16), "tensor").astype(jnp.float32)
    grad_input_norm, grad_norm_attn = norm_backward(
        normed_grad_one, norm_attn, factor_one, scaled_one
    )
    grad_tokens = (grad_hidden + grad_input_norm).astype(jnp.bfloat16)
    summed = lax.psum(
        (
            grad_norm_attn,
            grad_w_query,
            grad_w_key,
            grad_w_value,
            grad_w_out,
            grad_norm_ffn,
            grad_shared_gate,
            grad_shared_up,
            grad_shared_down,
        ),
        "dp",
    )
    return (
        output,
        grad_tokens,
        summed[0],
        summed[1],
        summed[2],
        summed[3],
        summed[4],
        summed[5],
        summed[6],
        summed[7],
        summed[8],
        grad_expert_gate,
        grad_expert_up,
        grad_expert_down,
    )


def solution(mesh):
    fast = mesh.shape["dp"] == 16 and mesh.shape["tensor"] == 2
    return jax.shard_map(
        shards_fast if fast else shards,
        mesh=mesh,
        in_specs=(
            P("dp", None),
            P("dp", None),
            P("dp", None),
            P("dp", None),
            P(),
            P(None, "tensor"),
            P(None, "tensor"),
            P(None, "tensor"),
            P("tensor", None),
            P(),
            P(None, "tensor"),
            P(None, "tensor"),
            P("tensor", None),
            P("dp", None, "tensor"),
            P("dp", None, "tensor"),
            P("dp", "tensor", None),
            P("dp", None),
        ),
        out_specs=(
            P("dp", None),
            P("dp", None),
            P(),
            P(None, "tensor"),
            P(None, "tensor"),
            P(None, "tensor"),
            P("tensor", None),
            P(),
            P(None, "tensor"),
            P(None, "tensor"),
            P("tensor", None),
            P("dp", None, "tensor"),
            P("dp", None, "tensor"),
            P("dp", "tensor", None),
        ),
        check_vma=False,
    )
```

```python
import functools
import jax
import jax.numpy as jnp
from jax import lax
from jax.experimental import pallas as pl
from jax.experimental.pallas import tpu as pltpu
from jax.sharding import PartitionSpec as P

DH = 128


epsilon = 1e-05
masked_value = -1e30


def rms_factor(values):
    return lax.rsqrt(jnp.mean(values * values, axis=-1, keepdims=True) + epsilon)


def norm_backward(grad_normed, gain_vector, factor, scaled):
    grad_scaled = grad_normed * gain_vector
    inner_mean = jnp.mean(grad_scaled * scaled, axis=-1, keepdims=True)
    return (factor * (grad_scaled - scaled * inner_mean), jnp.sum(grad_normed * scaled, axis=0))


def swish_grads(gated, upward, grad_hidden):
    sigma = jax.nn.sigmoid(gated)
    grad_gated = grad_hidden * upward * sigma * (1.0 + gated * (1.0 - sigma))
    grad_upward = grad_hidden * gated * sigma
    return (grad_gated.astype(jnp.bfloat16), grad_upward.astype(jnp.bfloat16))


def slot_positions(routes, expert_count):
    flat_routes = routes.reshape(-1)
    onehot = (flat_routes[:, None] == jnp.arange(expert_count, dtype=jnp.int32)[None, :]).astype(
        jnp.int32
    )
    earlier = jnp.cumsum(onehot, axis=0) - onehot
    return jnp.sum(earlier * onehot, axis=1).reshape(routes.shape)


def to_experts(buffer):
    return lax.all_to_all(buffer, "dp", split_axis=0, concat_axis=0, tiled=True)


def from_experts(partial_value):
    own_part = lax.psum_scatter(
        partial_value.astype(jnp.bfloat16), "tensor", scatter_dimension=1, tiled=True
    ).astype(jnp.float32)
    joined = lax.all_gather(own_part.astype(jnp.bfloat16), "tensor", axis=1, tiled=True).astype(
        own_part.dtype
    )
    return lax.all_to_all(
        joined.astype(jnp.bfloat16), "dp", split_axis=0, concat_axis=0, tiled=True
    ).astype(joined.dtype)


MESH = pl.DeviceIdType.MESH
ANY = pl.BlockSpec(memory_space=pl.ANY)
VMEM = pl.BlockSpec(memory_space=pltpu.VMEM)
DMA = pltpu.SemaphoreType.DMA
bf16, f32 = jnp.bfloat16, jnp.float32


def dot(first, second):
    return jnp.dot(first, second, preferred_element_type=f32)


def dot_t(first, second):
    return lax.dot_general(first, second, (((1,), (1,)), ((), ())), preferred_element_type=f32)


def dot_rows(first, second):
    return lax.dot_general(first, second, (((0,), (0,)), ((), ())), preferred_element_type=f32)


class Place:
    def __init__(self):
        self.dp = lax.axis_index("dp")
        self.t = lax.axis_index("tensor")
        self.x, self.y, self.z = self.dp % 2, (self.dp // 2) % 2, self.dp // 4
        digits = [0xE4, 0xE1, 0x1E, 0x1B]
        code = sum(jnp.where(self.z == i, d, 0) for i, d in enumerate(digits))
        self.near = lambda n: (code // (4**n if isinstance(n, int) else jnp.where(n == 0, 1, jnp.where(n == 1, 4, jnp.where(n == 2, 16, 64))))) % 4

    def flip(self, dx, dy, z):
        return z * 4 + (self.y + dy) % 2 * 2 + (self.x + dx) % 2

    def rel(self, da, db, z):
        t = self.t
        return self.flip((1 - t) * da + t * db, t * da + (1 - t) * db, z)

    def core(self):
        return (self.dp, 1 - self.t)

    def a(self):
        return (self.rel(1, 0, self.z), self.t)

    def b(self):
        return (self.rel(0, 1, self.z), self.t)

    def at_z(self, z):
        return (self.rel(0, 0, z), self.t)


def greet(place):
    barrier = pltpu.get_barrier_semaphore()
    partners = [place.core(), place.a(), place.b()] + [place.at_z((place.z + k) % 4) for k in (1, 2, 3)]
    for partner in partners:
        pl.semaphore_signal(barrier, inc=1, device_id=partner, device_id_type=MESH)
    pl.semaphore_wait(barrier, len(partners))


def remote(src, dst, send, recv, device):
    return pltpu.make_async_remote_copy(
        src_ref=src, dst_ref=dst, send_sem=send, recv_sem=recv, device_id=device, device_id_type=MESH
    )


class Gather:
    def __init__(self, place, part, sems, swap, zfirst):
        self.p, self.part, self.swap, self.zfirst = place, part, swap, zfirst
        self.us, self.ds, self.zr, self.as_, self.ar, self.bs, self.br = sems[:7]
        if swap:
            self.cs, self.cr = sems[7:9]

    def copy(self, j, send, recv, device):
        return remote(self.part(j), self.part(j), send, recv, device)

    def up(self, da, z):
        p = self.p
        return self.copy(p.rel(da, 0, z), self.us.at[da, z], self.zr.at[da, z], p.at_z((p.z + 1) % 4))

    def down(self, da, z):
        p = self.p
        return self.copy(p.rel(da, 0, z), self.ds.at[da, z], self.zr.at[da, z], p.at_z((p.z + 3) % 4))

    def to_a(self, z):
        return self.copy(self.p.rel(0, 0, z), self.as_.at[z], self.ar.at[z], self.p.a())

    def from_a(self, z):
        return self.copy(self.p.rel(1, 0, z), self.as_.at[z], self.ar.at[z], self.p.a())

    def to_b(self, da, z):
        return self.copy(self.p.rel(da, 0, z), self.bs.at[da, z], self.br.at[da, z], self.p.b())

    def from_b(self, da, z):
        return self.copy(self.p.rel(da, 1, z), self.bs.at[da, z], self.br.at[da, z], self.p.b())

    def to_core(self, j):
        return self.copy(j, self.cs.at[j], self.cr.at[j], self.p.core())

    def ups(self, z):
        return jnp.logical_and(z <= self.p.z, self.p.z < 3)

    def downs(self, z):
        return jnp.logical_and(z >= self.p.z, self.p.z > 0)

    def along_z(self, da, z):
        pl.when(self.ups(z))(lambda: self.up(da, z).start())
        pl.when(self.downs(z))(lambda: self.down(da, z).start())

    def other_core(self, da, db, z):
        if self.swap:
            self.to_core(self.p.rel(da, db, z)).start()

    def start(self):
        if not self.zfirst:
            self.to_a(self.p.z).start()
        self.along_z(0, self.p.z)
        if self.zfirst:
            self.to_a(self.p.z).start()
        self.to_b(0, self.p.z).start()

    def got_z(self, n, da=0):
        z = self.p.near(n)
        self.up(da, z).wait_recv()
        self.along_z(da, z)
        if self.zfirst:
            self.to_a(z).start()
        self.to_b(da, z).start()
        self.other_core(da, 0, z)

    def got_a(self, n):
        z = self.p.near(n)
        self.from_a(z).wait_recv()
        if not self.zfirst:
            self.along_z(1, z)
        self.to_b(1, z).start()
        self.other_core(1, 0, z)

    def got_b(self, da, n):
        z = self.p.near(n)
        self.from_b(da, z).wait_recv()
        self.other_core(da, 1, z)

    def wait_core(self, j):
        self.to_core(j).wait_recv()

    def finish(self):
        def ends(z, _):
            for da in (0,) if self.zfirst else (0, 1):
                pl.when(self.ups(z))(lambda: self.up(da, z).wait_send())
                pl.when(self.downs(z))(lambda: self.down(da, z).wait_send())
            if self.zfirst:
                self.to_a(z).wait_send()
            self.to_b(0, z).wait_send()
            self.to_b(1, z).wait_send()
            return 0

        lax.fori_loop(0, 4, ends, 0)
        if not self.zfirst:
            self.to_a(self.p.z).wait_send()
        if self.swap:

            def swaps(i, _):
                self.to_core((self.p.dp + 1 + i) % 16).wait_send()
                return 0

            lax.fori_loop(0, 15, swaps, 0)


def gather_sems(swap):
    kinds = [(2, 4)] * 3 + [(4,)] * 2 + [(2, 4)] * 2 + [(16,)] * (2 * swap)
    return [DMA(kind) for kind in kinds]


def add_into(dst, src):
    dst[...] = dst[...] + src[...]


class Scatter:
    def __init__(self, place, part, land, sems, zlast):
        self.p, self.part, self.zlast = place, part, zlast
        self.rb, self.ra, self.rz = land
        self.bs, self.br, self.as_, self.ar, self.zs, self.zr = sems

    def order(self, m):
        return self.p.near(3 - m)

    def to_b(self, da, z):
        return remote(self.part(self.p.rel(da, 1, z)), self.rb.at[da, z], self.bs.at[da, z], self.br.at[da, z], self.p.b())

    def to_a(self, z):
        slot = z if self.zlast else 0
        return remote(self.part(self.p.rel(1, 0, z)), self.ra.at[slot], self.as_.at[slot], self.ar.at[slot], self.p.a())

    def up(self, da, t):
        p = self.p
        return remote(self.part(p.rel(da, 0, t)), self.rz.at[da, t], self.zs.at[da, t], self.zr.at[da, t], p.at_z((p.z + 1) % 4))

    def down(self, da, t):
        p = self.p
        slot = jnp.where(t == p.z - 1, 4, t)
        return remote(self.part(p.rel(da, 0, t)), self.rz.at[da, slot], self.zs.at[da, t], self.zr.at[da, slot], p.at_z((p.z + 3) % 4))

    def landed(self, da, slot):
        p = self.p
        piece = self.rz.at[da, slot]
        remote(piece, piece, self.zs.at[da, 0], self.zr.at[da, slot], p.at_z((p.z + 1) % 4)).wait_recv()

    def send_b(self):
        def sends(i, _):
            self.to_b(1 - i // 4, self.order(i % 4)).start()
            return 0

        lax.fori_loop(0, 8, sends, 0)

    def got_b(self, da, z):
        self.to_b(da, z).wait_recv()
        add_into(self.part(self.p.rel(da, 0, z)), self.rb.at[da, z])

    def pass_z(self, da, t):
        p = self.p

        @pl.when(jnp.logical_or(jnp.logical_and(t > p.z, p.z > 0), jnp.logical_and(t < p.z, p.z < 3)))
        def _():
            self.landed(da, t)
            add_into(self.part(p.rel(da, 0, t)), self.rz.at[da, t])

        pl.when(t > p.z)(lambda: self.up(da, t).start())
        pl.when(t < p.z)(lambda: self.down(da, t).start())

    def end_z(self, da):
        p = self.p

        @pl.when(p.z > 0)
        def _():
            self.landed(da, p.z)
            add_into(self.part(p.rel(da, 0, p.z)), self.rz.at[da, p.z])

        @pl.when(p.z < 3)
        def _():
            self.landed(da, 4)
            add_into(self.part(p.rel(da, 0, p.z)), self.rz.at[da, 4])

    def far(self, m):
        z = self.order(m)
        self.got_b(1, z)
        if self.zlast:
            self.to_a(z).start()
        else:
            pl.when(m < 3)(lambda: self.pass_z(1, z))

    def turn(self):
        if not self.zlast:
            self.end_z(1)
            self.to_a(self.p.z).start()

    def got_a(self, z):
        self.to_a(z).wait_recv()
        add_into(self.part(self.p.rel(0, 0, z)), self.ra.at[z])

    def close(self, m):
        z = self.order(m)
        self.got_b(0, z)
        if self.zlast:
            self.got_a(z)
        pl.when(m < 3)(lambda: self.pass_z(0, z))

    def total(self):
        self.end_z(0)
        if not self.zlast:
            self.to_a(self.p.z).wait_recv()
            add_into(self.part(self.p.dp), self.ra.at[0])

    def finish(self):
        def ends(z, _):
            for da in (0,) if self.zlast else (0, 1):
                pl.when(z != self.p.z)(lambda: self.up(da, z).wait_send())
            if self.zlast:
                self.to_a(z).wait_send()
            self.to_b(0, z).wait_send()
            self.to_b(1, z).wait_send()
            return 0

        lax.fori_loop(0, 4, ends, 0)
        if not self.zlast:
            self.to_a(self.p.z).wait_send()


def scatter_land(rows, cols, zlast):
    kinds = [(2, 4), (4 if zlast else 1,), (1 if zlast else 2, 5)]
    return [pltpu.VMEM(kind + (rows, cols), bf16) for kind in kinds]


def scatter_sems():
    return [DMA(kind) for kind in [(2, 4), (2, 4), (4,), (4,), (2, 4), (2, 5)]]


class Both:
    def __init__(self, *members):
        self.members = members

    def __getattr__(self, name):
        def call(*args):
            for member in self.members:
                getattr(member, name)(*args)

        return call


def row_mean(values):
    return jnp.sum(values, axis=1, keepdims=True) * (1.0 / values.shape[1])


def factor_of(values):
    return lax.rsqrt(row_mean(values * values) + epsilon)


def visible_in(lens, seq):
    rows = lax.broadcasted_iota(jnp.int32, (seq, seq), 0)
    cols = lax.broadcasted_iota(jnp.int32, (seq, seq), 1)
    first, second = lens[0, 0], lens[0, 0] + lens[0, 1]

    def doc(i):
        return (i >= first).astype(jnp.int32) + (i >= second).astype(jnp.int32)

    return jnp.logical_and(doc(rows) == doc(cols), cols <= rows)


def group_rows(values, g, heads):
    cols = [values[:, (heads * g + h) * DH : (heads * g + h + 1) * DH] for h in range(heads)]
    return jnp.concatenate(cols, axis=0)


def group_probs(query, keys, visible):
    seq = keys.shape[0]
    scores = dot_t(query, keys) * DH ** (-0.5)
    scores = jnp.where(visible[None], scores.reshape(-1, seq, seq), masked_value).reshape(scores.shape)
    top = jnp.max(scores, axis=1, keepdims=True)
    exps = jnp.exp(scores - top)
    return exps / jnp.sum(exps, axis=1, keepdims=True)


def swish_all(gated, upward, grad):
    sigma = jax.nn.sigmoid(gated)
    active = gated * sigma
    grad_gated = grad * upward * (sigma * (1.0 + gated * (1.0 - sigma)))
    return active * upward, grad_gated.astype(bf16), (grad * active).astype(bf16)


def place_of(p, i):
    n = jnp.where(i < 4, i, jnp.where(i < 12, (i - 4) // 2, i - 12))
    dx = jnp.where(i < 4, 0, jnp.where(i < 12, (i + 1) % 2, 1))
    dy = jnp.where(i < 4, 0, jnp.where(i < 12, i % 2, 1))
    return dx, dy, p.near(n)


def front_kernel(
    tokens, lens, routes, weights, gain1_ref, gain2_ref, cot,
    hq, hk, hv, ho, heg, heu, hed, hsg, hsu, hsd,
    n2_out, cot_out, qkv, attended, hidden, mix_all, acts_a, acts_b, grad2,
    wk, wv, weg, weu, wed, wsg, wsu, wsd, wsem,
    n2v, cotv, gall, apart, mstage, astage, dstage, own, came, rb1, ra1, rz1, rb2, ra2, rz2,
    asem, msem, dsem, dcame, credit, lsem, fsem, *sems
):
    p = Place()
    half = pl.ds(pl.multiple_of(p.t * 768, 768), 768)
    cut = 96
    top, low = pl.ds(0, cut), pl.ds(cut, 256 - cut)

    def block(j, first=0, rows=256):
        return own.at[pl.ds(pl.multiple_of(j * 256 + first, 16), rows)]

    n2p = Gather(p, lambda j: n2v.at[j, top, half], sems[:9], True, True)
    n2q = Gather(p, lambda j: n2v.at[j, low, half], sems[9:18], True, False)
    ctp = Gather(p, lambda j: cotv.at[j, top, half], sems[18:27], True, True)
    ctq = Gather(p, lambda j: cotv.at[j, low, half], sems[27:36], True, False)
    gtg = Gather(p, lambda j: gall.at[j], sems[36:43], False, True)
    scp = Scatter(p, lambda j: block(j, 0, cut), (rb1, ra1, rz1), sems[43:49], True)
    scq = Scatter(p, lambda j: block(j, cut, 256 - cut), (rb2, ra2, rz2), sems[49:55], False)
    n2g, ctg, sct = Both(n2p, n2q), Both(ctp, ctq), Both(scp, scq)
    cog = Both(ctp, gtg)
    mine = pl.multiple_of(p.t * 768, 768)
    other = pl.multiple_of((1 - p.t) * 768, 768)

    own_cot = pltpu.make_async_copy(cot, cotv.at[p.dp], lsem.at[0])
    own_cot.start()
    wq, wo = own.at[pl.ds(0, 1536)], [own.at[pl.ds(1536 + 768 * i, 768)] for i in range(2)]
    pairs = [(hq, wq), (hk, wk), (hv, wv)] + [(ho.at[:, pl.ds(768 * i, 768)], wo[i]) for i in range(2)]
    pairs += list(zip((heg, heu, hed, hsg, hsu, hsd), (weg, weu, wed, wsg, wsu, wsd)))
    loads = [pltpu.make_async_copy(s, d, wsem.at[i]) for i, (s, d) in enumerate(pairs)]
    for load in loads[:5]:
        load.start()
    gain1, gain2 = gain1_ref[...].reshape(1, 1536), gain2_ref[...].reshape(1, 1536)
    experts = lax.broadcasted_iota(jnp.int32, (16, 256), 0)
    gates = jnp.zeros((16, 256), f32)
    for k in range(6):
        gates = gates + jnp.where(routes[k : k + 1, :] == experts, weights[k : k + 1, :], 0.0)
    gall[p.dp] = gates
    greet(p)
    own_cot.wait()
    ctg.start()
    gtg.start()
    for load in loads[5:]:
        load.start()

    def arrive(first, second, n):
        first.got_z(n)
        if n == 1:
            second.got_a(0)
        second.got_z(n)
        if n > 1:
            first.got_a(n - 2)
            second.got_z(n - 1, 1)

    inputs = tokens[...].astype(f32)
    n1 = (inputs * factor_of(inputs) * gain1).astype(bf16)
    for load in loads[:5]:
        load.wait()
    qkv[:, :768] = dot(n1, wq[...]).astype(bf16)
    arrive(cog, ctq, 1)
    qkv[:, 768:1024] = dot(n1, wk[...]).astype(bf16)
    qkv[:, 1024:] = dot(n1, wv[...]).astype(bf16)
    visible = visible_in(lens, 256)
    for g in range(2):
        query = group_rows(qkv[:, :768], g, 3)
        probs = group_probs(query, qkv[:, 768 + g * DH : 768 + (g + 1) * DH], visible).astype(bf16)
        out = dot(probs, qkv[:, 1024 + g * DH : 1024 + (g + 1) * DH]).astype(bf16)
        for h in range(3):
            attended[:, (3 * g + h) * DH : (3 * g + h + 1) * DH] = out[h * 256 : (h + 1) * 256, :]
        if g == 0:
            arrive(cog, ctq, 2)
    for i in range(2):
        apart[:, 768 * i : 768 * (i + 1)] = dot(attended[...], wo[i][...])
    swap_a = remote(apart, hidden, asem.at[0], asem.at[1], p.core())
    swap_a.start()
    arrive(cog, ctq, 3)
    swap_a.wait()
    hidden[...] = tokens[...].astype(f32) + (apart[...] + hidden[...])
    state = hidden[...]
    n2v[p.dp] = (state * factor_of(state) * gain2).astype(bf16)
    n2g.start()
    for load in loads[5:]:
        load.wait()

    def outs(i):
        dx, dy, z = place_of(p, i)
        j, slot = p.flip(dx, dy, z), i % 2
        cols = [pl.ds(0, 768), pl.ds(768, 768)]
        copies = [(mstage.at[slot, :, cols[h]], mix_all.at[h, j]) for h in range(2)]
        copies += [(astage.at[slot, :, pl.ds(0, 1536)], acts_a.at[j]), (astage.at[slot, :, pl.ds(1536, 768)], acts_b.at[j])]
        return [pltpu.make_async_copy(src, dst, msem.at[slot, k]) for k, (src, dst) in enumerate(copies)]

    def swap_d(i):
        return remote(dstage.at[i % 2, :, pl.ds(other, 768)], came.at[i % 4], dsem.at[i % 2], dcame.at[i % 4], p.core())

    def paired(i):
        dx, dy, z = place_of(p, i)
        j = p.flip(dx, dy, z)
        swap_d(i).wait_recv()
        add_into(block(j), came.at[i % 4])
        pl.when(i < 12)(lambda: pl.semaphore_signal(credit, inc=1, device_id=p.core(), device_id_type=MESH))
        da = (1 - p.t) * dx + p.t * dy
        db = (1 - p.t) * dy + p.t * dx

        @pl.when(db == 1)
        def _():
            scp.to_b(da, z).start()
            scq.to_b(da, z).start()

    def step(i, _):
        dx, dy, z = place_of(p, i)
        j = p.flip(dx, dy, z)

        def window(first, count, event):
            pl.when(jnp.logical_and(i >= first, i < first + count))(lambda: event(i - first))

        @pl.when(i == 1)
        def _():
            cog.got_a(2)
            ctq.got_z(3, 1)
            n2p.got_z(1)
            n2q.got_a(0)

        @pl.when(i == 2)
        def _():
            cog.got_a(3)

        window(2, 2, lambda n: n2p.got_z(n + 2))
        window(1, 3, lambda n: n2q.got_z(n + 1))
        window(2, 4, n2p.got_a)
        window(2, 3, lambda n: n2q.got_z(n + 1, 1))
        window(0, 4, lambda n: cog.got_b(0, n))
        window(0, 4, lambda n: ctq.got_b(0, n))
        window(3, 4, lambda n: n2g.got_b(0, n))
        window(6, 4, lambda n: cog.got_b(1, n))
        window(6, 4, lambda n: ctq.got_b(1, n))
        window(9, 4, lambda n: n2g.got_b(1, n))
        @pl.when(i > 0)
        def _():
            ctg.wait_core(j)
            n2g.wait_core(j)

        @pl.when(i >= 2)
        def _():
            for copy in outs(i - 2):
                copy.wait()
            swap_d(i - 2).wait_send()

        slot = i % 2
        rows, cots = n2v.at[j], cotv.at[j]
        gate = jnp.transpose(jnp.broadcast_to(gall[j, pl.ds(p.dp, 1), :], (128, 256)))[:, :1]
        gated, upward = dot(rows[...], weg[...]), dot(rows[...], weu[...])
        hid, dg, du = swish_all(gated, upward, dot_t(cots[...], wed[...]) * gate)
        hid = (gate * hid).astype(bf16)
        astage[slot, :, 0:256] = dg
        astage[slot, :, 256:512] = du
        astage[slot, :, 1536:1792] = hid
        mstage[slot] = dot(hid, wed[...]).astype(bf16)
        dstage[slot] = (dot_t(dg, weg[...]) + dot_t(du, weu[...])).astype(bf16)
        gated, upward = dot(rows[...], wsg[...]), dot(rows[...], wsu[...])
        hid, dg, du = swish_all(gated, upward, dot_t(cots[...], wsd[...]))
        astage[slot, :, 512:1024] = dg
        astage[slot, :, 1024:1536] = du
        astage[slot, :, 1792:] = hid.astype(bf16)

        @pl.when(i == 0)
        def _():
            mstage[slot] = (mstage[slot].astype(f32) + dot(astage[slot, :, 1792:], wsd[...])).astype(bf16)
            back = dot_t(astage[slot, :, 512:1024], wsg[...]) + dot_t(astage[slot, :, 1024:1536], wsu[...])
            dstage[slot] = (dstage[slot].astype(f32) + back).astype(bf16)

        for copy in outs(i):
            copy.start()
        pl.when(i >= 4)(lambda: pl.semaphore_wait(credit, 1))
        swap_d(i).start()
        block(j)[...] = dstage[slot, :, pl.ds(mine, 768)]
        pl.when(i > 0)(lambda: paired(i - 1))
        return 0

    lax.fori_loop(0, 16, step, 0)
    paired(15)
    ends = [pltpu.make_async_copy(n2v.at[:, :, pl.ds(768 * h, 768)], n2_out.at[h], lsem.at[h]) for h in range(2)]
    ends.append(pltpu.make_async_copy(cotv, cot_out, lsem.at[2]))
    for copy in ends:
        copy.start()

    def first(n, _):
        z = p.near(n)
        scp.got_b(0, z)
        scq.got_b(0, z)
        return 0

    lax.fori_loop(0, 4, first, 0)

    def pass_on(da):
        def run(m, _):
            scq.pass_z(da, scq.order(m))
            return 0

        lax.fori_loop(0, 3, run, 0)

    def second(n, _):
        z = p.near(n)
        scp.got_b(1, z)
        scp.to_a(z).start()
        scq.got_b(1, z)
        return 0

    def third(m, _):
        z = scp.order(m)
        scp.got_a(z)
        pl.when(m < 3)(lambda: scp.pass_z(0, z))
        return 0

    pass_on(0)
    lax.fori_loop(0, 4, second, 0)
    pass_on(1)
    scq.turn()
    lax.fori_loop(0, 4, third, 0)
    scp.total()
    scq.total()
    res = apart.at[:, pl.ds(0, 768)]
    res[...] = block(p.dp)[...].astype(f32)
    swap_r = remote(res, grad2.at[:, pl.ds(mine, 768)], fsem.at[0], fsem.at[1], p.core())
    keep_r = pltpu.make_async_copy(res, grad2.at[:, pl.ds(mine, 768)], fsem.at[2])
    swap_r.start()
    keep_r.start()
    for i in (14, 15):
        for copy in outs(i):
            copy.wait()
        swap_d(i).wait_send()
    n2g.finish()
    ctg.finish()
    gtg.finish()
    sct.finish()
    for copy in ends:
        copy.wait()
    keep_r.wait()
    swap_r.wait()


def front(tokens, lens, routes, gates, gain1, gain2, cot, *weights):
    big = (16, 256, 1536)
    sds = jax.ShapeDtypeStruct
    scratch = [pltpu.VMEM(w.shape, bf16) for w in weights[1:3] + weights[4:]] + [DMA((11,))]
    scratch += [
        pltpu.VMEM(big, bf16), pltpu.VMEM(big, bf16), pltpu.VMEM((16, 16, 256), f32), pltpu.VMEM((256, 1536), f32),
        pltpu.VMEM((2, 256, 1536), bf16), pltpu.VMEM((2, 256, 2304), bf16),
        pltpu.VMEM((2, 256, 1536), bf16), pltpu.VMEM((4096, 768), bf16), pltpu.VMEM((4, 256, 768), bf16),
    ]
    scratch += scatter_land(96, 768, True) + scatter_land(160, 768, False)
    scratch += [DMA((2,)), DMA((2, 4)), DMA((2,)), DMA((4,)), pltpu.SemaphoreType.REGULAR, DMA((3,)), DMA((3,))]
    scratch += gather_sems(True) * 4 + gather_sems(False) + scatter_sems() * 2
    return pl.pallas_call(
        front_kernel,
        out_shape=(
            sds((2, 16, 256, 768), bf16), sds(big, bf16), sds((256, 1280), bf16), sds((256, 768), bf16),
            sds((256, 1536), f32), sds((2, 16, 256, 768), bf16), sds(big, bf16), sds((16, 256, 768), bf16),
            sds((256, 1536), f32),
        ),
        in_specs=[VMEM, pl.BlockSpec(memory_space=pltpu.SMEM), VMEM, VMEM, VMEM, VMEM, ANY] + [ANY] * 10,
        out_specs=(ANY, ANY, VMEM, VMEM, VMEM, ANY, ANY, ANY, ANY),
        scratch_shapes=scratch,
        compiler_params=pltpu.CompilerParams(collective_id=1, has_side_effects=True, vmem_limit_bytes=63 << 20),
    )(tokens, lens, routes, gates, gain1, gain2, cot, *weights)


def back_kernel(
    grad2, hidden, tokens, cot, gain1_ref, gain2_ref, qkv, attended, lens,
    hq, hk, hv, ho, mix_all, n2_all, cot_all, acts_a, acts_b,
    output, grad_tokens, sum_a, sum_b, sum_n, wide,
    wqkv, wo, wsem, mown, mcame, mb1, ma1, mz1, mb2, ma2, mz2, mother,
    ga, gb, arb, ara, arz, brb, bra, brz, gain_all, dqkv, acc, lhs, rhs,
    msem, mcs, mcr, dsem, fsem, lsem, tsem, osem, *sems
):
    p = Place()
    gain1, gain2 = gain1_ref[...].reshape(1, 1536), gain2_ref[...].reshape(1, 1536)
    cut = 96
    mxp = Scatter(p, lambda j: mown.at[j, pl.ds(0, cut)], (mb1, ma1, mz1), sems[:6], True)
    mxq = Scatter(p, lambda j: mown.at[j, pl.ds(cut, 256 - cut)], (mb2, ma2, mz2), sems[6:12], False)
    mix = Both(mxp, mxq)
    sa = Scatter(p, lambda j: ga.at[j], (arb, ara, arz), sems[12:18], False)
    sb = Scatter(p, lambda j: gb.at[j], (brb, bra, brz), sems[18:24], True)
    gga = Gather(p, lambda j: wqkv.at[pl.ds(pl.multiple_of(96 * j, 96), 96)], sems[24:31], False, False)
    ggb = Gather(p, lambda j: wo.at[pl.ds(pl.multiple_of(48 * j, 48), 48)], sems[31:38], False, True)
    ggn = Gather(p, lambda j: gain_all.at[j], sems[38:45], False, True)
    dpart, dcame = acc.at[pl.ds(512, 256)], [acc.at[pl.ds(0, 256)], acc.at[pl.ds(256, 256)]]
    pairs = [(hq, wqkv.at[:, pl.ds(0, 768)]), (hk, wqkv.at[:, pl.ds(768, 256)]), (hv, wqkv.at[:, pl.ds(1024, 256)]), (ho, wo)]
    loads = [pltpu.make_async_copy(s, d, wsem.at[i]) for i, (s, d) in enumerate(pairs)]
    for load in reversed(loads):
        load.start()

    def swap(j):
        return remote(mix_all.at[1 - p.t, j], mcame.at[j], mcs.at[j], mcr.at[j], p.core())

    def load_mix(j):
        return pltpu.make_async_copy(mix_all.at[p.t, j], mown.at[j], msem.at[j])

    def paired(da, db):
        def pair(m, _):
            z = mxp.order(m)
            j = p.rel(da, db, z)
            load_mix(j).wait()
            swap(j).wait_recv()
            add_into(mown.at[j], mcame.at[j])
            if db:
                mxp.to_b(da, z).start()
                mxq.to_b(da, z).start()
            return 0

        lax.fori_loop(0, 4, pair, 0)

    greet(p)
    for da, db in ((1, 1), (1, 0), (0, 1), (0, 0)):

        def begin(m, _, da=da, db=db):
            z = mxp.order(m)
            swap(p.rel(da, db, z)).start()
            load_mix(p.rel(db, da, z)).start()
            return 0

        lax.fori_loop(0, 4, begin, 0)

    state = hidden[...]
    factor = factor_of(state)
    scaled = state * factor
    normed_grad = grad2[...]
    gain_sum2 = jnp.sum(normed_grad * scaled, axis=0, keepdims=True)
    weighted = normed_grad * gain2
    grad_hidden = cot[...].astype(f32) + factor * (weighted - scaled * row_mean(weighted * scaled))
    dpart[...] = grad_hidden
    grad_attn = grad_hidden.astype(bf16)
    paired(1, 1)
    loads[3].wait()
    for c in range(0, 1536, 512):
        rows = dot_rows(attended[...], grad_attn[:, c : c + 512]).astype(bf16)
        gb[:, :, c : c + 512] = rows.reshape(16, 48, 512)
    grad_att = dot_t(grad_attn, wo[...]).astype(bf16)
    sb.send_b()
    paired(1, 0)
    paired(0, 0)

    def mix_far(k, _):
        mix.far(k)
        return 0

    visible = visible_in(lens, 256)
    for g in range(2):
        query = group_rows(qkv[:, :768], g, 3)
        keys, values = qkv[:, 768 + g * DH : 768 + (g + 1) * DH], qkv[:, 1024 + g * DH : 1024 + (g + 1) * DH]
        probs = group_probs(query, keys, visible)
        grad_out = group_rows(grad_att, g, 3)
        grad_probs = dot_t(grad_out, values)
        row_dot = jnp.sum(probs * grad_probs, axis=1, keepdims=True)
        grad_scores = (probs * (grad_probs - row_dot)).astype(bf16)
        grad_query = (dot(grad_scores, keys) * DH ** (-0.5)).astype(bf16)
        for h in range(3):
            dqkv[:, (3 * g + h) * DH : (3 * g + h + 1) * DH] = grad_query[h * 256 : (h + 1) * 256, :]
        dqkv[:, 768 + g * DH : 768 + (g + 1) * DH] = (dot_rows(grad_scores, query) * DH ** (-0.5)).astype(bf16)
        dqkv[:, 1024 + g * DH : 1024 + (g + 1) * DH] = dot_rows(probs.astype(bf16), grad_out).astype(bf16)
        if g == 0:
            lax.fori_loop(0, 2, mix_far, 0)
        else:
            lax.fori_loop(2, 4, mix_far, 0)
            mxq.turn()
    inputs = tokens[...].astype(f32)
    factor_one = factor_of(inputs)
    n1 = (inputs * factor_one * gain1).astype(bf16)
    for c in range(0, 1280, 256):
        rows = dot_rows(n1, dqkv[:, c : c + 256]).astype(bf16)
        ga[:, :, c : c + 256] = rows.reshape(16, 96, 256)
    for load in loads[:3]:
        load.wait()
    dcame[0][...] = dot_t(dqkv[...], wqkv[...])
    sa.send_b()
    paired(0, 1)
    swap_d = remote(dcame[0], dcame[1], dsem.at[0], dsem.at[1], p.core())
    swap_d.start()

    swap_d.wait()
    normed_grad = dcame[0][...] + dcame[1][...]
    scaled = inputs * factor_one
    gain_sum1 = jnp.sum(normed_grad * scaled, axis=0, keepdims=True)
    weighted = normed_grad * gain1
    grad_tokens[...] = (dpart[...] + factor_one * (weighted - scaled * row_mean(weighted * scaled))).astype(bf16)
    for i in range(4):
        gain_all[p.dp, i : i + 1, :] = gain_sum1[:, i * 384 : (i + 1) * 384]
        gain_all[p.dp, 4 + i : 5 + i, :] = gain_sum2[:, i * 384 : (i + 1) * 384]
    ggn.start()
    swap_r = remote(mown.at[p.dp], mother, fsem.at[0], fsem.at[1], p.core())

    def operands(u):
        tile, j = u // 8, u % 8
        slot = u % 2
        low = tile < 2
        return low, [
            (n2_all.at[jnp.minimum(tile, 1), pl.ds(2 * j, 2)], acts_a.at[pl.ds(2 * j, 2)]),
            (acts_b.at[pl.ds(2 * j, 2)], cot_all.at[pl.ds(2 * j, 2)]),
        ], slot

    def fetch(u):
        low, (first, second), slot = operands(u)

        @pl.when(low)
        def _():
            pltpu.make_async_copy(first[0], lhs.at[slot], tsem.at[0, slot]).start()
            pltpu.make_async_copy(first[1], rhs.at[slot], tsem.at[1, slot]).start()

        @pl.when(jnp.logical_not(low))
        def _():
            pltpu.make_async_copy(second[0], lhs.at[slot], tsem.at[0, slot]).start()
            pltpu.make_async_copy(second[1], rhs.at[slot], tsem.at[1, slot]).start()

    def tile_out(tile):
        copies = [(rhs.at[1, h], wide.at[tile, pl.ds(256 * h, 256)]) for h in range(2)]
        copies += [(lhs.at[1, h], wide.at[tile, pl.ds(512, 256), pl.ds(768 * h, 768)]) for h in range(2)]
        return [pltpu.make_async_copy(src, dst, osem.at[k]) for k, (src, dst) in enumerate(copies)]

    def work(u):
        slot = u % 2
        pltpu.make_async_copy(acts_b.at[pl.ds(0, 2)], lhs.at[slot], tsem.at[0, slot]).wait()
        pltpu.make_async_copy(acts_a.at[pl.ds(0, 2)], rhs.at[slot], tsem.at[1, slot]).wait()
        fresh = u % 8 == 0

        @pl.when(jnp.logical_and(fresh, u > 0))
        def _():
            for copy in tile_out(u // 8 - 1):
                copy.wait()

        pl.when(u + 1 < 24)(lambda: fetch(u + 1))

        @pl.when(fresh)
        def _():
            acc[...] = jnp.zeros_like(acc)

        for c in range(0, 1536, 512):
            cols = slice(c, c + 512)
            acc[:, cols] = acc[:, cols] + dot_rows(lhs[slot].reshape(512, 768), rhs[slot, :, :, cols].reshape(512, 512))

        @pl.when(u % 8 == 7)
        def _():
            for h in range(2):
                rhs[1, h] = acc[256 * h : 256 * (h + 1), :].astype(bf16)
                lhs[1, h] = acc[512:, 768 * h : 768 * (h + 1)].astype(bf16)
            for copy in tile_out(u // 8):
                copy.start()


    fetch(0)

    def step(i, _):
        def window(first, count, event):
            pl.when(jnp.logical_and(i >= first, i < first + count))(lambda: event(i - first))

        def far(m):
            sb.far(m)
            sa.far(m)

        def close(m):
            sb.close(m)
            sa.close(m)

        window(0, 4, far)
        pl.when(i == 4)(sa.turn)
        window(4, 4, close)

        @pl.when(i == 8)
        def _():
            sb.total()
            ggb.part(p.dp)[...] = gb[p.dp]
            ggb.start()
            sa.total()
            gga.part(p.dp)[...] = ga[p.dp]
            gga.start()

        window(5, 3, lambda n: ggn.got_z(n + 1))
        window(8, 4, ggn.got_a)
        window(9, 3, lambda n: ggb.got_z(n + 1))
        pl.when(i == 9)(lambda: gga.got_a(0))
        window(9, 3, lambda n: gga.got_z(n + 1))
        window(10, 4, ggb.got_a)
        window(10, 3, lambda n: gga.got_z(n + 1, 1))
        for da in (0, 1):
            window(14 + 4 * da, 4, lambda n, da=da: ggb.got_b(da, n))
            window(14 + 4 * da, 4, lambda n, da=da: gga.got_b(da, n))
            window(14 + 4 * da, 4, lambda n, da=da: ggn.got_b(da, n))

        window(10, 4, mix.close)

        @pl.when(i == 15)
        def _():
            mix.total()
            swap_r.start()

        def some(u, _):
            work(u)
            return 0

        def done(i):
            return jnp.minimum(jnp.where(i < 8, 2 * i, 16 + 1 * (i - 8)), 24)

        lax.fori_loop(done(i), done(i + 1), some, 0)
        return 0

    lax.fori_loop(0, 24, step, 0)
    copies = [pltpu.make_async_copy(wqkv, sum_a, lsem.at[0]), pltpu.make_async_copy(wo, sum_b, lsem.at[1])]
    for copy in copies:
        copy.start()
    swap_r.wait()
    low = pl.multiple_of(p.t, 1)
    kept, came = mown[p.dp].astype(f32), mother[...].astype(f32)
    left = jnp.where(low == 0, kept, came)
    right = jnp.where(low == 0, came, kept)
    output[:, :768] = (hidden[:, :768] + left).astype(bf16)
    output[:, 768:] = (hidden[:, 768:] + right).astype(bf16)
    total = gain_all[0]
    for j in range(1, 16):
        total = total + gain_all[j]
    sum_n[...] = total

    def ends(j, _):
        swap(j).wait_send()
        return 0

    lax.fori_loop(0, 16, ends, 0)
    for plan in (mix, sa, sb, gga, ggb, ggn):
        plan.finish()
    for copy in tile_out(2):
        copy.wait()
    for copy in copies:
        copy.wait()


def back(grad2, hidden, tokens, cot, gain1, gain2, qkv, attended, lens, wq, wk, wv, wo, *saved):
    sds = jax.ShapeDtypeStruct
    half = (16, 256, 768)
    a, b = (16, 96, 1280), (16, 48, 1536)
    scratch = [pltpu.VMEM((1536, 1280), bf16), pltpu.VMEM((768, 1536), bf16), DMA((4,))]
    scratch += [pltpu.VMEM(half, bf16), pltpu.VMEM(half, bf16)] + scatter_land(96, 768, True) + scatter_land(160, 768, False)
    scratch += [pltpu.VMEM((256, 768), bf16), pltpu.VMEM(a, bf16), pltpu.VMEM(b, bf16)]
    scratch += scatter_land(*a[1:], False) + scatter_land(*b[1:], True)
    scratch += [
        pltpu.VMEM((16, 8, 384), f32), pltpu.VMEM((256, 1280), bf16),
        pltpu.VMEM((768, 1536), f32), pltpu.VMEM((2, 2, 256, 768), bf16), pltpu.VMEM((2, 2, 256, 1536), bf16),
    ]
    scratch += [DMA((16,)), DMA((16,)), DMA((16,)), DMA((2,)), DMA((2,)), DMA((2,)), DMA((2, 2)), DMA((4,))]
    scratch += scatter_sems() * 4 + gather_sems(False) * 3
    return pl.pallas_call(
        back_kernel,
        out_shape=(sds((256, 1536), bf16), sds((256, 1536), bf16), sds((1536, 1280), bf16), sds((768, 1536), bf16), sds((8, 384), f32), sds((3, 768, 1536), bf16)),
        in_specs=[VMEM] * 8 + [pl.BlockSpec(memory_space=pltpu.SMEM)] + [ANY] * 9,
        out_specs=(VMEM, VMEM, ANY, ANY, VMEM, ANY),
        scratch_shapes=scratch,
        compiler_params=pltpu.CompilerParams(collective_id=2, has_side_effects=True, vmem_limit_bytes=63 << 20),
    )(grad2, hidden, tokens, cot, gain1, gain2, qkv, attended, lens, wq, wk, wv, wo, *saved)


def finish_kernel(sum_a, sum_b, ins, downs, out_in, grad_in, gains, wq, wk, wv, wo, ge, ue, gs, us, de, ds, out, grad, g1, g2):
    i = pl.program_id(0)
    rows = sum_a[...].astype(f32)
    wq[...], wk[...], wv[...] = rows[:, :768], rows[:, 768:1024], rows[:, 1024:]
    wo[...] = sum_b[...].astype(f32)
    rows = ins[0].astype(f32)
    ge[0], ue[0], gs[...], us[...] = rows[:, :256], rows[:, 256:512], rows[:, 512:1024], rows[:, 1024:]

    @pl.when(i < 4)
    def _():
        de[0] = downs[0].astype(f32)

    @pl.when(i >= 4)
    def _():
        ds[...] = downs[0].astype(f32)

    @pl.when(i < 8)
    def _():
        out[...] = out_in[...]
        grad[...] = grad_in[...]

    @pl.when(i == 0)
    def _():
        for ref, first in ((g1, 0), (g2, 4)):
            ref[...] = jnp.concatenate([gains[first + r : first + r + 1, :] for r in range(4)], axis=1).reshape(1536)


def finish(sum_a, sum_b, wide, output, grad_tokens, gains):
    sds, spec = jax.ShapeDtypeStruct, pl.BlockSpec

    def rows(n, cols):
        return spec((n, cols), lambda i: (i, 0))

    def expert(cols):
        return spec((1, 128, cols), lambda i: (0, i, 0))

    early = spec((32, 1536), lambda i: (jnp.minimum(i, 7), 0))
    return pl.pallas_call(
        finish_kernel,
        grid=(12,),
        out_shape=(
            sds((1536, 768), f32), sds((1536, 256), f32), sds((1536, 256), f32), sds((768, 1536), f32),
            sds((1, 1536, 256), f32), sds((1, 1536, 256), f32), sds((1536, 512), f32), sds((1536, 512), f32),
            sds((1, 256, 1536), f32), sds((512, 1536), f32), sds((256, 1536), bf16), sds((256, 1536), bf16),
            sds((1536,), f32), sds((1536,), f32),
        ),
        in_specs=[
            rows(128, 1280), rows(64, 1536), spec((1, 128, 1536), lambda i: (i // 6, i % 6, 0)),
            spec((1, 64, 1536), lambda i: (2, i, 0)), early, early, spec((8, 384), lambda i: (0, 0)),
        ],
        out_specs=(
            rows(128, 768), rows(128, 256), rows(128, 256), rows(64, 1536), expert(256), expert(256), rows(128, 512), rows(128, 512),
            spec((1, 64, 1536), lambda i: (0, jnp.minimum(i, 3), 0)), spec((64, 1536), lambda i: (jnp.maximum(i - 4, 0), 0)),
            early, early, spec((1536,), lambda i: (0,)), spec((1536,), lambda i: (0,)),
        ),
        compiler_params=pltpu.CompilerParams(vmem_limit_bytes=63 << 20),
    )(sum_a, sum_b, wide, wide, output, grad_tokens, gains)


def shards_fast(
    tokens, doc_lens, routes, gate_weights, norm_attn, w_query, w_key, w_value, w_out, norm_ffn,
    shared_gate, shared_up, shared_down, expert_gate, expert_up, expert_down, cotangent,
):
    n2_all, cot_all, qkv, attended, hidden, mix_all, acts_a, acts_b, grad2 = front(
        tokens, doc_lens, routes.T, gate_weights.T, norm_attn, norm_ffn, cotangent, w_query, w_key, w_value, w_out,
        expert_gate[0], expert_up[0], expert_down[0], shared_gate, shared_up, shared_down,
    )
    output, grad_tokens, sum_a, sum_b, gains, wide = back(
        grad2, hidden, tokens, cotangent, norm_attn, norm_ffn, qkv, attended, doc_lens, w_query, w_key, w_value, w_out, mix_all,
        n2_all, cot_all, acts_a, acts_b,
    )
    wq, wk, wv, wo, gate_e, up_e, gate_s, up_s, down_e, down_s, output, grad_tokens, gain1, gain2 = finish(
        sum_a, sum_b, wide, output, grad_tokens, gains
    )
    return output, grad_tokens, gain1, wq, wk, wv, wo, gain2, gate_s, up_s, down_s, gate_e, up_e, down_e


def shards(
    tokens,
    doc_lens,
    routes,
    gate_weights,
    norm_attn,
    w_query,
    w_key,
    w_value,
    w_out,
    norm_ffn,
    shared_gate,
    shared_up,
    shared_down,
    expert_gate,
    expert_up,
    expert_down,
    cotangent,
):
    seq_len, width = tokens.shape
    head_dim = DH
    kv_heads = w_key.shape[1] // head_dim
    q_heads = w_query.shape[1] // head_dim
    group_size = q_heads // kv_heads
    score_scale = head_dim ** (-0.5)
    expert_count = lax.axis_size("dp") * expert_gate.shape[0]
    capacity = 3 * seq_len * routes.shape[1] // (2 * expert_count)
    positions = jnp.arange(seq_len, dtype=jnp.int32)
    doc_ends = jnp.cumsum(doc_lens[0])
    doc_index = jnp.sum((positions[:, None] >= doc_ends[None, :]).astype(jnp.int32), axis=1)
    visible = (doc_index[:, None] == doc_index[None, :]) & (
        positions[None, :] <= positions[:, None]
    )
    inputs = tokens.astype(jnp.float32)
    factor_one = rms_factor(inputs)
    scaled_one = inputs * factor_one
    normed_one = (scaled_one * norm_attn).astype(jnp.bfloat16)
    query = (
        jnp.dot(normed_one, w_query, preferred_element_type=jnp.float32)
        .astype(jnp.bfloat16)
        .reshape(seq_len, kv_heads, group_size, head_dim)
    )
    keys = (
        jnp.dot(normed_one, w_key, preferred_element_type=jnp.float32)
        .astype(jnp.bfloat16)
        .reshape(seq_len, kv_heads, head_dim)
    )
    values = (
        jnp.dot(normed_one, w_value, preferred_element_type=jnp.float32)
        .astype(jnp.bfloat16)
        .reshape(seq_len, kv_heads, head_dim)
    )

    def score_block():
        raw = (
            jnp.einsum("ikgd,jkd->kgij", query, keys, preferred_element_type=jnp.float32)
            * score_scale
        )
        return jnp.where(visible, raw, masked_value)

    scores = score_block()
    row_max = jnp.max(scores, axis=-1, keepdims=True)
    log_total = row_max + jnp.log(jnp.sum(jnp.exp(scores - row_max), axis=-1, keepdims=True))
    probs_low = jnp.exp(scores - log_total).astype(jnp.bfloat16)
    attended = (
        jnp.einsum("kgij,jkd->ikgd", probs_low, values, preferred_element_type=jnp.float32)
        .astype(jnp.bfloat16)
        .reshape(seq_len, q_heads * head_dim)
    )
    attn_part = jnp.dot(attended, w_out, preferred_element_type=jnp.float32)
    hidden_state = inputs + lax.psum(attn_part, "tensor")
    factor_two = rms_factor(hidden_state)
    scaled_two = hidden_state * factor_two
    normed_two = (scaled_two * norm_ffn).astype(jnp.bfloat16)
    shared_gated = jnp.dot(normed_two, shared_gate, preferred_element_type=jnp.float32)
    shared_upward = jnp.dot(normed_two, shared_up, preferred_element_type=jnp.float32)
    shared_hidden = (shared_gated * jax.nn.sigmoid(shared_gated) * shared_upward).astype(
        jnp.bfloat16
    )
    shared_part = jnp.dot(shared_hidden, shared_down, preferred_element_type=jnp.float32)
    position = slot_positions(routes, expert_count)
    owners = jnp.repeat(positions, routes.shape[1])
    slot_rows = (
        jnp.full((expert_count, capacity), seq_len, jnp.int32)
        .at[routes.reshape(-1), position.reshape(-1)]
        .set(owners)
    )
    padded = jnp.concatenate([normed_two, jnp.zeros((1, width), jnp.bfloat16)], axis=0)
    dispatched = to_experts(padded[slot_rows])
    local_rows = dispatched.reshape(-1, width)
    expert_gated = jnp.dot(local_rows, expert_gate[0], preferred_element_type=jnp.float32)
    expert_upward = jnp.dot(local_rows, expert_up[0], preferred_element_type=jnp.float32)
    expert_hidden = (expert_gated * jax.nn.sigmoid(expert_gated) * expert_upward).astype(
        jnp.bfloat16
    )
    expert_part = jnp.dot(
        expert_hidden, expert_down[0], preferred_element_type=jnp.float32
    ).reshape(dispatched.shape)
    returned = from_experts(expert_part)
    mixture = jnp.sum(gate_weights[:, :, None] * returned[routes, position], axis=1)
    branches = lax.psum(shared_part.astype(jnp.bfloat16), "tensor").astype(jnp.float32) + mixture
    output = (hidden_state + branches).astype(jnp.bfloat16)
    grad_result = cotangent.astype(jnp.float32)
    grad_shared_down = jnp.einsum(
        "sf,sd->fd", shared_hidden, cotangent, preferred_element_type=jnp.float32
    )
    grad_shared_hidden = jnp.einsum(
        "sd,fd->sf", cotangent, shared_down, preferred_element_type=jnp.float32
    )
    grad_sg, grad_su = swish_grads(shared_gated, shared_upward, grad_shared_hidden)
    grad_shared_gate = jnp.einsum(
        "sd,sf->df", normed_two, grad_sg, preferred_element_type=jnp.float32
    )
    grad_shared_up = jnp.einsum(
        "sd,sf->df", normed_two, grad_su, preferred_element_type=jnp.float32
    )
    shared_back_part = jnp.einsum(
        "sf,df->sd", grad_sg, shared_gate, preferred_element_type=jnp.float32
    ) + jnp.einsum("sf,df->sd", grad_su, shared_up, preferred_element_type=jnp.float32)
    routed_grad = (gate_weights[:, :, None] * grad_result[:, None, :]).astype(jnp.bfloat16)
    back_buffer = (
        jnp.zeros((expert_count, capacity, width), jnp.bfloat16)
        .at[routes, position]
        .set(routed_grad)
    )
    arrived_grad = to_experts(back_buffer).reshape(-1, width)
    grad_expert_down = jnp.einsum(
        "rf,rd->fd", expert_hidden, arrived_grad, preferred_element_type=jnp.float32
    )[None]
    grad_expert_hidden = jnp.einsum(
        "rd,fd->rf", arrived_grad, expert_down[0], preferred_element_type=jnp.float32
    )
    grad_eg, grad_eu = swish_grads(expert_gated, expert_upward, grad_expert_hidden)
    grad_expert_gate = jnp.einsum(
        "rd,rf->df", local_rows, grad_eg, preferred_element_type=jnp.float32
    )[None]
    grad_expert_up = jnp.einsum(
        "rd,rf->df", local_rows, grad_eu, preferred_element_type=jnp.float32
    )[None]
    expert_back_part = (
        jnp.einsum("rf,df->rd", grad_eg, expert_gate[0], preferred_element_type=jnp.float32)
        + jnp.einsum("rf,df->rd", grad_eu, expert_up[0], preferred_element_type=jnp.float32)
    ).reshape(dispatched.shape)
    returned_grad = from_experts(expert_back_part)
    routed_back = jnp.sum(returned_grad[routes, position], axis=1)
    normed_grad = (
        lax.psum(shared_back_part.astype(jnp.bfloat16), "tensor").astype(jnp.float32) + routed_back
    )
    grad_hidden_norm, grad_norm_ffn = norm_backward(normed_grad, norm_ffn, factor_two, scaled_two)
    grad_hidden = grad_result + grad_hidden_norm
    grad_attn = grad_hidden.astype(jnp.bfloat16)
    grad_w_out = jnp.einsum("sa,sd->ad", attended, grad_attn, preferred_element_type=jnp.float32)
    grad_attended = (
        jnp.einsum("sd,ad->sa", grad_attn, w_out, preferred_element_type=jnp.float32)
        .astype(jnp.bfloat16)
        .reshape(seq_len, kv_heads, group_size, head_dim)
    )
    probs_again = jnp.exp(score_block() - log_total)
    grad_probs = jnp.einsum(
        "ikgd,jkd->kgij", grad_attended, values, preferred_element_type=jnp.float32
    )
    row_dot = jnp.sum(probs_again * grad_probs, axis=-1, keepdims=True)
    grad_scores = (probs_again * (grad_probs - row_dot)).astype(jnp.bfloat16)
    grad_query = (
        (
            jnp.einsum("kgij,jkd->ikgd", grad_scores, keys, preferred_element_type=jnp.float32)
            * score_scale
        )
        .astype(jnp.bfloat16)
        .reshape(seq_len, q_heads * head_dim)
    )
    grad_keys = (
        (
            jnp.einsum("kgij,ikgd->jkd", grad_scores, query, preferred_element_type=jnp.float32)
            * score_scale
        )
        .astype(jnp.bfloat16)
        .reshape(seq_len, kv_heads * head_dim)
    )
    grad_values = (
        jnp.einsum(
            "kgij,ikgd->jkd",
            probs_again.astype(jnp.bfloat16),
            grad_attended,
            preferred_element_type=jnp.float32,
        )
        .astype(jnp.bfloat16)
        .reshape(seq_len, kv_heads * head_dim)
    )
    grad_w_query = jnp.einsum(
        "sd,sa->da", normed_one, grad_query, preferred_element_type=jnp.float32
    )
    grad_w_key = jnp.einsum("sd,sa->da", normed_one, grad_keys, preferred_element_type=jnp.float32)
    grad_w_value = jnp.einsum(
        "sd,sa->da", normed_one, grad_values, preferred_element_type=jnp.float32
    )
    attn_back_part = jnp.einsum(
        "sa,da->sd", grad_query, w_query, preferred_element_type=jnp.float32
    )
    attn_back_part = attn_back_part + jnp.einsum(
        "sa,da->sd", grad_keys, w_key, preferred_element_type=jnp.float32
    )
    attn_back_part = attn_back_part + jnp.einsum(
        "sa,da->sd", grad_values, w_value, preferred_element_type=jnp.float32
    )
    normed_grad_one = lax.psum(attn_back_part.astype(jnp.bfloat16), "tensor").astype(jnp.float32)
    grad_input_norm, grad_norm_attn = norm_backward(
        normed_grad_one, norm_attn, factor_one, scaled_one
    )
    grad_tokens = (grad_hidden + grad_input_norm).astype(jnp.bfloat16)
    summed = lax.psum(
        (
            grad_norm_attn,
            grad_w_query,
            grad_w_key,
            grad_w_value,
            grad_w_out,
            grad_norm_ffn,
            grad_shared_gate,
            grad_shared_up,
            grad_shared_down,
        ),
        "dp",
    )
    return (
        output,
        grad_tokens,
        summed[0],
        summed[1],
        summed[2],
        summed[3],
        summed[4],
        summed[5],
        summed[6],
        summed[7],
        summed[8],
        grad_expert_gate,
        grad_expert_up,
        grad_expert_down,
    )


def solution(mesh):
    fast = mesh.shape["dp"] == 16 and mesh.shape["tensor"] == 2
    return jax.shard_map(
        shards_fast if fast else shards,
        mesh=mesh,
        in_specs=(
            P("dp", None),
            P("dp", None),
            P("dp", None),
            P("dp", None),
            P(),
            P(None, "tensor"),
            P(None, "tensor"),
            P(None, "tensor"),
            P("tensor", None),
            P(),
            P(None, "tensor"),
            P(None, "tensor"),
            P("tensor", None),
            P("dp", None, "tensor"),
            P("dp", None, "tensor"),
            P("dp", "tensor", None),
            P("dp", None),
        ),
        out_specs=(
            P("dp", None),
            P("dp", None),
            P(),
            P(None, "tensor"),
            P(None, "tensor"),
            P(None, "tensor"),
            P("tensor", None),
            P(),
            P(None, "tensor"),
            P(None, "tensor"),
            P("tensor", None),
            P("dp", None, "tensor"),
            P("dp", None, "tensor"),
            P("dp", "tensor", None),
        ),
        check_vma=False,
    )
```
